32 devices in a mesh: expert: 32 (over z, y, x, core).
Axes of the slice: x: 2, y: 2, z: 4, core: 2. Of those that a mesh axis runs over, the one named last changes fastest.
Arguments:
- tokens: bfloat16 [4096, 1024], P('expert'), may hold values from -6 to 6
- gain_attend: bfloat16 [1024], P('expert'), may hold values from 0.5 to 1.5
- joint_weight: bfloat16 [1024, 3072], P('expert'), may hold values from -0.1875 to 0.1875
- merge_weight: bfloat16 [1024, 1024], P('expert'), may hold values from -0.5 to 0.5
- gain_feed: bfloat16 [1024], P('expert'), may hold values from 0.5 to 1.5
- up_weight: bfloat16 [1024, 4096], P('expert'), may hold values from -0.1875 to 0.1875
- down_weight: bfloat16 [4096, 1024], P('expert'), may hold values from -0.1875 to 0.1875
- router_weight: bfloat16 [1024, 32], P('expert'), may hold values from -0.12988281 to 0.12988281
- mix_weight: bfloat16 [1024, 2], P('expert'), may hold values from -0.1796875 to 0.1796875
- widen_weight: bfloat16 [32, 1024, 4096], P('expert'), may hold values from -0.1875 to 0.1875
- narrow_weight: bfloat16 [32, 4096, 1024], P('expert'), may hold values from -9.875 to 9.875
- routes: int32 [4096, 1], P('expert'), may hold values from 0 to 31; in each aligned block of 128 rows (0 to 127, 128 to 255, ...) at most 8 rows name the same one
- segments: int32 [32, 128], P('expert'), may hold values from 0 to 7, never falling along the last dimension, each value on 1 to 64 neighbouring positions
- cotangent: bfloat16 [4096, 1024], P('expert'), may hold values from -6 to 6
Outputs:
- result: bfloat16 [4096, 1024], P('expert')
- tokens_grad: bfloat16 [4096, 1024], P('expert')
- attend_grad: float32 [1024], P('expert')
- joint_grad: float32 [1024, 3072], P('expert')
- merge_grad: float32 [1024, 1024], P('expert')
- feed_grad: float32 [1024], P('expert')
- up_grad: float32 [1024, 4096], P('expert')
- down_grad: float32 [4096, 1024], P('expert')
- router_grad: float32 [1024, 32], P('expert')
- mix_grad: float32 [1024, 2], P('expert')
- widen_grad: float32 [32, 1024, 4096], P('expert')
- narrow_grad: float32 [32, 4096, 1024], P('expert')
The draws below stay inside these ranges and needn't reach their ends.
Inputs may be any that keep to these rules, and one draw needn't show every extreme that they name: `routes`: no expert is named by more than 8 of the rows of one device; some expert is named by exactly 8 rows of one device. `segments`: along each sequence the numbers never fall; each document holds 1 to 64 positions, one exactly 64.
All inputs are finite; a program needn't handle non-finite values.
Results may differ from the reference program's by a relative error of at most 0.014.
Values may be sent and summed in bfloat16 or wider, within the bound.
No kernel may reach another device: no remote copies, remote signals or barrier semaphores. Data moves between devices by JAX's collectives and lax.ppermute only.
A program may use at most 192 MiB of HBM per device.

```python
import math
import jax
import jax.numpy as jnp
import numpy as np
from jax import lax

D = 1024
HEADS = 16
HEAD_DIM = 64
FF = 4096
TOK_DEV = 128
EXPERTS = 32
SEQS = 32
TOKENS = 4096
CAP = 8
DOCS = 8
DOC_MOST = 64


def steps_of(own_key, extent, shards, low, top_value):
    level, own = 1.0, jax.random.fold_in(own_key, 6)
    for dim, shards_of in shards:
        heights = jnp.exp(jax.random.uniform(jax.random.fold_in(own, dim), (shards_of,), jnp.float32, low / len(shards), top_value / len(shards)))
        level = level * jnp.repeat(heights, extent[dim] // shards_of).reshape([-1 if axis == dim else 1 for axis in range(len(extent))])
    return level


def profile(count, total, bound, slope):
    loads = [(1 << 20) // math.isqrt(standing ** slope) + 1 for standing in range(2, count + 1)]
    rest, holding = total - bound - (count - 1), [1] * (count - 1)
    while rest > 0:
        candidates = [i for i in range(count - 1) if holding[i] < bound]
        mass, left = sum([loads[i] for i in candidates]), rest
        for i in candidates:
            more = min(bound - holding[i], max(1, left * loads[i] // mass), rest)
            holding[i] = holding[i] + more
            rest = rest - more
    return np.array([bound] + holding)


def uneven(key, count, total, limit, lean):
    if count == 2:
        one = jax.random.randint(key, (), max(1, total - limit), min(limit, total - 1) + 1)
        return jnp.stack([one, total - one])
    lengths = jnp.asarray(profile(count, total, limit, lean), jnp.int32)
    couples = (count - 1) // 2
    donor, sink = lengths[1:1 + 2 * couples:2], lengths[2:2 + 2 * couples:2]
    margin = jnp.minimum(donor - 1, limit - sink)
    shifted = jax.random.randint(jax.random.fold_in(key, 1), (couples,), 0, 1 << 20) % (margin + 1)
    lengths = lengths.at[1:1 + 2 * couples:2].set(donor - shifted).at[2:2 + 2 * couples:2].set(sink + shifted)
    return lengths[jax.random.permutation(jax.random.fold_in(key, 2), count)]


def deal_out(key, own, number, rows, amount, top, most, skew):
    order = jax.random.permutation(key, amount)
    crowded, common = load_shares(amount, rows * top, most, skew, True), load_shares(amount, rows * top, most, skew, False)
    places = jnp.arange(amount)

    def named(tallies, rotation):
        used = int((tallies > 0).sum())
        fixed = max(1, used // 4)
        moved = fixed + (places - fixed + rotation * (used - fixed)) % max(1, amount - fixed)
        return jnp.zeros((amount,), jnp.int32).at[order[jnp.where(places < fixed, places, moved)]].set(jnp.asarray(tallies, jnp.int32))

    tallies = jnp.where(number % 4 == 0, named(crowded, number // 4), named(common, number - number // 4 - 1))
    mixed = jax.random.permutation(jax.random.fold_in(own, 3), amount)
    donor, sink = mixed[0:amount // 2 * 2:2], mixed[1:amount // 2 * 2:2]
    room = jnp.minimum(tallies[donor] - 1, most - tallies[sink]) // 2
    room = jnp.where((donor == order[0]) | (sink == order[0]) | (tallies[sink] == 0), 0, jnp.maximum(room, 0))
    moved = jax.random.randint(jax.random.fold_in(own, 4), (amount // 2,), 0, 1 << 20) % (room + 1)
    tallies = tallies.at[donor].add(-moved).at[sink].add(moved)
    items = jnp.searchsorted(jnp.cumsum(tallies), jnp.arange(rows * top), side="right").astype(jnp.int32)
    table = items.reshape(top, rows).T
    table = table[jax.random.permutation(jax.random.fold_in(own, 1), rows)]
    rotation = jax.random.randint(jax.random.fold_in(own, 2), (rows, 1), 0, top)
    return jnp.take_along_axis(table, (jnp.arange(top)[None, :] + rotation) % top, axis=1)


def load_shares(amount, total, bound, skew, full):
    weights = [(1 << 20) // math.isqrt(standing ** skew) + 1 for standing in range(1, amount + 1)]
    largest = bound if full else min(bound, max(-(-total // amount), total * weights[0] // sum(weights)))
    least = 1 if total - largest >= amount - 1 else 0
    counts, rest = [largest] + [least] * (amount - 1), total - largest - least * (amount - 1)
    while rest > 0:
        candidates = [i for i in range(1, amount) if counts[i] < largest] or [i for i in range(1, amount) if counts[i] < bound]
        whole, left = sum([weights[i] for i in candidates]), rest
        for i in candidates:
            more = min(bound - counts[i], max(1, left * weights[i] // whole), rest)
            counts[i] = counts[i] + more
            rest = rest - more
    return np.array(counts)


def centred(key, extent, scale, bound, split=(), kind=jnp.bfloat16):
    values = jax.random.normal(key, extent, jnp.float32) * scale
    if len(split) > 0:
        values = steps_of(key, extent, split, -0.22, 0.18) * values
    return jnp.clip(values, min=-bound, max=bound).astype(kind)


def setup_inputs(seed: int = 0) -> dict:
    key_of = jax.random.split(jax.random.key(seed), 15)
    tokens = centred(key_of[0], (TOKENS, D), 1.0, 6.0, ((0, 32),))
    gain_attend = jnp.clip(1.0 + 0.1 * jax.random.normal(key_of[1], (D,), jnp.float32), 0.5, 1.5).astype(jnp.bfloat16)
    joint_weight = centred(key_of[2], (D, 3 * D), D ** -0.5, 0.1875, ((0, 32),))
    merge_weight = centred(key_of[3], (D, D), (D // 8) ** -0.5, 0.5, ((0, 32),))
    gain_feed = jnp.clip(1.0 + 0.1 * jax.random.normal(key_of[4], (D,), jnp.float32), 0.5, 1.5).astype(jnp.bfloat16)
    up_weight = centred(key_of[5], (D, FF), D ** -0.5, 0.1875, ((0, 32),))
    down_weight = centred(key_of[6], (FF, D), (FF // 4) ** -0.5, 0.1875, ((0, 32),))
    router_weight = centred(key_of[7], (D, EXPERTS), 0.022, 0.12988281, ((0, 32),))
    mix_weight = centred(key_of[8], (D, 2), 0.03, 0.1796875, ((0, 32),))
    widen_weight = centred(key_of[9], (EXPERTS, D, FF), D ** -0.5, 0.1875, ((0, 32),))
    narrow_weight = centred(key_of[10], (EXPERTS, FF, D), (3.3 * EXPERTS / FF ** 0.5), 9.875, ((0, 32),))
    routes_keys = jax.random.split(jax.random.fold_in(key_of[11], 1), TOKENS // TOK_DEV)
    routes_turns = jax.random.permutation(jax.random.fold_in(key_of[11], 3), TOKENS // TOK_DEV)
    routes = jax.vmap(lambda own, number: deal_out(jax.random.fold_in(key_of[11], 2), own, number, TOK_DEV, EXPERTS, 1, CAP, 2))(routes_keys, routes_turns).reshape((TOKENS, 1))
    segments = jax.vmap(lambda own: jnp.searchsorted(jnp.cumsum(uneven(own, DOCS, TOK_DEV, DOC_MOST, 2)), jnp.arange(TOK_DEV), side="right"))(jax.random.split(key_of[12], SEQS)).reshape((SEQS, TOK_DEV)).astype(jnp.int32)
    cotangent = centred(key_of[13], (TOKENS, D), 1.0, 6.0, ((0, 32),))
    return dict(tokens=tokens, gain_attend=gain_attend, joint_weight=joint_weight, merge_weight=merge_weight, gain_feed=gain_feed, up_weight=up_weight, down_weight=down_weight, router_weight=router_weight, mix_weight=mix_weight, widen_weight=widen_weight, narrow_weight=narrow_weight, routes=routes, segments=segments, cotangent=cotangent)


@jax.custom_vjp
def low(v):
    return lax.optimization_barrier(v.astype(jnp.bfloat16)).astype(jnp.float32)

@jax.custom_vjp
def low_back(v):
    return v

def low_keep(v):
    return (low(v), None)

def low_pass(kept, grad):
    return (grad,)

def back_keep(v):
    return (v, None)

def back_low(kept, grad):
    return (low(grad),)
low.defvjp(low_keep, low_pass)
low_back.defvjp(back_keep, back_low)
epsilon = 1e-05
hidden_pad = -1e+30

def layer_norm(values, gain):
    mean = lax.optimization_barrier(jnp.mean(values, axis=-1, keepdims=True))
    centered = values - mean
    spread = lax.optimization_barrier(jnp.mean(centered * centered, axis=-1, keepdims=True))
    return centered * lax.rsqrt(spread + epsilon) * gain

def gelu_tanh(values):
    return jax.nn.gelu(values, approximate=True)

def matmul(left, right):
    return jnp.dot(left, right, precision=lax.Precision.HIGHEST, preferred_element_type=jnp.float32)

def attend_block(block):
    joint, segment = block
    group, length = segment.shape
    parts = joint.reshape(group, length, 3, HEADS, HEAD_DIM)
    query = parts[:, :, 0]
    keys = parts[:, :, 1]
    values = parts[:, :, 2]
    raw = jnp.einsum('gqhd,gkhd->ghqk', query, keys, precision=lax.Precision.HIGHEST) * (1.0 / math.sqrt(HEAD_DIM))
    position = jnp.arange(length, dtype=jnp.int32)
    causal = position[:, None] >= position[None, :]
    allowed = causal[None] & (segment[:, :, None] == segment[:, None, :])
    scores = low_back(jnp.where(allowed[:, None], raw, hidden_pad))
    weights = low(jax.nn.softmax(scores, axis=-1))
    out = jnp.einsum('ghqk,gkhd->gqhd', weights, values, precision=lax.Precision.HIGHEST)
    return out.reshape(group, length, HEADS * HEAD_DIM)

def layer_forward(inputs, gain_attend, joint_weight, merge_weight, gain_feed, up_weight, down_weight, router_weight, mix_weight, widen_weight, narrow_weight, onehot, slot, segments):
    first = low(layer_norm(inputs, gain_attend))
    joint = low(low_back(matmul(first, joint_weight)))
    group = math.gcd(SEQS, max(1, 4096 // TOK_DEV))
    blocks = (joint.reshape(SEQS // group, group, TOK_DEV, 3 * D), segments.reshape(SEQS // group, group, TOK_DEV))
    attended = lax.map(jax.checkpoint(attend_block), blocks).reshape(TOKENS, D)
    attended = low(low_back(attended))
    residual = inputs + low_back(matmul(attended, merge_weight))
    second = low(layer_norm(residual, gain_feed))
    act = low(gelu_tanh(low_back(matmul(second, up_weight))))
    dense = low_back(matmul(act, down_weight))
    chances = jax.nn.softmax(low_back(matmul(second, router_weight)), axis=-1)
    gate = lax.optimization_barrier(jnp.sum(chances * onehot, axis=1))
    mix = jax.nn.softmax(low_back(matmul(second, mix_weight)), axis=-1)
    rows = jnp.zeros((EXPERTS * SEQS * CAP, D), jnp.float32).at[slot].set(low_back(second))
    rows = rows.reshape(EXPERTS, SEQS * CAP, D)
    upper = low_back(jnp.einsum('erd,edf->erf', rows, widen_weight, precision=lax.Precision.HIGHEST))
    expert_act = low(gelu_tanh(upper))
    expert_out = low(low_back(jnp.einsum('erf,efd->erd', expert_act, narrow_weight, precision=lax.Precision.HIGHEST)))
    returned = expert_out.reshape(EXPERTS * SEQS * CAP, D)[slot]
    return residual + mix[:, 0:1] * dense + mix[:, 1:2] * gate[:, None] * returned

def reference(tokens, gain_attend, joint_weight, merge_weight, gain_feed, up_weight, down_weight, router_weight, mix_weight, widen_weight, narrow_weight, routes, segments, cotangent):
    chosen = routes[:, 0].astype(jnp.int32)
    onehot_int = (chosen[:, None] == jnp.arange(EXPERTS, dtype=jnp.int32)[None, :]).astype(jnp.int32)
    counted = jnp.cumsum(onehot_int.reshape(SEQS, TOK_DEV, EXPERTS), axis=1).reshape(TOKENS, EXPERTS)
    rank = lax.optimization_barrier(jnp.sum((counted - 1) * onehot_int, axis=1))
    sequence = jnp.arange(TOKENS, dtype=jnp.int32) // TOK_DEV
    slot = (chosen * (SEQS * CAP) + sequence * CAP + rank).astype(jnp.int32)
    onehot = onehot_int.astype(jnp.float32)

    def forward(a0, a1, a2, a3, a4, a5, a6, a7, a8, a9, a10):
        return layer_forward(a0, a1, a2, a3, a4, a5, a6, a7, a8, a9, a10, onehot, slot, segments)
    output, pullback = jax.vjp(forward, tokens.astype(jnp.float32), gain_attend.astype(jnp.float32), joint_weight.astype(jnp.float32), merge_weight.astype(jnp.float32), gain_feed.astype(jnp.float32), up_weight.astype(jnp.float32), down_weight.astype(jnp.float32), router_weight.astype(jnp.float32), mix_weight.astype(jnp.float32), widen_weight.astype(jnp.float32), narrow_weight.astype(jnp.float32))
    grads = pullback(cotangent.astype(jnp.float32))
    return (output.astype(jnp.bfloat16), grads[0].astype(jnp.bfloat16), grads[1], grads[2], grads[3], grads[4], grads[5], grads[6], grads[7], grads[8], grads[9], grads[10])
```

```python
import math

import jax
import jax.numpy as jnp
from jax import lax
from jax.sharding import PartitionSpec as P

HEAD_DIM = 64
TEAM = 8
EPSILON = 1e-05
HIDDEN = -1e30
F32 = jnp.float32
BF16 = jnp.bfloat16


def dot(left, right):
    return jnp.dot(left, right, preferred_element_type=F32)


def dot_tn(left, right):
    return lax.dot_general(left, right, (((0,), (0,)), ((), ())), preferred_element_type=F32)


def dot_nt(left, right):
    return lax.dot_general(left, right, (((1,), (1,)), ((), ())), preferred_element_type=F32)


def gelu(values):
    return jax.nn.gelu(values, approximate=True)


def gelu_grad(values, grad):
    return jax.vjp(gelu, values)[1](grad)[0]


def normed(values):
    mean = jnp.mean(values, axis=-1, keepdims=True)
    centered = values - mean
    spread = jnp.mean(centered * centered, axis=-1, keepdims=True)
    scale = lax.rsqrt(spread + EPSILON)
    return centered * scale, scale


def norm_back(dn, unit, scale):
    return scale * (
        dn
        - jnp.mean(dn, axis=-1, keepdims=True)
        - unit * jnp.mean(dn * unit, axis=-1, keepdims=True)
    )


def body(
    tokens,
    gain_attend,
    joint_weight,
    merge_weight,
    gain_feed,
    up_weight,
    down_weight,
    router_weight,
    mix_weight,
    widen_weight,
    narrow_weight,
    routes,
    segments,
    cotangent,
):
    count = lax.axis_size("expert")
    teams = count // TEAM
    me = lax.axis_index("expert")
    place_in_team = me % TEAM
    length, width = tokens.shape
    capacity = max(2, 2 * length // count)
    planes = [[g * TEAM + p for p in range(TEAM)] for g in range(teams)]
    lines = [[g * TEAM + p for g in range(teams)] for p in range(TEAM)]
    rows = joint_weight.shape[0]
    slice_width = width // TEAM
    hidden = up_weight.shape[1]
    block = hidden // count

    def swap(value, mask):
        return lax.ppermute(value, "expert", [(i, i ^ mask) for i in range(count)])

    def exchange(value):
        return lax.all_to_all(value, "expert", 0, 0, tiled=True)

    def team_exchange(value):
        return lax.all_to_all(value, "expert", 0, 0, tiled=True, axis_index_groups=planes)

    def team_gather(value):
        near = jnp.stack([value, swap(value, 2), swap(value, 4), swap(value, 6)])
        return jnp.concatenate([near, swap(near, 1)])

    def team_scatter(value):
        half = value[:4] + swap(value[4:].astype(BF16), 1).astype(F32)
        sent = half.astype(BF16)
        return half[0] + sum(swap(sent[j], 2 * j).astype(F32) for j in (1, 2, 3))

    relative = jnp.array([2 * j + k for k in range(2) for j in range(4)], jnp.int32)
    members = place_in_team ^ relative
    inverse = jnp.array([(m % 2) * 4 + m // 2 for m in range(8)], jnp.int32)
    places = inverse[place_in_team ^ jnp.arange(8, dtype=jnp.int32)]

    small = jnp.concatenate(
        [router_weight, mix_weight, gain_attend[:, None], gain_feed[:, None]], axis=1
    )
    small_width = -(-small.shape[1] // 128) * 128
    small = jnp.pad(small, ((0, 0), (0, small_width - small.shape[1])))
    pack = joint_weight.reshape(rows, 3, TEAM, slice_width).transpose(2, 0, 1, 3)
    pack = pack.reshape(TEAM, rows, 3 * slice_width)
    pack = jnp.concatenate(
        [pack, jnp.broadcast_to(small[None], (TEAM, rows, small_width))], axis=2
    )
    pack = jnp.broadcast_to(pack[None], (teams,) + pack.shape).reshape(count, rows, -1)
    got = exchange(pack).reshape(width, -1)
    joint_part = got[:, : 3 * slice_width]
    small = got[:, 3 * slice_width :]
    router = small[:, :count]
    mix_w = small[:, count : count + 2]
    gain_a = small[:, count + 2].astype(F32)
    gain_f = small[:, count + 3].astype(F32)

    merge = lax.all_gather(merge_weight, "expert", axis=0, tiled=True)
    up_part = up_weight.reshape(rows, teams, TEAM, block).transpose(2, 0, 1, 3)
    up_part = team_exchange(up_part.reshape(TEAM, rows, teams * block)).reshape(TEAM * rows, -1)
    up_part = lax.all_gather(up_part, "expert", axis=0, tiled=True, axis_index_groups=lines)
    down_part = lax.all_gather(down_weight, "expert", axis=0, tiled=True, axis_index_groups=lines)

    x_all = team_gather(tokens).reshape(-1, width).astype(F32)
    segment = team_gather(segments)[:, 0]
    unit_a, scale_a = normed(x_all)
    first = (unit_a * gain_a).astype(BF16)
    joint = dot(first, joint_part).astype(BF16)
    heads = slice_width // HEAD_DIM
    parts = joint.reshape(TEAM, length, 3, heads, HEAD_DIM)
    query, keys, values = parts[:, :, 0], parts[:, :, 1], parts[:, :, 2]
    shrink = 1.0 / math.sqrt(HEAD_DIM)
    scores = jnp.einsum("gqhd,gkhd->ghqk", query, keys, preferred_element_type=F32) * shrink
    position = jnp.arange(length)
    allowed = (position[:, None] >= position[None, :]) & (
        segment[:, :, None] == segment[:, None, :]
    )
    scores = jnp.where(allowed[:, None], scores, HIDDEN)
    top = jnp.max(scores, axis=-1, keepdims=True)
    chance = jnp.exp(scores - top)
    chance = chance / jnp.sum(chance, axis=-1, keepdims=True)
    weights = chance.astype(BF16)
    attended = jnp.einsum("ghqk,gkhd->gqhd", weights, values, preferred_element_type=F32)
    attended_part = attended.astype(BF16).reshape(TEAM, length, slice_width)
    attended = team_exchange(attended_part[places])
    attended = attended.transpose(1, 0, 2).reshape(length, width)

    x = tokens.astype(F32)
    residual = x + dot(attended, merge)
    unit_f, scale_f = normed(residual)
    second = (unit_f * gain_f).astype(BF16)
    grad = cotangent.astype(F32)
    onehot = (routes == jnp.arange(count, dtype=jnp.int32)[None]).astype(F32)
    rank = jnp.sum((jnp.cumsum(onehot, axis=0) - 1.0) * onehot, axis=1).astype(jnp.int32)
    slot = routes[:, 0] * capacity + rank
    placing = (jnp.arange(count * capacity, dtype=jnp.int32)[:, None] == slot[None]).astype(BF16)
    chances = jax.nn.softmax(dot(second, router), axis=-1)
    gate = jnp.sum(chances * onehot, axis=1, keepdims=True)
    mix = jax.nn.softmax(dot(second, mix_w), axis=-1)
    d_out = (grad * (mix[:, 1:2] * gate)).astype(BF16)
    outgoing = dot(placing, jnp.concatenate([second, d_out], axis=1)).astype(BF16)
    received = exchange(outgoing.reshape(count, capacity, -1)).reshape(count * capacity, -1)

    widen, narrow = widen_weight[0], narrow_weight[0]
    expert_rows, d_expert = received[:, :width], received[:, width:]
    expert_upper = dot(expert_rows, widen)
    expert_act = gelu(expert_upper).astype(BF16)
    expert_out = dot(expert_act, narrow).astype(BF16)
    d_eupper = gelu_grad(expert_upper, dot_nt(d_expert, narrow)).astype(BF16)
    d_rows = dot_nt(d_eupper, widen).astype(BF16)
    back = jnp.concatenate([expert_out, d_rows], axis=1).reshape(count, capacity, -1)
    back = exchange(back).reshape(count * capacity, -1)
    narrow_grad = dot_tn(expert_act, d_expert)[None]
    widen_grad = dot_tn(expert_rows, d_eupper)[None]

    second_all = team_gather(second).reshape(-1, width)
    grad_all = team_gather(cotangent).reshape(-1, width).astype(F32)
    upper = dot(second_all, up_part)
    act = gelu(upper).astype(BF16)
    dense = team_scatter(dot(act, down_part).reshape(TEAM, length, width))
    mix_all = jax.nn.softmax(dot(second_all, mix_w), axis=-1)
    d_dense = (grad_all * mix_all[:, 0:1]).astype(BF16)
    down_grad = dot_tn(act, d_dense).astype(BF16)
    d_upper = gelu_grad(upper, dot_nt(d_dense, down_part)).astype(BF16)
    up_grad = dot_tn(second_all, d_upper).astype(BF16)
    d_second = team_scatter(dot_nt(d_upper, up_part).reshape(TEAM, length, width))
    down_grad = lax.all_to_all(
        down_grad.reshape(teams, block, width), "expert", 0, 0, tiled=True, axis_index_groups=lines
    )
    down_grad = jnp.sum(down_grad.astype(F32), axis=0)
    up_grad = exchange(up_grad.reshape(count, rows, teams * block))
    up_grad = jnp.sum(up_grad.reshape(teams, TEAM, rows, teams, block).astype(F32), axis=0)
    up_grad = up_grad.transpose(1, 2, 0, 3).reshape(rows, hidden)

    back = dot_tn(placing, back)
    returned, d_back = back[:, :width], back[:, width:]
    result = residual + mix[:, 0:1] * dense + mix[:, 1:2] * gate * returned
    along = jnp.sum(grad * returned, axis=1, keepdims=True)
    d_mixcol = jnp.concatenate([jnp.sum(grad * dense, axis=1, keepdims=True), gate * along], axis=1)
    d_mixlog = (mix * (d_mixcol - jnp.sum(mix * d_mixcol, axis=1, keepdims=True))).astype(BF16)
    d_logits = (chances * (onehot - gate) * (mix[:, 1:2] * along)).astype(BF16)
    d_second = d_second + d_back + dot_nt(d_logits, router) + dot_nt(d_mixlog, mix_w)
    feed_grad = jnp.sum(d_second * unit_f, axis=0)
    d_residual = grad + norm_back(d_second * gain_f, unit_f, scale_f)
    d_merged = d_residual.astype(BF16)

    side = jnp.concatenate([d_logits, d_mixlog], axis=1)
    side = jnp.pad(side, ((0, 0), (0, small_width - side.shape[1])))
    sent = jnp.concatenate([d_merged, side], axis=1)
    last = jnp.pad(feed_grad.astype(BF16)[None], ((0, 15), (0, small_width)))
    sent = team_gather(jnp.concatenate([sent, last], axis=0))
    d_merged_all = sent[:, :length, :width].reshape(-1, width)
    side_all = sent[:, :length, width:].reshape(-1, small_width)
    feed_part = jnp.sum(sent[:, length, :width].astype(F32), axis=0)
    start = place_in_team * slice_width
    merge_part = lax.dynamic_slice(merge, (start, 0), (slice_width, width))
    d_attended = dot_nt(d_merged_all, merge_part).astype(BF16)
    merge_grad = dot_tn(attended_part.reshape(-1, slice_width), d_merged_all)
    second_part = lax.dynamic_slice(second_all, (0, start), (TEAM * length, slice_width))
    side_grad = dot_tn(second_part, side_all)
    feed_part = lax.dynamic_slice(feed_part, (start,), (slice_width,))
    side_grad = side_grad.at[:, count + 2].set(feed_part)
    merge_grad = jnp.concatenate([merge_grad, side_grad], axis=1).astype(BF16)
    merge_grad = lax.psum_scatter(
        merge_grad, "expert", scatter_dimension=0, tiled=True, axis_index_groups=lines
    )
    merge_grad = lax.ppermute(
        merge_grad,
        "expert",
        [(g * TEAM + p, p * teams + g) for g in range(teams) for p in range(TEAM)],
    ).astype(F32)

    d_attended = d_attended.reshape(TEAM, length, heads, HEAD_DIM)
    d_weights = jnp.einsum("gqhd,gkhd->ghqk", d_attended, values, preferred_element_type=F32)
    d_scores = chance * (d_weights - jnp.sum(chance * d_weights, axis=-1, keepdims=True))
    d_scores = d_scores.astype(BF16)
    d_query = jnp.einsum("ghqk,gkhd->gqhd", d_scores, keys, preferred_element_type=F32) * shrink
    d_keys = jnp.einsum("ghqk,gqhd->gkhd", d_scores, query, preferred_element_type=F32) * shrink
    d_values = jnp.einsum("ghqk,gqhd->gkhd", weights, d_attended, preferred_element_type=F32)
    d_joint = jnp.stack([d_query, d_keys, d_values], axis=2).astype(BF16)
    d_joint = d_joint.reshape(TEAM * length, 3 * slice_width)
    d_first = dot_nt(d_joint, joint_part)
    attend_part = jnp.sum(d_first * unit_a, axis=0)
    joint_grad = dot_tn(first, d_joint)
    joint_grad = jnp.concatenate(
        [joint_grad, jnp.pad(attend_part[:, None], ((0, 0), (0, 127)))], axis=1
    ).astype(BF16)
    joint_grad = exchange(joint_grad.reshape(count, rows, -1))
    joint_grad = jnp.sum(joint_grad.reshape(teams, TEAM, rows, -1).astype(F32), axis=0)
    attend_grad = jnp.sum(joint_grad[:, :, 3 * slice_width], axis=0)
    joint_grad = joint_grad[:, :, : 3 * slice_width].reshape(TEAM, rows, 3, slice_width)
    joint_grad = joint_grad.transpose(1, 2, 0, 3).reshape(rows, 3 * width)
    d_first = team_scatter(d_first.reshape(TEAM, length, width))
    unit_x, scale_x = normed(x)
    tokens_grad = (d_residual + norm_back(d_first * gain_a, unit_x, scale_x)).astype(BF16)

    return (
        result.astype(BF16),
        tokens_grad,
        attend_grad,
        joint_grad,
        merge_grad[:, :width],
        merge_grad[:, width + count + 2],
        up_grad,
        down_grad,
        merge_grad[:, width : width + count],
        merge_grad[:, width + count : width + count + 2],
        widen_grad,
        narrow_grad,
    )


def solution(mesh):
    one, two, three = P("expert"), P("expert", None), P("expert", None, None)
    return jax.shard_map(
        body,
        mesh=mesh,
        in_specs=(two, one, two, two, one, two, two, two, two, three, three, two, two, two),
        out_specs=(two, two, one, two, two, one, two, two, two, two, three, three),
        check_vma=False,
    )
```

```python
import functools
import math

import jax
import jax.numpy as jnp
from jax import lax
from jax.experimental import pallas as pl
from jax.experimental.pallas import tpu as pltpu
from jax.sharding import PartitionSpec as P

HEAD_DIM = 64
TEAM = 8
EPSILON = 1e-05
HIDDEN = -1e30
F32 = jnp.float32
BF16 = jnp.bfloat16
CURVE = math.sqrt(2.0 / math.pi)
MIB = 1 << 20


def dot(left, right):
    return jnp.dot(left, right, preferred_element_type=F32)


def dot_tn(left, right):
    return lax.dot_general(left, right, (((0,), (0,)), ((), ())), preferred_element_type=F32)


def dot_nt(left, right):
    return lax.dot_general(left, right, (((1,), (1,)), ((), ())), preferred_element_type=F32)


def gelu_both(u):
    square = u * u
    bent = jnp.tanh(CURVE * u * (1.0 + 0.044715 * square))
    half = 0.5 * (1.0 + bent)
    slope = half + 0.5 * CURVE * u * (1.0 - bent * bent) * (1.0 + 0.134145 * square)
    return u * half, slope


def normed(values):
    mean = jnp.mean(values, axis=-1, keepdims=True)
    centered = values - mean
    spread = jnp.mean(centered * centered, axis=-1, keepdims=True)
    scale = lax.rsqrt(spread + EPSILON)
    return centered * scale, scale


def norm_back(dn, unit, scale):
    return scale * (
        dn
        - jnp.mean(dn, axis=-1, keepdims=True)
        - unit * jnp.mean(dn * unit, axis=-1, keepdims=True)
    )


def lanes(shape):
    return lax.broadcasted_iota(jnp.int32, shape, 1)


def sublanes(shape):
    return lax.broadcasted_iota(jnp.int32, shape, 0)


def gain_rows(small, count):
    shape = (8, small.shape[1])
    pick = (lanes(shape) == sublanes(shape) + count + 2) & (sublanes(shape) < 2)
    return dot_nt(jnp.where(pick, 1.0, 0.0).astype(BF16), small)


def column_of(rows, lane, width):
    shape = (rows.shape[0], width)
    pick = jnp.where((lanes(shape) == lane) & (sublanes(shape) == 0), 1.0, 0.0).astype(BF16)
    return dot_tn(rows.astype(BF16), pick)


def visible(segment_row, length):
    shape = (length, length)
    row, column = sublanes(shape), lanes(shape)
    segment = jnp.sum(jnp.where(row == column, segment_row, 0.0), axis=1, keepdims=True)
    return (row >= column) & (segment == segment_row)


def chance_of(query, keys, allowed):
    scores = dot_nt(query, keys) * (1.0 / math.sqrt(HEAD_DIM))
    scores = jnp.where(allowed, scores, HIDDEN)
    grown = jnp.exp(scores - jnp.max(scores, axis=1, keepdims=True))
    return grown * (1.0 / jnp.sum(grown, axis=1, keepdims=True))


def params(mib=56, **more):
    return pltpu.CompilerParams(vmem_limit_bytes=mib * MIB, **more)


def cost(flops=1):
    return pl.CostEstimate(flops=flops, bytes_accessed=1, transcendentals=0)


def shaped(dtype, *shape):
    return jax.ShapeDtypeStruct(shape, dtype)


def pack_kernel(
    joint_ref, up_ref, router_ref, mix_ref, gain_a_ref, gain_f_ref, pack_ref, *, teams
):
    rows = joint_ref.shape[0]
    width = joint_ref.shape[1] // 3
    part = width // TEAM
    block = up_ref.shape[1] // (teams * TEAM)
    count = router_ref.shape[1]
    wide = pack_ref.shape[2] - teams * block
    shape = (rows, wide - 3 * part)
    spread = (count, shape[1])
    spread = jnp.where(lanes(spread) == sublanes(spread), 1.0, 0.0).astype(BF16)
    small = dot(router_ref[...], spread)
    lane = lanes(shape)
    square = (rows, rows)
    same = sublanes(square) == lanes(square)
    columns = [mix_ref[0:1], mix_ref[1:2], gain_a_ref[...], gain_f_ref[...]]
    for i, row in enumerate(columns):
        column = jnp.sum(jnp.where(same, row.astype(F32), 0.0), axis=1, keepdims=True)
        small += jnp.where(lane == count + i, column, 0.0)
    small = small.astype(BF16)
    for p in range(TEAM):
        pieces = [joint_ref[:, c * width + p * part : c * width + (p + 1) * part] for c in range(3)]
        for g in range(teams):
            start = (g * TEAM + p) * block
            pieces.append(up_ref[:, start : start + block])
        pack_ref[p] = jnp.concatenate(pieces[:3] + [small] + pieces[3:], axis=1)


def attend_kernel(
    place_ref, near_ref, far_ref, near_seg, far_seg, got_ref, joint_ref, out_ref, *, count
):
    length = out_ref.shape[1]
    part = out_ref.shape[2]
    gains = gain_rows(got_ref[:, 3 * part :], count)
    x = jnp.concatenate([near_ref[0], far_ref[0]], axis=0).astype(F32)
    unit, _ = normed(x)
    first = (unit * gains[0:1]).astype(BF16)
    joint = dot(first, got_ref[:, : 3 * part]).astype(BF16)
    lane = lanes((length, part))
    for k, ref in enumerate((near_seg, far_seg)):
        allowed = visible(ref[0, :, :length].astype(F32)[0:1], length)
        own = joint[k * length : (k + 1) * length]
        query, keys, values = own[:, :part], own[:, part : 2 * part], own[:, 2 * part :]
        total = jnp.zeros((length, part), F32)
        for h in range(part // HEAD_DIM):
            mine = lane // HEAD_DIM == h
            chance = chance_of(jnp.where(mine, query, 0), keys, allowed)
            total += dot(chance.astype(BF16), jnp.where(mine, values, 0))
        slot = (place_ref[0] & 1) ^ k
        joint_ref[slot] = own
        out_ref[slot] = total.astype(BF16)


def attend(place, near, far, got, length, count):
    half, _, width = near.shape
    part = width // TEAM
    pair = lambda j, place: ((place[0] >> 1) ^ j, 0, 0)
    block = pl.BlockSpec((1, length, width), lambda j, place: (j, 0, 0))
    segs = pl.BlockSpec((1, 16, width), lambda j, place: (j, length // 16, 0))
    outs = (shaped(BF16, TEAM, length, 3 * part), shaped(BF16, TEAM, length, part))
    return pl.pallas_call(
        functools.partial(attend_kernel, count=count),
        grid_spec=pltpu.PrefetchScalarGridSpec(
            num_scalar_prefetch=1,
            grid=(half,),
            in_specs=[block, block, segs, segs, pl.BlockSpec(got.shape, lambda j, place: (0, 0))],
            out_specs=[
                pl.BlockSpec((2, length, 3 * part), pair),
                pl.BlockSpec((2, length, part), pair),
            ],
        ),
        out_shape=outs,
        compiler_params=params(),
        cost_estimate=cost(),
        name="attend",
    )(place, near, far, near, far, got)


def attend_back_kernel(
    place_ref, near_ref, far_ref, near_seg, far_seg, near_att, far_att, got_ref, joint_ref, d_ref,
    side_ref, keep_ref, send_ref, grad_ref, grad_acc, merge_acc, gain_acc, *, count,
):
    step = pl.program_id(0)
    length = joint_ref.shape[1]
    part = d_ref.shape[2]
    shrink = 1.0 / math.sqrt(HEAD_DIM)
    gains = gain_rows(got_ref[:, 3 * part :], count)
    x = jnp.concatenate([near_ref[0], far_ref[0]], axis=0).astype(F32)
    unit, _ = normed(x)
    first = (unit * gains[0:1]).astype(BF16)
    lane = lanes((length, part))
    d_joints = []
    d_merged = []
    for k, ref in enumerate((near_seg, far_seg)):
        allowed = visible(ref[0, :, :length].astype(F32)[0:1], length)
        slot = (place_ref[0] & 1) ^ k
        own = joint_ref[slot]
        both = d_ref[slot]
        d_own = both[:length]
        d_merged.append(both[length:])
        query, keys, values = own[:, :part], own[:, part : 2 * part], own[:, 2 * part :]
        d_query = jnp.zeros((length, part), F32)
        d_keys = jnp.zeros((length, part), F32)
        d_values = jnp.zeros((length, part), F32)
        for h in range(part // HEAD_DIM):
            mine = lane // HEAD_DIM == h
            q = jnp.where(mine, query, 0)
            d_head = jnp.where(mine, d_own, 0)
            chance = chance_of(q, keys, allowed)
            d_weights = dot_nt(d_head, values)
            inner = jnp.sum(chance * d_weights, axis=1, keepdims=True)
            d_scores = (chance * (d_weights - inner)).astype(BF16)
            d_query += dot(d_scores, jnp.where(mine, keys, 0))
            d_keys += dot_tn(d_scores, q)
            d_values += dot_tn(chance.astype(BF16), d_head)
        d_joints.append(
            jnp.concatenate([d_query * shrink, d_keys * shrink, d_values], axis=1).astype(BF16)
        )
    d_joint = jnp.concatenate(d_joints, axis=0)
    d_first = dot_nt(d_joint, got_ref[:, : 3 * part])
    keep_ref[0] = d_first[:length]
    send_ref[0] = d_first[length:].astype(BF16)
    attended = jnp.concatenate([near_att[0], far_att[0]], axis=0)

    @pl.when(step == 0)
    def _():
        grad_acc[...] = jnp.zeros_like(grad_acc)
        merge_acc[...] = jnp.zeros_like(merge_acc)
        gain_acc[...] = jnp.zeros_like(gain_acc)

    grad_acc[...] += dot_tn(first, d_joint)
    merge_acc[...] += dot_tn(attended, jnp.concatenate(d_merged, axis=0))
    gain_acc[0:1] += jnp.sum(d_first * unit, axis=0, keepdims=True)

    @pl.when(step == pl.num_programs(0) - 1)
    def _():
        grad_ref[:, : 3 * part] = grad_acc[...].astype(BF16)
        gain = column_of(gain_acc[...], count + 3, side_ref.shape[1])
        grad_ref[:, 3 * part : -part] = (side_ref[...] + gain).astype(BF16)
        grad_ref[:, -part:] = merge_acc[...].astype(BF16)


def attend_back(place, near, far, near_att, far_att, got, joint, d_both, side, count):
    half, _, width = near.shape
    length = joint.shape[1]
    part = width // TEAM
    pair = lambda j, place: ((place[0] >> 1) ^ j, 0, 0)
    step = lambda j, place: (j, 0, 0)
    whole = lambda j, place: (0, 0)
    block = pl.BlockSpec((1, length, width), step)
    segs = pl.BlockSpec((1, 16, width), lambda j, place: (j, length // 16, 0))
    outs = (
        shaped(F32, half, length, width),
        shaped(BF16, half, length, width),
        shaped(BF16, width, 4 * part + side.shape[1]),
    )
    return pl.pallas_call(
        functools.partial(attend_back_kernel, count=count),
        grid_spec=pltpu.PrefetchScalarGridSpec(
            num_scalar_prefetch=1,
            grid=(half,),
            in_specs=[
                block,
                block,
                segs,
                segs,
                block,
                block,
                pl.BlockSpec(got.shape, whole),
                pl.BlockSpec((2, length, 3 * part), pair),
                pl.BlockSpec((2, 2 * length, part), pair),
                pl.BlockSpec(side.shape, whole),
            ],
            out_specs=[block, block, pl.BlockSpec(outs[2].shape, whole)],
            scratch_shapes=[
                pltpu.VMEM((width, 3 * part), F32),
                pltpu.VMEM((width, part), F32),
                pltpu.VMEM((8, width), F32),
            ],
        ),
        out_shape=outs,
        compiler_params=params(),
        cost_estimate=cost(int(2e10)),
        name="attend_back",
    )(place, near, far, near, far, near_att, far_att, got, joint, d_both, side)


def middle_kernel(
    att_ref, merge_ref, x_ref, g_ref, small_ref, routes_ref,
    residual_ref, second_ref, attended_ref, stats_ref, placing_ref, out_ref, *, count, capacity,
):
    length, width = x_ref.shape
    small = small_ref[:, 3 * width // TEAM :]
    gains = gain_rows(small, count)
    attended = jnp.concatenate([att_ref[p] for p in range(TEAM)], axis=1)
    residual = x_ref[...].astype(F32) + dot(attended, merge_ref[...])
    residual_ref[...] = residual
    unit, _ = normed(residual)
    second = (unit * gains[1:2]).astype(BF16)
    second_ref[...] = second
    attended_ref[...] = attended
    logits = dot(second, small)
    lane = lanes(logits.shape)
    routed = jnp.where(lane < count, logits, HIDDEN)
    grown = jnp.exp(routed - jnp.max(routed, axis=1, keepdims=True))
    chances = grown * (1.0 / jnp.sum(grown, axis=1, keepdims=True))
    mixed = jnp.where((lane >= count) & (lane < count + 2), logits, HIDDEN)
    grown = jnp.exp(mixed - jnp.max(mixed, axis=1, keepdims=True))
    mix = grown * (1.0 / jnp.sum(grown, axis=1, keepdims=True))
    routes = routes_ref[...]
    onehot = lane == routes
    gate = jnp.sum(jnp.where(onehot, chances, 0.0), axis=1, keepdims=True)
    mix_expert = jnp.sum(jnp.where(lane == count + 1, mix, 0.0), axis=1, keepdims=True)
    stats_ref[...] = chances + mix + jnp.where(lane == count + 2, gate, 0.0)
    shape = (length, length)
    before = jnp.where(sublanes(shape) > lanes(shape), 1.0, 0.0).astype(BF16)
    marked = jnp.where(onehot, 1.0, 0.0)
    rank = jnp.sum(marked * dot(before, marked.astype(BF16)), axis=1, keepdims=True)
    slot = routes * capacity + rank.astype(jnp.int32)
    placing = jnp.where(lanes((length, count * capacity)) == slot, 1.0, 0.0).astype(BF16)
    placing_ref[...] = placing
    d_out = (g_ref[...].astype(F32) * (mix_expert * gate)).astype(BF16)
    out_ref[:, :width] = dot_tn(placing, second).astype(BF16)
    out_ref[:, width:] = dot_tn(placing, d_out).astype(BF16)


def middle(att, merge, tokens, cotangent, got, routes, count, capacity):
    length, width = tokens.shape
    lanes_small = got.shape[1] - 3 * width // TEAM
    outs = (
        shaped(F32, length, width),
        shaped(BF16, length, width),
        shaped(BF16, length, width),
        shaped(F32, length, lanes_small),
        shaped(BF16, length, count * capacity),
        shaped(BF16, count * capacity, 2 * width),
    )
    return pl.pallas_call(
        functools.partial(middle_kernel, count=count, capacity=capacity),
        out_shape=outs,
        compiler_params=params(),
        cost_estimate=cost(),
        name="middle",
    )(att, merge, tokens, cotangent, got, routes)


def expert_kernel(rows_ref, widen_ref, narrow_ref, act_ref, d_ref, back_ref, acc):
    step = pl.program_id(0)
    width = rows_ref.shape[1] // 2
    upper = dot(rows_ref[:, :width], widen_ref[0])
    act, slope = gelu_both(upper)
    act = act.astype(BF16)
    act_ref[...] = act
    d_upper = (slope * dot_nt(rows_ref[:, width:], narrow_ref[0])).astype(BF16)
    d_ref[...] = d_upper

    @pl.when(step == 0)
    def _():
        acc[...] = jnp.zeros_like(acc)

    acc[:, :width] += dot(act, narrow_ref[0])
    acc[:, width:] += dot_nt(d_upper, widen_ref[0])

    @pl.when(step == pl.num_programs(0) - 1)
    def _():
        back_ref[...] = acc[...].astype(BF16)


def expert(rows, widen, narrow, chunk=512):
    slots, width = rows.shape[0], rows.shape[1] // 2
    hidden = widen.shape[2]
    outs = (
        shaped(BF16, slots, hidden),
        shaped(BF16, slots, hidden),
        shaped(BF16, slots, 2 * width),
    )
    piece = pl.BlockSpec((slots, chunk), lambda f: (0, f))
    whole = pl.BlockSpec((slots, 2 * width), lambda f: (0, 0))
    return pl.pallas_call(
        expert_kernel,
        grid=(hidden // chunk,),
        in_specs=[
            whole,
            pl.BlockSpec((1, width, chunk), lambda f: (0, 0, f)),
            pl.BlockSpec((1, chunk, width), lambda f: (0, f, 0)),
        ],
        out_specs=[piece, piece, whole],
        out_shape=outs,
        scratch_shapes=[pltpu.VMEM((slots, 2 * width), F32)],
        compiler_params=params(),
        cost_estimate=cost(),
        name="expert",
    )(rows, widen, narrow)


def narrow_grad_kernel(rows_ref, act_ref, out_ref):
    out_ref[0] = dot_tn(act_ref[...], rows_ref[...])


def narrow_grads(rows, act, chunk=512):
    slots, width = rows.shape[0], rows.shape[1] // 2
    hidden = act.shape[1]
    return pl.pallas_call(
        narrow_grad_kernel,
        grid=(hidden // chunk,),
        in_specs=[
            pl.BlockSpec((slots, width), lambda f: (0, 1)),
            pl.BlockSpec((slots, chunk), lambda f: (0, f)),
        ],
        out_specs=pl.BlockSpec((1, chunk, width), lambda f: (0, f, 0)),
        out_shape=shaped(F32, 1, hidden, width),
        compiler_params=params(),
        cost_estimate=cost(),
        name="narrow_grads",
    )(rows, act)


def widen_grad_kernel(rows_ref, d_ref, out_ref):
    out_ref[0] = dot_tn(rows_ref[...], d_ref[...])


def widen_grads(rows, d_upper, chunk=128):
    slots, width = rows.shape[0], rows.shape[1] // 2
    hidden = d_upper.shape[1]
    return pl.pallas_call(
        widen_grad_kernel,
        grid=(width // chunk,),
        in_specs=[
            pl.BlockSpec((slots, chunk), lambda f: (0, f)),
            pl.BlockSpec((slots, hidden), lambda f: (0, 0)),
        ],
        out_specs=pl.BlockSpec((1, chunk, hidden), lambda f: (0, f, 0)),
        out_shape=shaped(F32, 1, width, hidden),
        compiler_params=params(),
        cost_estimate=cost(),
        name="widen_grads",
    )(rows, d_upper)


def feed_kernel(
    near_ref, far_ref, g_near_ref, g_far_ref, both_ref, small_ref,
    keep_ref, low_ref, high_ref, keep_dense_ref, send_dense_ref, up_grad_ref, down_grad_ref,
    up_acc, down_acc, up_ref, down_ref, *, count,
):
    step = pl.program_id(0)
    length, width = near_ref.shape[1:]

    @pl.when(step == 0)
    def _():
        up_acc[...] = jnp.zeros_like(up_acc)
        down_acc[...] = jnp.zeros_like(down_acc)
        hidden = up_ref.shape[1]
        tall = both_ref.shape[1] // 2
        for g in range(both_ref.shape[0]):
            down_ref[g * tall : (g + 1) * tall] = both_ref[g, :tall]
            for i in range(width // hidden):
                start = (g * (width // hidden) + i) * tall
                up_ref[start : start + tall] = both_ref[g, tall:, i * hidden : (i + 1) * hidden]

    second = jnp.concatenate([near_ref[0], far_ref[0]], axis=0)
    g = jnp.concatenate([g_near_ref[0], g_far_ref[0]], axis=0).astype(F32)
    logits = dot(second, small_ref[:, 3 * width // TEAM :])
    lane = lanes(logits.shape)
    mixed = jnp.where((lane >= count) & (lane < count + 2), logits, HIDDEN)
    grown = jnp.exp(mixed - jnp.max(mixed, axis=1, keepdims=True))
    mix = jnp.sum(jnp.where(lane == count, grown, 0.0), axis=1, keepdims=True)
    mix = mix * (1.0 / jnp.sum(grown, axis=1, keepdims=True))
    d_dense = (g * mix).astype(BF16)
    act, slope = gelu_both(dot(second, up_ref[...]))
    act = act.astype(BF16)
    d_upper = (slope * dot_nt(d_dense, down_ref[...])).astype(BF16)
    d_second = dot_nt(d_upper, up_ref[...])
    dense = dot(act, down_ref[...])
    along = jnp.sum(g * dense, axis=1, keepdims=True)
    rest = along - along.astype(BF16).astype(F32)
    lane = lanes((2 * length, 128))
    along = jnp.where(lane == 0, along, 0.0) + jnp.where(lane == 1, rest, 0.0)
    keep_ref[0, :, :width] = d_second[:length]
    keep_ref[0, :, width:] = along[:length]
    sent = d_second[length:].astype(BF16)
    low_ref[0] = sent[:, : width // 2]
    high_ref[0, :, : width // 2] = sent[:, width // 2 :]
    high_ref[0, :, width // 2 :] = along[length:].astype(BF16)
    keep_dense_ref[0] = dense[:length]
    send_dense_ref[0] = dense[length:].astype(BF16)

    up_acc[...] += dot_tn(second, d_upper)
    down_acc[...] += dot_tn(act, d_dense)

    @pl.when(step == pl.num_programs(0) - 1)
    def _():
        up_grad_ref[...] = up_acc[...].astype(BF16)
        down_grad_ref[...] = down_acc[...].astype(BF16)


def feed(near, far, g_near, g_far, both, got, count):
    half, length, width = near.shape
    hidden = both.shape[0] * both.shape[1] // 2
    block = pl.BlockSpec((1, length, width), lambda j: (j, 0, 0))
    wide = pl.BlockSpec((1, length, width + 128), lambda j: (j, 0, 0))
    low = pl.BlockSpec((1, length, width // 2), lambda j: (j, 0, 0))
    high = pl.BlockSpec((1, length, width // 2 + 128), lambda j: (j, 0, 0))
    whole = lambda a: pl.BlockSpec(a.shape, lambda j: (0,) * len(a.shape))
    outs = (
        shaped(F32, half, length, width + 128),
        shaped(BF16, half, length, width // 2),
        shaped(BF16, half, length, width // 2 + 128),
        shaped(F32, half, length, width),
        shaped(BF16, half, length, width),
        shaped(BF16, width, hidden),
        shaped(BF16, hidden, width),
    )
    return pl.pallas_call(
        functools.partial(feed_kernel, count=count),
        grid=(half,),
        in_specs=[block, block, block, block, whole(both), whole(got)],
        out_specs=[wide, low, high, block, block, whole(outs[5]), whole(outs[6])],
        out_shape=outs,
        scratch_shapes=[
            pltpu.VMEM((width, hidden), F32),
            pltpu.VMEM((hidden, width), F32),
            pltpu.VMEM((width, hidden), BF16),
            pltpu.VMEM((hidden, width), BF16),
        ],
        compiler_params=params(),
        cost_estimate=cost(),
        name="feed",
    )(near, far, g_near, g_far, both, got)


def halve_kernel(keep_ref, *refs, pieces):
    got_refs, own_ref, send_refs = refs[:pieces], refs[pieces], refs[pieces + 1 :]
    start = 0
    for got_ref in got_refs:
        part = slice(start, start + got_ref.shape[2])
        own_ref[:, part] = keep_ref[0, :, part] + got_ref[0].astype(F32)
        for j, ref in enumerate(send_refs):
            total = keep_ref[j + 1, :, part] + got_ref[j + 1].astype(F32)
            ref[:, part] = total.astype(BF16)
        start = part.stop


def halve(keep, got):
    half, length, width = keep.shape
    outs = (shaped(F32, length, width),) + (shaped(BF16, length, width),) * (half - 1)
    return pl.pallas_call(
        functools.partial(halve_kernel, pieces=len(got)),
        out_shape=outs,
        compiler_params=params(),
        cost_estimate=cost(),
        name="halve",
    )(keep, *got)


def after_kernel(
    own_ref, r1_ref, r2_ref, r3_ref, back_ref, placing_ref, residual_ref, stats_ref, g_ref,
    small_ref, merge_ref, routes_ref, second_ref,
    result_ref, d_residual_ref, side_ref, d_ref, *, count,
):
    length, width = g_ref.shape
    part = width // TEAM
    small = small_ref[:, 3 * part :]
    gains = gain_rows(small, count)
    summed = (
        own_ref[...] + r1_ref[...].astype(F32) + r2_ref[...].astype(F32) + r3_ref[...].astype(F32)
    )
    d_second = summed[:, :width]
    d_mix_dense = jnp.sum(summed[:, width:], axis=1, keepdims=True)
    stats = stats_ref[...]
    lane = lanes(stats.shape)
    column = lambda i: jnp.sum(jnp.where(lane == i, stats, 0.0), axis=1, keepdims=True)
    mix_dense, mix_expert, gate = column(count), column(count + 1), column(count + 2)
    residual = residual_ref[...]
    g = g_ref[...].astype(F32)
    returned = dot(placing_ref[...], back_ref[:, :width])
    result_ref[...] = residual + mix_expert * gate * returned
    along = jnp.sum(g * returned, axis=1, keepdims=True)
    d_mix_expert = gate * along
    mean = mix_dense * d_mix_dense + mix_expert * d_mix_expert
    onehot = jnp.where(lane == routes_ref[...], 1.0, 0.0)
    side = jnp.where(lane < count, stats * (onehot - gate) * (mix_expert * along), 0.0)
    side += jnp.where(lane == count, mix_dense * (d_mix_dense - mean), 0.0)
    side += jnp.where(lane == count + 1, mix_expert * (d_mix_expert - mean), 0.0)
    side = side.astype(BF16)
    d_second += dot(placing_ref[...], back_ref[:, width:]) + dot_nt(side, small)
    unit, scale = normed(residual)
    d_residual = g + norm_back(d_second * gains[1:2], unit, scale)
    d_residual_ref[...] = d_residual
    d_merged = d_residual.astype(BF16)
    side_grad = dot_tn(second_ref[...], side)
    feed_row = jnp.sum(d_second * unit, axis=0, keepdims=True)
    feed_rows = jnp.where(sublanes((8, width)) == 0, feed_row, 0.0)
    side_ref[...] = side_grad + column_of(feed_rows, count + 2, side.shape[1])
    d_att = dot_nt(d_merged, merge_ref[...]).astype(BF16)
    for p in range(TEAM):
        d_ref[p, :length] = d_att[:, p * part : (p + 1) * part]
        d_ref[p, length:] = d_merged[:, p * part : (p + 1) * part]


def after(
    own, others, back, placing, residual, stats, cotangent, got, merge, routes, second, count
):
    length, width = cotangent.shape
    part = width // TEAM
    outs = (
        shaped(F32, length, width),
        shaped(F32, length, width),
        shaped(F32, width, got.shape[1] - 3 * part),
        shaped(BF16, TEAM, 2 * length, part),
    )
    return pl.pallas_call(
        functools.partial(after_kernel, count=count),
        out_shape=outs,
        compiler_params=params(),
        cost_estimate=cost(),
        name="after",
    )(own, *others, back, placing, residual, stats, cotangent, got, merge, routes, second)


def last_kernel(
    own_ref, r1_ref, r2_ref, r3_ref, dense_ref, d1_ref, d2_ref, d3_ref, part_ref, stats_ref,
    x_ref, d_residual_ref, small_ref, out_ref, result_ref, *, count,
):
    part = x_ref.shape[1] // TEAM
    gains = gain_rows(small_ref[:, 3 * part :], count)
    add = lambda a, b, c, d: a[...] + b[...].astype(F32) + c[...].astype(F32) + d[...].astype(F32)
    d_first = add(own_ref, r1_ref, r2_ref, r3_ref)
    unit, scale = normed(x_ref[...].astype(F32))
    out_ref[...] = (
        d_residual_ref[...] + norm_back(d_first * gains[0:1], unit, scale)
    ).astype(BF16)
    stats = stats_ref[...]
    mix_dense = jnp.sum(jnp.where(lanes(stats.shape) == count, stats, 0.0), axis=1, keepdims=True)
    dense = add(dense_ref, d1_ref, d2_ref, d3_ref)
    result_ref[...] = (part_ref[...] + mix_dense * dense).astype(BF16)


def last(own, others, dense, more, part, stats, tokens, d_residual, got, count):
    return pl.pallas_call(
        functools.partial(last_kernel, count=count),
        out_shape=(shaped(BF16, *tokens.shape),) * 2,
        compiler_params=params(),
        cost_estimate=cost(),
        name="last",
    )(own, *others, dense, *more, part, stats, tokens, d_residual, got)


def owner_kernel(
    got_ref, joint_ref, merge_ref, up_ref, attend_ref, feed_ref, router_ref, mix_ref, *, teams, count
):
    rows = joint_ref.shape[0]
    part = merge_ref.shape[1] // TEAM
    width = part * TEAM
    block = up_ref.shape[1] // (TEAM * teams)
    wide = got_ref.shape[2] - teams * block
    total = jnp.zeros((rows, wide - 4 * part), F32)
    for p in range(TEAM):
        own = got_ref[p].astype(F32)
        for c in range(3):
            start = c * width + p * part
            joint_ref[:, start : start + part] = own[:, c * part : (c + 1) * part]
        total += own[:, 3 * part : wide - part]
        merge_ref[:, p * part : (p + 1) * part] = own[:, wide - part : wide]
        for g in range(teams):
            start = (g * TEAM + p) * block
            up_ref[:, start : start + block] = own[:, wide + g * block : wide + (g + 1) * block]
    router_ref[...] = total[:, :count]
    same = sublanes((rows, rows)) == lanes((rows, rows))

    def row(lane):
        column = jnp.sum(jnp.where(lanes(total.shape) == lane, total, 0.0), axis=1, keepdims=True)
        return jnp.sum(jnp.where(same, column, 0.0), axis=0, keepdims=True)

    mix_ref[0:1] = row(count)
    mix_ref[1:2] = row(count + 1)
    feed_ref[...] = row(count + 2)
    attend_ref[...] = row(count + 3)


def owner_sums(got, width, hidden, count, teams):
    rows = got.shape[1]
    outs = (
        shaped(F32, rows, 3 * width),
        shaped(F32, rows, width),
        shaped(F32, rows, hidden),
        shaped(F32, 1, rows),
        shaped(F32, 1, rows),
        shaped(F32, rows, count),
        shaped(F32, 2, rows),
    )
    return pl.pallas_call(
        functools.partial(owner_kernel, teams=teams, count=count),
        out_shape=outs,
        compiler_params=params(),
        cost_estimate=cost(),
        name="owner_sums",
    )(got)


def order_kernel(place_ref, near_ref, far_ref, out_ref):
    teams, _, rows, _ = out_ref.shape
    for k, ref in enumerate((near_ref, far_ref)):
        for j in range(TEAM // 2):
            for d in range(teams):
                team = (place_ref[1] + d) & (teams - 1)
                out_ref[team, place_ref[0] ^ (2 * j + k)] = ref[j, d * rows : (d + 1) * rows]


def order(place, near, far, teams):
    _, tall, width = near.shape
    out = shaped(BF16, teams, TEAM, tall // teams, width)
    return pl.pallas_call(
        order_kernel,
        in_specs=[pl.BlockSpec(memory_space=pltpu.SMEM)]
        + [pl.BlockSpec(memory_space=pltpu.VMEM)] * 2,
        out_shape=out,
        compiler_params=params(),
        cost_estimate=cost(),
        name="order",
    )(place, near, far)


def body(
    tokens,
    gain_attend,
    joint_weight,
    merge_weight,
    gain_feed,
    up_weight,
    down_weight,
    router_weight,
    mix_weight,
    widen_weight,
    narrow_weight,
    routes,
    segments,
    cotangent,
):
    count = lax.axis_size("expert")
    teams = count // TEAM
    place = (lax.axis_index("expert") & (TEAM - 1)).astype(jnp.int32)
    team = lax.axis_index("expert") >> 3
    place_arg = jnp.stack([place, team.astype(jnp.int32)])
    length, width = tokens.shape
    capacity = max(2, 2 * length // count)
    planes = [[g * TEAM + p for p in range(TEAM)] for g in range(teams)]
    lines = [[g * TEAM + p for g in range(teams)] for p in range(TEAM)]
    rows = joint_weight.shape[0]
    part = width // TEAM
    hidden = up_weight.shape[1]
    block = hidden // count

    def swap(value, mask):
        return lax.ppermute(value, "expert", [(i, i ^ mask) for i in range(count)])

    def exchange(value):
        return lax.all_to_all(value, "expert", 0, 0, tiled=True)

    def team_exchange(value):
        return lax.all_to_all(value, "expert", 0, 0, tiled=True, axis_index_groups=planes)

    def line_gather(value):
        return lax.all_gather(value, "expert", axis=0, tiled=True, axis_index_groups=lines)

    def line_scatter(value):
        return lax.psum_scatter(
            value, "expert", scatter_dimension=0, tiled=True, axis_index_groups=lines
        )

    def together(*values):
        return lax.optimization_barrier(values)

    def team_sends(value):
        return [value, swap(value, 2), swap(value, 4), swap(value, 6)]

    def team_joins(values):
        near = jnp.stack(values)
        return near, swap(near, 1)

    def team_scatter(keep, *sent):
        own, *sends = halve(keep, [swap(a, 1) for a in sent])
        return own, [swap(s, 2 * j + 2) for j, s in enumerate(sends)]

    small_width = -(-(count + 4) // 128) * 128
    pack_out = shaped(BF16, TEAM, rows, 3 * part + small_width + teams * block)
    pack = pl.pallas_call(
        functools.partial(pack_kernel, teams=teams),
        out_shape=pack_out,
        compiler_params=params(),
        cost_estimate=cost(),
        name="pack",
    )(
        joint_weight,
        up_weight,
        router_weight,
        mix_weight.T,
        gain_attend[None],
        gain_feed[None],
    )
    pack, merge_weight = together(pack, merge_weight)
    pack = team_exchange(pack).reshape(TEAM * rows, -1)
    pack, tokens, merge_weight = together(pack, tokens, merge_weight)
    wide = 3 * part + small_width
    x_sent = jnp.concatenate(
        [
            tokens,
            jnp.pad(segments.astype(BF16), ((0, 15), (0, width - length))),
        ],
        axis=0,
    )
    got = line_gather(pack[:, :wide])
    x_near, pack = together(jnp.stack(team_sends(x_sent)), pack)
    x_far = swap(x_near, 1)
    tall = TEAM * rows * teams * block // width
    up_pack = pack[:, wide:].reshape(-1, tall, teams * block)
    up_pack = up_pack.transpose(1, 0, 2).reshape(tall, width)
    both = jnp.concatenate([down_weight, up_pack], axis=0)
    both = line_gather(both).reshape(teams, 2 * tall, width)
    from_team = lambda d: [
        ((g + d) % teams * TEAM + p, g * TEAM + p) for g in range(teams) for p in range(TEAM)
    ]
    merge_line = jnp.concatenate(
        [merge_weight]
        + [lax.ppermute(merge_weight, "expert", from_team(d)) for d in range(1, teams)],
        axis=0,
    )
    merge_near, merge_far = team_joins(team_sends(merge_line))
    merge_near, cotangent = together(merge_near, cotangent)
    g_parts = team_sends(cotangent)

    joint, attended = attend(place_arg, x_near, x_far, got, length, count)
    arrived = team_exchange(attended)
    merge = order(place_arg, merge_near, merge_far, teams).reshape(width, width)
    merge, *g_parts = together(merge, *g_parts)
    g_near, g_far = team_joins(g_parts)
    residual, second, attended, stats, placing, outgoing = middle(
        arrived, merge, tokens, cotangent, got, routes, count, capacity
    )
    received = exchange(outgoing.reshape(count, capacity, -1)).reshape(count * capacity, -1)
    s_near, attended = together(jnp.stack(team_sends(second)), attended)
    s_far = swap(s_near, 1)
    a_parts = team_sends(attended)
    received, s_near, s_far, g_far = together(received, s_near, s_far, g_far)
    act, d_eupper, back = expert(received, widen_weight, narrow_weight)
    back, s_near, both, *a_parts = together(back, s_near, both, *a_parts)
    back = exchange(back.reshape(count, capacity, -1)).reshape(count * capacity, -1)
    keep, low, high, keep_dense, send_dense, up_grad, down_grad = feed(
        s_near, s_far, g_near, g_far, both, got, count
    )
    up_grad = line_scatter(up_grad)
    own, others = team_scatter(keep, low, high)
    own, send_dense = together(own, send_dense)
    a_near, a_far = team_joins(a_parts)
    dense, more = team_scatter(keep_dense, send_dense)
    result, d_residual, side, d_both = after(
        own, others, back, placing, residual, stats, cotangent, got, merge, routes, second, count
    )
    d_both, act, down_grad = together(d_both, act, down_grad)
    down_grad = line_scatter(down_grad)
    d_both = team_exchange(d_both)
    narrow_grad = narrow_grads(received, act)
    d_both, narrow_grad = together(d_both, narrow_grad)
    keep, send, grads = attend_back(
        place_arg, x_near, x_far, a_near, a_far, got, joint, d_both, side, count
    )
    grads, send, up_grad, down_grad, d_eupper = together(
        grads, send, up_grad, down_grad, d_eupper
    )
    grads = line_scatter(grads)
    own, others = team_scatter(keep, send)
    own, d_eupper = together(own, d_eupper)
    widen_grad = widen_grads(received, d_eupper)
    grads, widen_grad, *rest = together(grads, widen_grad, *others, *more)
    others, more = rest[:3], rest[3:]
    tokens_grad, result = last(
        own, others, dense, more, result, stats, tokens, d_residual, got, count
    )
    grads = jnp.concatenate([grads, up_grad], axis=1).reshape(TEAM, rows, -1)
    grads = team_exchange(grads)
    joint_grad, merge_grad, up_grad, attend_grad, feed_grad, router_grad, mix_grad = owner_sums(
        grads, width, hidden, count, teams
    )
    return (
        result,
        tokens_grad,
        attend_grad.reshape(rows),
        joint_grad,
        merge_grad,
        feed_grad.reshape(rows),
        up_grad,
        down_grad.astype(F32),
        router_grad,
        mix_grad.T,
        widen_grad,
        narrow_grad,
    )


def solution(mesh):
    one, two, three = P("expert"), P("expert", None), P("expert", None, None)
    return jax.shard_map(
        body,
        mesh=mesh,
        in_specs=(two, one, two, two, one, two, two, two, two, three, three, two, two, two),
        out_specs=(two, two, one, two, two, one, two, two, two, two, three, three),
        check_vma=False,
    )
```

```python
import functools
import math

import jax
import jax.numpy as jnp
from jax import lax
from jax.experimental import pallas as pl
from jax.experimental.pallas import tpu as pltpu
from jax.sharding import PartitionSpec as P

HEAD_DIM = 64
TEAM = 8
EPSILON = 1e-05
HIDDEN = -1e30
F32 = jnp.float32
BF16 = jnp.bfloat16
CURVE = math.sqrt(2.0 / math.pi)
MIB = 1 << 20


def dot(left, right):
    return jnp.dot(left, right, preferred_element_type=F32)


def dot_tn(left, right):
    return lax.dot_general(left, right, (((0,), (0,)), ((), ())), preferred_element_type=F32)


def dot_nt(left, right):
    return lax.dot_general(left, right, (((1,), (1,)), ((), ())), preferred_element_type=F32)


def gelu_both(u):
    square = u * u
    bent = jnp.tanh(u * (CURVE + (CURVE * 0.044715) * square))
    half = 0.5 + 0.5 * bent
    slope = half + u * (1.0 - bent * bent) * (0.5 * CURVE + (0.5 * CURVE * 0.134145) * square)
    return u * half, slope


def normed(values):
    mean = jnp.mean(values, axis=-1, keepdims=True)
    centered = values - mean
    spread = jnp.mean(centered * centered, axis=-1, keepdims=True)
    scale = lax.rsqrt(spread + EPSILON)
    return centered * scale, scale


def norm_back(dn, unit, scale):
    return scale * (
        dn
        - jnp.mean(dn, axis=-1, keepdims=True)
        - unit * jnp.mean(dn * unit, axis=-1, keepdims=True)
    )


def lanes(shape):
    return lax.broadcasted_iota(jnp.int32, shape, 1)


def sublanes(shape):
    return lax.broadcasted_iota(jnp.int32, shape, 0)


def gain_rows(small, count):
    shape = (8, small.shape[1])
    pick = (lanes(shape) == sublanes(shape) + count + 2) & (sublanes(shape) < 2)
    return dot_nt(jnp.where(pick, 1.0, 0.0).astype(BF16), small)


def column_of(rows, lane, width):
    shape = (rows.shape[0], width)
    pick = jnp.where((lanes(shape) == lane) & (sublanes(shape) == 0), 1.0, 0.0).astype(BF16)
    return dot_tn(rows.astype(BF16), pick)


def visible(segment_row, length):
    shape = (length, length)
    row, column = sublanes(shape), lanes(shape)
    segment = jnp.sum(jnp.where(row == column, segment_row, 0.0), axis=1, keepdims=True)
    return (row >= column) & (segment == segment_row)


def chance_of(query, keys, allowed):
    scores = dot_nt(query, keys) * (1.0 / math.sqrt(HEAD_DIM))
    scores = jnp.where(allowed, scores, HIDDEN)
    grown = jnp.exp(scores - jnp.max(scores, axis=1, keepdims=True))
    return grown * (1.0 / jnp.sum(grown, axis=1, keepdims=True))


def params(mib=56, **more):
    return pltpu.CompilerParams(vmem_limit_bytes=mib * MIB, **more)


def cost(flops=1):
    return pl.CostEstimate(flops=flops, bytes_accessed=1, transcendentals=0)


def shaped(dtype, *shape):
    return jax.ShapeDtypeStruct(shape, dtype)


def pack_kernel(
    joint_ref, up_ref, router_ref, mix_ref, gain_a_ref, gain_f_ref, pack_ref, *, teams
):
    rows = joint_ref.shape[0]
    width = joint_ref.shape[1] // 3
    part = width // TEAM
    block = up_ref.shape[1] // (teams * TEAM)
    count = router_ref.shape[1]
    wide = pack_ref.shape[2] - teams * block
    shape = (rows, wide - 3 * part)
    spread = (count, shape[1])
    spread = jnp.where(lanes(spread) == sublanes(spread), 1.0, 0.0).astype(BF16)
    small = dot(router_ref[...], spread)
    lane = lanes(shape)
    square = (rows, rows)
    same = sublanes(square) == lanes(square)
    columns = [mix_ref[0:1], mix_ref[1:2], gain_a_ref[...], gain_f_ref[...]]
    for i, row in enumerate(columns):
        column = jnp.sum(jnp.where(same, row.astype(F32), 0.0), axis=1, keepdims=True)
        small += jnp.where(lane == count + i, column, 0.0)
    small = small.astype(BF16)
    for p in range(TEAM):
        pieces = [joint_ref[:, c * width + p * part : c * width + (p + 1) * part] for c in range(3)]
        for g in range(teams):
            start = (g * TEAM + p) * block
            pieces.append(up_ref[:, start : start + block])
        pack_ref[p] = jnp.concatenate(pieces[:3] + [small] + pieces[3:], axis=1)


def attend_kernel(place_ref, n0_ref, n1_ref, f0_ref, f1_ref, got_ref, joint_ref, out_ref, *, count):
    _, length, part = out_ref.shape
    members = [ref.at[i] for ref in (n0_ref, n1_ref, f0_ref, f1_ref) for i in range(2)]
    gains = gain_rows(got_ref[:, 3 * part :], count)
    lane = lanes((length, part))
    for j in range(TEAM // 2):
        pair = (members[j], members[j + TEAM // 2])
        x = jnp.concatenate([ref[:length] for ref in pair], axis=0).astype(F32)
        unit, _ = normed(x)
        first = (unit * gains[0:1]).astype(BF16)
        joint = dot(first, got_ref[:, : 3 * part]).astype(BF16)
        for k, ref in enumerate(pair):
            allowed = visible(ref[length:, :length].astype(F32)[0:1], length)
            own = joint[k * length : (k + 1) * length]
            query, keys, values = own[:, :part], own[:, part : 2 * part], own[:, 2 * part :]
            total = jnp.zeros((length, part), F32)
            for h in range(part // HEAD_DIM):
                mine = lane // HEAD_DIM == h
                chance = chance_of(jnp.where(mine, query, 0), keys, allowed)
                total += dot(chance.astype(BF16), jnp.where(mine, values, 0))
            member = place_ref[0] ^ (2 * j + k)
            joint_ref[member] = own
            out_ref[member] = total.astype(BF16)


def attend(place, xs, got, length, count):
    part = xs[0].shape[2] // TEAM
    return pl.pallas_call(
        functools.partial(attend_kernel, count=count),
        in_specs=[pl.BlockSpec(memory_space=pltpu.SMEM)]
        + [pl.BlockSpec(memory_space=pltpu.VMEM)] * 5,
        out_shape=(shaped(BF16, TEAM, length, 3 * part), shaped(BF16, TEAM, length, part)),
        compiler_params=params(56),
        cost_estimate=cost(),
        name="attend",
    )(place, *xs, got)


def attend_back_kernel(
    place_ref, n0_ref, n1_ref, f0_ref, f1_ref, near_att, far_att, got_ref, joint_ref, d_ref, side_ref,
    keep_ref, send_ref, grad_ref, d_joint_ref, first_ref, unit_ref, *, count,
):
    _, length, wide = joint_ref.shape
    part = wide // 3
    half, _, width = near_att.shape
    shrink = 1.0 / math.sqrt(HEAD_DIM)
    gains = gain_rows(got_ref[:, 3 * part :], count)
    lane = lanes((length, part))
    d_merged = []
    members = [ref.at[i] for ref in (n0_ref, n1_ref, f0_ref, f1_ref) for i in range(2)]
    for k in range(2):
        for j in range(half):
            ref = members[k * half + j]
            rows = slice((k * half + j) * length, (k * half + j + 1) * length)
            unit, _ = normed(ref[:length].astype(F32))
            unit_ref[rows] = unit
            first_ref[rows] = (unit * gains[0:1]).astype(BF16)
            allowed = visible(ref[length:, :length].astype(F32)[0:1], length)
            member = place_ref[0] ^ (2 * j + k)
            own = joint_ref[member]
            both = d_ref[member]
            d_own = both[:length]
            d_merged.append(both[length:])
            query, keys, values = own[:, :part], own[:, part : 2 * part], own[:, 2 * part :]
            d_query = jnp.zeros((length, part), F32)
            d_keys = jnp.zeros((length, part), F32)
            d_values = jnp.zeros((length, part), F32)
            for h in range(part // HEAD_DIM):
                mine = lane // HEAD_DIM == h
                q = jnp.where(mine, query, 0)
                d_head = jnp.where(mine, d_own, 0)
                chance = chance_of(q, keys, allowed)
                d_weights = dot_nt(d_head, values)
                inner = jnp.sum(chance * d_weights, axis=1, keepdims=True)
                d_scores = (chance * (d_weights - inner)).astype(BF16)
                d_query += dot(d_scores, jnp.where(mine, keys, 0))
                d_keys += dot_tn(d_scores, q)
                d_values += dot_tn(chance.astype(BF16), d_head)
            d_joint_ref[rows, :part] = (d_query * shrink).astype(BF16)
            d_joint_ref[rows, part : 2 * part] = (d_keys * shrink).astype(BF16)
            d_joint_ref[rows, 2 * part :] = d_values.astype(BF16)
    d_joint = d_joint_ref[...]
    d_first = dot_nt(d_joint, got_ref[:, : 3 * part])
    tall = half * length
    keep_ref[...] = d_first[:tall].reshape(keep_ref.shape)
    send_ref[...] = d_first[tall:].astype(BF16).reshape(send_ref.shape)
    gain = jnp.sum(d_first * unit_ref[...], axis=0, keepdims=True)
    gain = jnp.where(sublanes((8, width)) == 0, gain, 0.0)
    grad_ref[:, : 3 * part] = dot_tn(first_ref[...], d_joint).astype(BF16)
    side = side_ref[...] + column_of(gain, count + 3, side_ref.shape[1])
    grad_ref[:, 3 * part : -part] = side.astype(BF16)
    merged = dot_tn(near_att[...].reshape(tall, width), jnp.concatenate(d_merged[:half], axis=0))
    merged += dot_tn(far_att[...].reshape(tall, width), jnp.concatenate(d_merged[half:], axis=0))
    grad_ref[:, -part:] = merged.astype(BF16)


def attend_back(place, xs, near_att, far_att, got, joint, d_both, side, count):
    half, length, width = near_att.shape
    part = width // TEAM
    tall = TEAM * length
    outs = (
        shaped(F32, half, length, width),
        shaped(BF16, half, length, width),
        shaped(BF16, width, 4 * part + side.shape[1]),
    )
    return pl.pallas_call(
        functools.partial(attend_back_kernel, count=count),
        in_specs=[pl.BlockSpec(memory_space=pltpu.SMEM)]
        + [pl.BlockSpec(memory_space=pltpu.VMEM)] * 10,
        out_shape=outs,
        scratch_shapes=[
            pltpu.VMEM((tall, 3 * part), BF16),
            pltpu.VMEM((tall, width), BF16),
            pltpu.VMEM((tall, width), F32),
        ],
        compiler_params=params(56),
        cost_estimate=cost(int(2e10)),
        name="attend_back",
    )(place, *xs, near_att, far_att, got, joint, d_both, side)


def middle_kernel(
    att_ref, merge_ref, x_ref, small_ref, routes_ref, placing_ref,
    residual_ref, second_ref, attended_ref, stats_ref, out_ref, *, count,
):
    length, width = x_ref.shape
    small = small_ref[:, 3 * width // TEAM :]
    gains = gain_rows(small, count)
    attended = jnp.concatenate([att_ref[p] for p in range(TEAM)], axis=1)
    residual = x_ref[...].astype(F32) + dot(attended, merge_ref[...])
    residual_ref[...] = residual
    unit, _ = normed(residual)
    second = (unit * gains[1:2]).astype(BF16)
    second_ref[...] = second
    attended_ref[...] = attended
    logits = dot(second, small)
    lane = lanes(logits.shape)
    routed = jnp.where(lane < count, logits, HIDDEN)
    grown = jnp.exp(routed - jnp.max(routed, axis=1, keepdims=True))
    chances = grown * (1.0 / jnp.sum(grown, axis=1, keepdims=True))
    mixed = jnp.where((lane >= count) & (lane < count + 2), logits, HIDDEN)
    grown = jnp.exp(mixed - jnp.max(mixed, axis=1, keepdims=True))
    mix = grown * (1.0 / jnp.sum(grown, axis=1, keepdims=True))
    routes = routes_ref[...]
    onehot = lane == routes
    gate = jnp.sum(jnp.where(onehot, chances, 0.0), axis=1, keepdims=True)
    mix_expert = jnp.sum(jnp.where(lane == count + 1, mix, 0.0), axis=1, keepdims=True)
    stats_ref[...] = chances + mix + jnp.where(lane == count + 2, gate, 0.0)
    scale = mix_expert * gate
    high = scale.astype(BF16).astype(F32)
    middle_part = (scale - high).astype(BF16).astype(F32)
    low = scale - high - middle_part
    spread = (length, out_ref.shape[1] - width)
    lane = lanes(spread)
    scales = jnp.where(lane == 0, high, 0.0) + jnp.where(lane == 1, middle_part, 0.0)
    scales += jnp.where(lane == 2, low, 0.0)
    placing = placing_ref[...]
    out_ref[:, :width] = dot_tn(placing, second).astype(BF16)
    out_ref[:, width:] = dot_tn(placing, scales.astype(BF16)).astype(BF16)


def place_kernel(routes_ref, g_ref, placing_ref, out_ref, *, count, capacity):
    length = g_ref.shape[0]
    routes = routes_ref[...]
    onehot = jnp.where(lanes((length, -(-count // 128) * 128)) == routes, 1.0, 0.0)
    shape = (length, length)
    before = jnp.where(sublanes(shape) > lanes(shape), 1.0, 0.0).astype(BF16)
    rank = jnp.sum(onehot * dot(before, onehot.astype(BF16)), axis=1, keepdims=True)
    slot = routes * capacity + rank.astype(jnp.int32)
    placing = jnp.where(lanes((length, count * capacity)) == slot, 1.0, 0.0).astype(BF16)
    placing_ref[...] = placing
    out_ref[...] = dot_tn(placing, g_ref[...]).astype(BF16)


def place_rows(routes, cotangent, count, capacity):
    length, width = cotangent.shape
    return pl.pallas_call(
        functools.partial(place_kernel, count=count, capacity=capacity),
        out_shape=(
            shaped(BF16, length, count * capacity),
            shaped(BF16, count * capacity, width),
        ),
        compiler_params=params(56),
        cost_estimate=cost(),
        name="place_rows",
    )(routes, cotangent)


def middle(att, merge, tokens, got, routes, placing, count):
    length, width = tokens.shape
    lanes_small = got.shape[1] - 3 * width // TEAM
    outs = (
        shaped(F32, length, width),
        shaped(BF16, length, width),
        shaped(BF16, length, width),
        shaped(F32, length, lanes_small),
        shaped(BF16, placing.shape[1], width + 128),
    )
    return pl.pallas_call(
        functools.partial(middle_kernel, count=count),
        out_shape=outs,
        compiler_params=params(56),
        cost_estimate=cost(),
        name="middle",
    )(att, merge, tokens, got, routes, placing)


def expert_kernel(
    rows_ref, g_ref, widen_hbm, narrow_hbm, act_hbm, d_hbm, back_ref, d_out_ref,
    widen_ref, narrow_ref, act_ref, d_ref, in_sems, out_sems, *, chunk,
):
    width, hidden = widen_ref.shape
    copies = []
    for i in range(hidden // chunk):
        part = pl.ds(i * chunk, chunk)
        wide = (widen_hbm.at[0, :, part], widen_ref.at[:, part], in_sems.at[2 * i])
        tall = (narrow_hbm.at[0, part, :], narrow_ref.at[part, :], in_sems.at[2 * i + 1])
        copies.append([pltpu.make_async_copy(*wide), pltpu.make_async_copy(*tall)])
    for pair in copies:
        for copy in pair:
            copy.start()
    scale = jnp.sum(rows_ref[:, width:].astype(F32), axis=1, keepdims=True)
    d_out_ref[...] = (g_ref[...].astype(F32) * scale).astype(BF16)
    for i, pair in enumerate(copies):
        for copy in pair:
            copy.wait()
        part = slice(i * chunk, (i + 1) * chunk)
        upper = dot(rows_ref[:, :width], widen_ref[:, part])
        d_act = dot_nt(d_out_ref[...], narrow_ref[part])
        act, slope = gelu_both(upper)
        act_ref[:, part] = act.astype(BF16)
        d_ref[:, part] = (slope * d_act).astype(BF16)
    outs = [
        pltpu.make_async_copy(act_ref, act_hbm, out_sems.at[0]),
        pltpu.make_async_copy(d_ref, d_hbm, out_sems.at[1]),
    ]
    for copy in outs:
        copy.start()
    back_ref[:, :width] = dot(act_ref[...], narrow_ref[...]).astype(BF16)
    back_ref[:, width:] = dot_nt(d_ref[...], widen_ref[...]).astype(BF16)
    for copy in outs:
        copy.wait()


def expert(rows, g_rows, widen, narrow, chunk=1024):
    slots, width = g_rows.shape
    hidden = widen.shape[2]
    left = pl.BlockSpec(memory_space=pl.ANY)
    here = pl.BlockSpec(memory_space=pltpu.VMEM)
    return pl.pallas_call(
        functools.partial(expert_kernel, chunk=chunk),
        in_specs=[here, here, left, left],
        out_specs=[left, left, here, here],
        out_shape=(
            shaped(BF16, slots, hidden),
            shaped(BF16, slots, hidden),
            shaped(BF16, slots, 2 * width),
            shaped(BF16, slots, width),
        ),
        scratch_shapes=[
            pltpu.VMEM((width, hidden), BF16),
            pltpu.VMEM((hidden, width), BF16),
            pltpu.VMEM((slots, hidden), BF16),
            pltpu.VMEM((slots, hidden), BF16),
            pltpu.SemaphoreType.DMA((2 * (hidden // chunk),)),
            pltpu.SemaphoreType.DMA((2,)),
        ],
        compiler_params=params(56),
        cost_estimate=cost(),
        name="expert",
    )(rows, g_rows, widen, narrow)


def narrow_grad_kernel(rows_ref, act_ref, out_ref):
    out_ref[0] = dot_tn(act_ref[...], rows_ref[...])


def narrow_grads(rows, act, chunk=512):
    slots, width = rows.shape
    hidden = act.shape[1]
    return pl.pallas_call(
        narrow_grad_kernel,
        grid=(hidden // chunk,),
        in_specs=[
            pl.BlockSpec((slots, width), lambda f: (0, 0)),
            pl.BlockSpec((slots, chunk), lambda f: (0, f)),
        ],
        out_specs=pl.BlockSpec((1, chunk, width), lambda f: (0, f, 0)),
        out_shape=shaped(F32, 1, hidden, width),
        compiler_params=params(56),
        cost_estimate=cost(),
        name="narrow_grads",
    )(rows, act)


def widen_grad_kernel(rows_ref, d_ref, out_ref):
    out_ref[0] = dot_tn(rows_ref[...], d_ref[...])


def widen_grads(rows, d_upper, width, chunk=128):
    slots = rows.shape[0]
    hidden = d_upper.shape[1]
    return pl.pallas_call(
        widen_grad_kernel,
        grid=(width // chunk,),
        in_specs=[
            pl.BlockSpec((slots, chunk), lambda f: (0, f)),
            pl.BlockSpec((slots, hidden), lambda f: (0, 0)),
        ],
        out_specs=pl.BlockSpec((1, chunk, hidden), lambda f: (0, f, 0)),
        out_shape=shaped(F32, 1, width, hidden),
        compiler_params=params(56),
        cost_estimate=cost(),
        name="widen_grads",
    )(rows, d_upper)


def feed_kernel(
    near_ref, far_ref, g_near_ref, g_far_ref, up_ref, down_ref, small_ref,
    keep_ref, low_ref, high_ref, keep_dense_ref, send_dense_ref, up_grad_ref, down_grad_ref,
    *, count,
):
    half, length, width = near_ref.shape
    tall = half * length
    near, far = near_ref[...].reshape(tall, width), far_ref[...].reshape(tall, width)
    second = jnp.concatenate([near, far], axis=0)
    g = jnp.concatenate(
        [g_near_ref[...].reshape(tall, width), g_far_ref[...].reshape(tall, width)], axis=0
    ).astype(F32)
    logits = dot(second, small_ref[:, 3 * width // TEAM :])
    lane = lanes(logits.shape)
    mixed = jnp.where((lane >= count) & (lane < count + 2), logits, HIDDEN)
    grown = jnp.exp(mixed - jnp.max(mixed, axis=1, keepdims=True))
    mix = jnp.sum(jnp.where(lane == count, grown, 0.0), axis=1, keepdims=True)
    mix = mix * (1.0 / jnp.sum(grown, axis=1, keepdims=True))
    d_dense = (g * mix).astype(BF16)
    act, slope = gelu_both(dot(second, up_ref[...]))
    act = act.astype(BF16)
    d_upper = (slope * dot_nt(d_dense, down_ref[...])).astype(BF16)
    d_second = dot_nt(d_upper, up_ref[...])
    dense = dot(act, down_ref[...])
    along = jnp.sum(g * dense, axis=1, keepdims=True)
    rest = along - along.astype(BF16).astype(F32)
    lane = lanes((2 * tall, 128))
    along = jnp.where(lane == 0, along, 0.0) + jnp.where(lane == 1, rest, 0.0)
    keep_ref[:, :, :width] = d_second[:tall].reshape(half, length, width)
    keep_ref[:, :, width:] = along[:tall].reshape(half, length, 128)
    sent = d_second[tall:].astype(BF16).reshape(half, length, width)
    low_ref[...] = sent[:, :, : width // 2]
    high_ref[:, :, : width // 2] = sent[:, :, width // 2 :]
    high_ref[:, :, width // 2 :] = along[tall:].astype(BF16).reshape(half, length, 128)
    keep_dense_ref[...] = dense[:tall].reshape(half, length, width)
    send_dense_ref[...] = dense[tall:].astype(BF16).reshape(half, length, width)
    up_grad_ref[...] = dot_tn(second, d_upper).astype(BF16)
    down_grad_ref[...] = dot_tn(act, d_dense).astype(BF16)


def feed(near, far, g_near, g_far, up, down, got, count):
    half, length, width = near.shape
    hidden = up.shape[1]
    outs = (
        shaped(F32, half, length, width + 128),
        shaped(BF16, half, length, width // 2),
        shaped(BF16, half, length, width // 2 + 128),
        shaped(F32, half, length, width),
        shaped(BF16, half, length, width),
        shaped(BF16, width, hidden),
        shaped(BF16, hidden, width),
    )
    return pl.pallas_call(
        functools.partial(feed_kernel, count=count),
        out_shape=outs,
        compiler_params=params(56),
        cost_estimate=cost(),
        name="feed",
    )(near, far, g_near, g_far, up, down, got)


def halve_kernel(keep_ref, *refs, pieces):
    got_refs, own_ref, send_refs = refs[:pieces], refs[pieces], refs[pieces + 1 :]
    start = 0
    for got_ref in got_refs:
        part = slice(start, start + got_ref.shape[2])
        own_ref[:, part] = keep_ref[0, :, part] + got_ref[0].astype(F32)
        for j, ref in enumerate(send_refs):
            total = keep_ref[j + 1, :, part] + got_ref[j + 1].astype(F32)
            ref[:, part] = total.astype(BF16)
        start = part.stop


def halve(keep, got):
    half, length, width = keep.shape
    outs = (shaped(F32, length, width),) + (shaped(BF16, length, width),) * (half - 1)
    return pl.pallas_call(
        functools.partial(halve_kernel, pieces=len(got)),
        out_shape=outs,
        compiler_params=params(20),
        cost_estimate=cost(),
        name="halve",
    )(keep, *got)


def after_kernel(
    own_ref, r1_ref, r2_ref, r3_ref, back_ref, placing_ref, residual_ref, stats_ref, g_ref,
    small_ref, merge_ref, routes_ref, second_ref,
    result_ref, d_residual_ref, side_ref, d_ref, *, count,
):
    length, width = g_ref.shape
    part = width // TEAM
    small = small_ref[:, 3 * part :]
    gains = gain_rows(small, count)
    summed = (
        own_ref[...] + r1_ref[...].astype(F32) + r2_ref[...].astype(F32) + r3_ref[...].astype(F32)
    )
    d_second = summed[:, :width]
    d_mix_dense = jnp.sum(summed[:, width:], axis=1, keepdims=True)
    stats = stats_ref[...]
    lane = lanes(stats.shape)
    column = lambda i: jnp.sum(jnp.where(lane == i, stats, 0.0), axis=1, keepdims=True)
    mix_dense, mix_expert, gate = column(count), column(count + 1), column(count + 2)
    residual = residual_ref[...]
    g = g_ref[...].astype(F32)
    returned = dot(placing_ref[...], back_ref[:, :width])
    result_ref[...] = residual + mix_expert * gate * returned
    along = jnp.sum(g * returned, axis=1, keepdims=True)
    d_mix_expert = gate * along
    mean = mix_dense * d_mix_dense + mix_expert * d_mix_expert
    onehot = jnp.where(lane == routes_ref[...], 1.0, 0.0)
    side = jnp.where(lane < count, stats * (onehot - gate) * (mix_expert * along), 0.0)
    side += jnp.where(lane == count, mix_dense * (d_mix_dense - mean), 0.0)
    side += jnp.where(lane == count + 1, mix_expert * (d_mix_expert - mean), 0.0)
    side = side.astype(BF16)
    d_second += dot(placing_ref[...], back_ref[:, width:]) + dot_nt(side, small)
    unit, scale = normed(residual)
    d_residual = g + norm_back(d_second * gains[1:2], unit, scale)
    d_residual_ref[...] = d_residual
    d_merged = d_residual.astype(BF16)
    side_grad = dot_tn(second_ref[...], side)
    feed_row = jnp.sum(d_second * unit, axis=0, keepdims=True)
    feed_rows = jnp.where(sublanes((8, width)) == 0, feed_row, 0.0)
    side_ref[...] = side_grad + column_of(feed_rows, count + 2, side.shape[1])
    d_att = dot_nt(d_merged, merge_ref[...]).astype(BF16)
    for p in range(TEAM):
        d_ref[p, :length] = d_att[:, p * part : (p + 1) * part]
        d_ref[p, length:] = d_merged[:, p * part : (p + 1) * part]


def after(
    own, others, back, placing, residual, stats, cotangent, got, merge, routes, second, count
):
    length, width = cotangent.shape
    part = width // TEAM
    outs = (
        shaped(F32, length, width),
        shaped(F32, length, width),
        shaped(F32, width, got.shape[1] - 3 * part),
        shaped(BF16, TEAM, 2 * length, part),
    )
    return pl.pallas_call(
        functools.partial(after_kernel, count=count),
        out_shape=outs,
        compiler_params=params(56),
        cost_estimate=cost(),
        name="after",
    )(own, *others, back, placing, residual, stats, cotangent, got, merge, routes, second)


def last_kernel(
    own_ref, r1_ref, r2_ref, r3_ref, dense_ref, d1_ref, d2_ref, d3_ref, part_ref, stats_ref,
    x_ref, d_residual_ref, small_ref, out_ref, result_ref, *, count,
):
    part = x_ref.shape[1] // TEAM
    gains = gain_rows(small_ref[:, 3 * part :], count)
    add = lambda a, b, c, d: a[...] + b[...].astype(F32) + c[...].astype(F32) + d[...].astype(F32)
    d_first = add(own_ref, r1_ref, r2_ref, r3_ref)
    unit, scale = normed(x_ref[...].astype(F32))
    out_ref[...] = (
        d_residual_ref[...] + norm_back(d_first * gains[0:1], unit, scale)
    ).astype(BF16)
    stats = stats_ref[...]
    mix_dense = jnp.sum(jnp.where(lanes(stats.shape) == count, stats, 0.0), axis=1, keepdims=True)
    dense = add(dense_ref, d1_ref, d2_ref, d3_ref)
    result_ref[...] = (part_ref[...] + mix_dense * dense).astype(BF16)


def last(own, others, dense, more, part, stats, tokens, d_residual, got, count):
    return pl.pallas_call(
        functools.partial(last_kernel, count=count),
        out_shape=(shaped(BF16, *tokens.shape),) * 2,
        compiler_params=params(16),
        cost_estimate=cost(),
        name="last",
    )(own, *others, dense, *more, part, stats, tokens, d_residual, got)


def owner_kernel(
    got_ref, up_got_ref, joint_ref, merge_ref, up_ref, attend_ref, feed_ref, router_ref, mix_ref,
    *, count,
):
    teams, _, rows, wide = got_ref.shape
    part = merge_ref.shape[1] // TEAM
    width = part * TEAM
    block = up_ref.shape[1] // (TEAM * teams)
    total = jnp.zeros((rows, wide - 4 * part), F32)
    for p in range(TEAM):
        own = got_ref[0, p].astype(F32)
        for g in range(1, teams):
            own += got_ref[g, p].astype(F32)
        for c in range(3):
            start = c * width + p * part
            joint_ref[:, start : start + part] = own[:, c * part : (c + 1) * part]
        total += own[:, 3 * part : wide - part]
        merge_ref[:, p * part : (p + 1) * part] = own[:, wide - part :]
        for g in range(teams):
            start = (g * TEAM + p) * block
            piece = up_got_ref[p, :, g * block : (g + 1) * block]
            up_ref[:, start : start + block] = piece.astype(F32)
    router_ref[...] = total[:, :count]
    same = sublanes((rows, rows)) == lanes((rows, rows))

    def row(lane):
        column = jnp.sum(jnp.where(lanes(total.shape) == lane, total, 0.0), axis=1, keepdims=True)
        return jnp.sum(jnp.where(same, column, 0.0), axis=0, keepdims=True)

    mix_ref[0:1] = row(count)
    mix_ref[1:2] = row(count + 1)
    feed_ref[...] = row(count + 2)
    attend_ref[...] = row(count + 3)


def owner_sums(got, up, width, hidden, count):
    rows = got.shape[2]
    outs = (
        shaped(F32, rows, 3 * width),
        shaped(F32, rows, width),
        shaped(F32, rows, hidden),
        shaped(F32, 1, rows),
        shaped(F32, 1, rows),
        shaped(F32, rows, count),
        shaped(F32, 2, rows),
    )
    return pl.pallas_call(
        functools.partial(owner_kernel, count=count),
        out_shape=outs,
        compiler_params=params(12),
        cost_estimate=cost(),
        name="owner_sums",
    )(got, up)


def order_kernel(place_ref, near_ref, far_ref, out_ref):
    teams, _, rows, _ = out_ref.shape
    for k, ref in enumerate((near_ref, far_ref)):
        for j in range(TEAM // 2):
            for d in range(teams):
                team = (place_ref[1] + d) & (teams - 1)
                out_ref[team, place_ref[0] ^ (2 * j + k)] = ref[j, d * rows : (d + 1) * rows]


def order(place, near, far, teams):
    _, tall, width = near.shape
    out = shaped(BF16, teams, TEAM, tall // teams, width)
    return pl.pallas_call(
        order_kernel,
        in_specs=[pl.BlockSpec(memory_space=pltpu.SMEM)]
        + [pl.BlockSpec(memory_space=pltpu.VMEM)] * 2,
        out_shape=out,
        compiler_params=params(56),
        cost_estimate=cost(),
        name="order",
    )(place, near, far)


def body(
    tokens,
    gain_attend,
    joint_weight,
    merge_weight,
    gain_feed,
    up_weight,
    down_weight,
    router_weight,
    mix_weight,
    widen_weight,
    narrow_weight,
    routes,
    segments,
    cotangent,
):
    count = lax.axis_size("expert")
    teams = count // TEAM
    place = (lax.axis_index("expert") & (TEAM - 1)).astype(jnp.int32)
    team = lax.axis_index("expert") >> 3
    place_arg = jnp.stack([place, team.astype(jnp.int32)])
    length, width = tokens.shape
    capacity = max(2, 2 * length // count)
    planes = [[g * TEAM + p for p in range(TEAM)] for g in range(teams)]
    lines = [[g * TEAM + p for g in range(teams)] for p in range(TEAM)]
    rows = joint_weight.shape[0]
    part = width // TEAM
    hidden = up_weight.shape[1]
    block = hidden // count

    def swap(value, mask):
        return lax.ppermute(value, "expert", [(i, i ^ mask) for i in range(count)])

    def exchange(value):
        return lax.all_to_all(value, "expert", 0, 0, tiled=True)

    def team_exchange(value):
        return lax.all_to_all(value, "expert", 0, 0, tiled=True, axis_index_groups=planes)

    def line_gather(value):
        return lax.all_gather(value, "expert", axis=0, tiled=True, axis_index_groups=lines)

    def line_scatter(value):
        return lax.psum_scatter(
            value, "expert", scatter_dimension=0, tiled=True, axis_index_groups=lines
        )

    def together(*values):
        return lax.optimization_barrier(values)

    def team_sends(value):
        return [value, swap(value, 2), swap(value, 4), swap(value, 6)]

    def team_joins(values):
        near = jnp.stack(values)
        return near, swap(near, 1)

    def team_scatter(keep, *sent):
        own, *sends = halve(keep, [swap(a, 1) for a in sent])
        return own, [swap(s, 2 * j + 2) for j, s in enumerate(sends)]

    small_width = -(-(count + 4) // 128) * 128
    pack_out = shaped(BF16, TEAM, rows, 3 * part + small_width + teams * block)
    pack = pl.pallas_call(
        functools.partial(pack_kernel, teams=teams),
        out_shape=pack_out,
        compiler_params=params(56),
        cost_estimate=cost(),
        name="pack",
    )(
        joint_weight,
        up_weight,
        router_weight,
        mix_weight.T,
        gain_attend[None],
        gain_feed[None],
    )
    pack, merge_weight = together(pack, merge_weight)
    pack = team_exchange(pack).reshape(TEAM * rows, -1)
    placing, g_rows = place_rows(routes, cotangent, count, capacity)
    from_team = lambda d: [
        ((g + d) % teams * TEAM + p, g * TEAM + p) for g in range(teams) for p in range(TEAM)
    ]
    merge_line = [merge_weight]
    merge_line += [lax.ppermute(merge_weight, "expert", from_team(d)) for d in range(1, teams)]
    pack, tokens, g_rows, *merge_line = together(pack, tokens, g_rows, *merge_line)
    joint_rows, g_rows = together(pack[:, : 3 * part + small_width], g_rows)
    g_rows = exchange(g_rows.reshape(count, capacity, width)).reshape(count * capacity, width)
    merge_line = jnp.concatenate(merge_line, axis=0)
    wide = 3 * part + small_width
    x_sent = jnp.concatenate(
        [
            tokens,
            jnp.pad(segments.astype(BF16), ((0, 15), (0, width - length))),
        ],
        axis=0,
    )
    got = line_gather(joint_rows)
    sends = team_sends(x_sent)
    xs = [jnp.stack(sends[:2]), jnp.stack(sends[2:])]
    *xs, pack, g_rows = together(*xs, pack, g_rows)
    xs = xs + [swap(x, 1) for x in xs]
    up_part = line_gather(pack[:, 3 * part + small_width :])
    merge_parts = team_sends(merge_line)

    joint, attended = attend(place_arg, xs, got, length, count)
    attended, *merge_parts = together(attended, *merge_parts)
    merge_near, merge_far = team_joins(merge_parts)
    arrived = team_exchange(attended)
    merge = order(place_arg, merge_near, merge_far, teams).reshape(width, width)
    residual, second, attended, stats, outgoing = middle(
        arrived, merge, tokens, got, routes, placing, count
    )
    received = exchange(outgoing.reshape(count, capacity, -1)).reshape(count * capacity, -1)
    s_near, attended, up_part = together(jnp.stack(team_sends(second)), attended, up_part)
    s_far = swap(s_near, 1)
    a_parts = team_sends(jnp.concatenate([attended, cotangent], axis=0))
    received, s_near, s_far, down_own = together(received, s_near, s_far, down_weight)
    down_part = line_gather(down_own)
    act, d_eupper, back, d_out = expert(received, g_rows, widen_weight, narrow_weight)
    back, s_near, up_part, *a_parts = together(back, s_near, up_part, *a_parts)
    g_near, g_far = team_joins([a[length:] for a in a_parts])
    a_parts = [a[:length] for a in a_parts]
    back = exchange(back.reshape(count, capacity, -1)).reshape(count * capacity, -1)
    keep, low, high, keep_dense, send_dense, up_grad, down_grad = feed(
        s_near, s_far, g_near, g_far, up_part, down_part, got, count
    )
    up_grad = line_scatter(up_grad)
    own, others = team_scatter(keep, low, high)
    own, send_dense, down_grad, d_eupper = together(own, send_dense, down_grad, d_eupper)
    down_grad = line_scatter(down_grad)
    widen_grad = widen_grads(received, d_eupper, width)
    back, widen_grad = together(back, widen_grad)
    a_near, a_far = team_joins(a_parts)
    dense, more = team_scatter(keep_dense, send_dense)
    result, d_residual, side, d_both = after(
        own, others, back, placing, residual, stats, cotangent, got, merge, routes, second, count
    )
    d_both, act = together(d_both, act)
    d_both = team_exchange(d_both)
    narrow_grad = narrow_grads(d_out, act)
    d_both, narrow_grad, up_grad = together(d_both, narrow_grad, up_grad)
    up_grad = team_exchange(up_grad.reshape(TEAM, rows, -1))
    keep, send, grads = attend_back(
        place_arg, xs, a_near, a_far, got, joint, d_both, side, count
    )
    grads, send, up_grad, down_grad = together(grads, send, up_grad, down_grad)
    grads = exchange(grads.reshape(count, rows, -1))
    own, others = team_scatter(keep, send)
    tokens_grad, result = last(
        own, others, dense, more, result, stats, tokens, d_residual, got, count
    )
    grads, tokens_grad = together(grads, tokens_grad)
    grads = grads.reshape(teams, TEAM, rows, -1)
    joint_grad, merge_grad, up_grad, attend_grad, feed_grad, router_grad, mix_grad = owner_sums(
        grads, up_grad, width, hidden, count
    )
    return (
        result,
        tokens_grad,
        attend_grad.reshape(rows),
        joint_grad,
        merge_grad,
        feed_grad.reshape(rows),
        up_grad,
        down_grad.astype(F32),
        router_grad,
        mix_grad.T,
        widen_grad,
        narrow_grad,
    )


def solution(mesh):
    one, two, three = P("expert"), P("expert", None), P("expert", None, None)
    return jax.shard_map(
        body,
        mesh=mesh,
        in_specs=(two, one, two, two, one, two, two, two, two, three, three, two, two, two),
        out_specs=(two, two, one, two, two, one, two, two, two, two, three, three),
        check_vma=False,
    )
```

```python
import functools
import math

import jax
import jax.numpy as jnp
from jax import lax
from jax.experimental import pallas as pl
from jax.experimental.pallas import tpu as pltpu
from jax.sharding import PartitionSpec as P

HEAD_DIM = 64
TEAM = 8
EPSILON = 1e-05
HIDDEN = -1e30
F32 = jnp.float32
BF16 = jnp.bfloat16
CURVE = math.sqrt(2.0 / math.pi)
MIB = 1 << 20


def dot(left, right):
    return jnp.dot(left, right, preferred_element_type=F32)


def dot_tn(left, right):
    return lax.dot_general(left, right, (((0,), (0,)), ((), ())), preferred_element_type=F32)


def dot_nt(left, right):
    return lax.dot_general(left, right, (((1,), (1,)), ((), ())), preferred_element_type=F32)


def gelu_both(u):
    square = u * u
    bent = jnp.tanh(u * (CURVE + (CURVE * 0.044715) * square))
    half = 0.5 + 0.5 * bent
    slope = half + u * (1.0 - bent * bent) * (0.5 * CURVE + (0.5 * CURVE * 0.134145) * square)
    return u * half, slope


def normed(values):
    mean = jnp.mean(values, axis=-1, keepdims=True)
    centered = values - mean
    spread = jnp.mean(centered * centered, axis=-1, keepdims=True)
    scale = lax.rsqrt(spread + EPSILON)
    return centered * scale, scale


def norm_back(dn, unit, scale):
    return scale * (
        dn
        - jnp.mean(dn, axis=-1, keepdims=True)
        - unit * jnp.mean(dn * unit, axis=-1, keepdims=True)
    )


def lanes(shape):
    return lax.broadcasted_iota(jnp.int32, shape, 1)


def sublanes(shape):
    return lax.broadcasted_iota(jnp.int32, shape, 0)


def gain_rows(small, count):
    shape = (8, small.shape[1])
    pick = (lanes(shape) == sublanes(shape) + count + 2) & (sublanes(shape) < 2)
    return dot_nt(jnp.where(pick, 1.0, 0.0).astype(BF16), small)


def column_of(rows, lane, width):
    shape = (rows.shape[0], width)
    pick = jnp.where((lanes(shape) == lane) & (sublanes(shape) == 0), 1.0, 0.0).astype(BF16)
    return dot_tn(rows.astype(BF16), pick)


def visible(segment_row, length):
    shape = (length, length)
    row, column = sublanes(shape), lanes(shape)
    segment = jnp.sum(jnp.where(row == column, segment_row, 0.0), axis=1, keepdims=True)
    return (row >= column) & (segment == segment_row)


def chance_of(query, keys, allowed):
    scores = dot_nt(query, keys) * (1.0 / math.sqrt(HEAD_DIM))
    scores = jnp.where(allowed, scores, HIDDEN)
    grown = jnp.exp(scores - jnp.max(scores, axis=1, keepdims=True))
    return grown * (1.0 / jnp.sum(grown, axis=1, keepdims=True))


def params(mib=56, **more):
    return pltpu.CompilerParams(vmem_limit_bytes=mib * MIB, **more)


def cost(flops=1):
    return pl.CostEstimate(flops=flops, bytes_accessed=1, transcendentals=0)


def shaped(dtype, *shape):
    return jax.ShapeDtypeStruct(shape, dtype)


def pack_kernel(
    joint_ref, up_ref, router_ref, mix_ref, gain_a_ref, gain_f_ref, pack_ref, *, teams
):
    rows = joint_ref.shape[0]
    width = joint_ref.shape[1] // 3
    part = width // TEAM
    block = up_ref.shape[1] // (teams * TEAM)
    count = router_ref.shape[1]
    wide = pack_ref.shape[2] - teams * block
    shape = (rows, wide - 3 * part)
    spread = (count, shape[1])
    spread = jnp.where(lanes(spread) == sublanes(spread), 1.0, 0.0).astype(BF16)
    small = dot(router_ref[...], spread)
    lane = lanes(shape)
    square = (rows, rows)
    same = sublanes(square) == lanes(square)
    columns = [mix_ref[0:1], mix_ref[1:2], gain_a_ref[...], gain_f_ref[...]]
    for i, row in enumerate(columns):
        column = jnp.sum(jnp.where(same, row.astype(F32), 0.0), axis=1, keepdims=True)
        small += jnp.where(lane == count + i, column, 0.0)
    small = small.astype(BF16)
    for p in range(TEAM):
        pieces = [joint_ref[:, c * width + p * part : c * width + (p + 1) * part] for c in range(3)]
        for g in range(teams):
            start = (g * TEAM + p) * block
            pieces.append(up_ref[:, start : start + block])
        pack_ref[p] = jnp.concatenate(pieces[:3] + [small] + pieces[3:], axis=1)


def attend_kernel(place_ref, n0_ref, n1_ref, f0_ref, f1_ref, got_ref, joint_ref, out_ref, *, count):
    _, length, part = out_ref.shape
    members = [ref.at[i] for ref in (n0_ref, n1_ref, f0_ref, f1_ref) for i in range(2)]
    gains = gain_rows(got_ref[:, 3 * part :], count)
    lane = lanes((length, part))
    for j in range(TEAM // 2):
        pair = (members[j], members[j + TEAM // 2])
        x = jnp.concatenate([ref[:length] for ref in pair], axis=0).astype(F32)
        unit, _ = normed(x)
        first = (unit * gains[0:1]).astype(BF16)
        joint = dot(first, got_ref[:, : 3 * part]).astype(BF16)
        for k, ref in enumerate(pair):
            allowed = visible(ref[length:, :length].astype(F32)[0:1], length)
            own = joint[k * length : (k + 1) * length]
            query, keys, values = own[:, :part], own[:, part : 2 * part], own[:, 2 * part :]
            total = jnp.zeros((length, part), F32)
            for h in range(part // HEAD_DIM):
                mine = lane // HEAD_DIM == h
                chance = chance_of(jnp.where(mine, query, 0), keys, allowed)
                total += dot(chance.astype(BF16), jnp.where(mine, values, 0))
            member = place_ref[0] ^ (2 * j + k)
            joint_ref[member] = own
            out_ref[member] = total.astype(BF16)


def attend(place, xs, got, length, count):
    part = xs[0].shape[2] // TEAM
    return pl.pallas_call(
        functools.partial(attend_kernel, count=count),
        in_specs=[pl.BlockSpec(memory_space=pltpu.SMEM)]
        + [pl.BlockSpec(memory_space=pltpu.VMEM)] * 5,
        out_shape=(shaped(BF16, TEAM, length, 3 * part), shaped(BF16, TEAM, length, part)),
        compiler_params=params(56),
        cost_estimate=cost(),
        name="attend",
    )(place, *xs, got)


def attend_back_kernel(
    place_ref, n0_ref, n1_ref, f0_ref, f1_ref, near_att, far_att, got_ref, joint_ref, d_ref, side_ref,
    keep_ref, send_ref, grad_ref, d_joint_ref, first_ref, unit_ref, d_merged_ref, *, count,
):
    _, length, wide = joint_ref.shape
    part = wide // 3
    half, _, width = near_att.shape
    shrink = 1.0 / math.sqrt(HEAD_DIM)
    gains = gain_rows(got_ref[:, 3 * part :], count)
    lane = lanes((length, part))

    def step(i, carry, start, k, ref):
        j = start + i
        rows = pl.ds(pl.multiple_of((k * half + j) * length, length), length)
        x = ref[i]
        unit, _ = normed(x[:length].astype(F32))
        unit_ref[rows] = unit
        first_ref[rows] = (unit * gains[0:1]).astype(BF16)
        allowed = visible(x[length:, :length].astype(F32)[0:1], length)
        member = place_ref[0] ^ (2 * j + k)
        own = joint_ref[member]
        both = d_ref[member]
        d_own = both[:length]
        d_merged_ref[rows] = both[length:]
        query, keys, values = own[:, :part], own[:, part : 2 * part], own[:, 2 * part :]
        d_query = jnp.zeros((length, part), F32)
        d_keys = jnp.zeros((length, part), F32)
        d_values = jnp.zeros((length, part), F32)
        for h in range(part // HEAD_DIM):
            mine = lane // HEAD_DIM == h
            q = jnp.where(mine, query, 0)
            d_head = jnp.where(mine, d_own, 0)
            chance = chance_of(q, keys, allowed)
            d_weights = dot_nt(d_head, values)
            inner = jnp.sum(chance * d_weights, axis=1, keepdims=True)
            d_scores = (chance * (d_weights - inner)).astype(BF16)
            d_query += dot(d_scores, jnp.where(mine, keys, 0))
            d_keys += dot_tn(d_scores, q)
            d_values += dot_tn(chance.astype(BF16), d_head)
        d_joint_ref[rows, :part] = (d_query * shrink).astype(BF16)
        d_joint_ref[rows, part : 2 * part] = (d_keys * shrink).astype(BF16)
        d_joint_ref[rows, 2 * part :] = d_values.astype(BF16)
        return carry

    for k, pair in enumerate(((n0_ref, n1_ref), (f0_ref, f1_ref))):
        for a, ref in enumerate(pair):
            lax.fori_loop(0, 2, functools.partial(step, start=2 * a, k=k, ref=ref), 0)
    d_joint = d_joint_ref[...]
    d_first = dot_nt(d_joint, got_ref[:, : 3 * part])
    tall = half * length
    keep_ref[...] = d_first[:tall].reshape(keep_ref.shape)
    send_ref[...] = d_first[tall:].astype(BF16).reshape(send_ref.shape)
    gain = jnp.sum(d_first * unit_ref[...], axis=0, keepdims=True)
    gain = jnp.where(sublanes((8, width)) == 0, gain, 0.0)
    grad_ref[:, : 3 * part] = dot_tn(first_ref[...], d_joint).astype(BF16)
    side = side_ref[...] + column_of(gain, count + 3, side_ref.shape[1])
    grad_ref[:, 3 * part : -part] = side.astype(BF16)
    d_merged = d_merged_ref[...]
    merged = dot_tn(near_att[...].reshape(tall, width), d_merged[:tall])
    merged += dot_tn(far_att[...].reshape(tall, width), d_merged[tall:])
    grad_ref[:, -part:] = merged.astype(BF16)


def attend_back(place, xs, near_att, far_att, got, joint, d_both, side, count):
    half, length, width = near_att.shape
    part = width // TEAM
    tall = TEAM * length
    outs = (
        shaped(F32, half, length, width),
        shaped(BF16, half, length, width),
        shaped(BF16, width, 4 * part + side.shape[1]),
    )
    return pl.pallas_call(
        functools.partial(attend_back_kernel, count=count),
        in_specs=[pl.BlockSpec(memory_space=pltpu.SMEM)]
        + [pl.BlockSpec(memory_space=pltpu.VMEM)] * 10,
        out_shape=outs,
        scratch_shapes=[
            pltpu.VMEM((tall, 3 * part), BF16),
            pltpu.VMEM((tall, width), BF16),
            pltpu.VMEM((tall, width), F32),
            pltpu.VMEM((tall, part), BF16),
        ],
        compiler_params=params(56),
        cost_estimate=cost(int(2e10)),
        name="attend_back",
    )(place, *xs, near_att, far_att, got, joint, d_both, side)


def middle_kernel(
    att_ref, merge_ref, x_ref, small_ref, routes_ref, placing_ref,
    residual_ref, second_ref, attended_ref, stats_ref, out_ref, *, count,
):
    length, width = x_ref.shape
    small = small_ref[:, 3 * width // TEAM :]
    gains = gain_rows(small, count)
    attended = jnp.concatenate([att_ref[p] for p in range(TEAM)], axis=1)
    residual = x_ref[...].astype(F32) + dot(attended, merge_ref[...])
    residual_ref[...] = residual
    unit, _ = normed(residual)
    second = (unit * gains[1:2]).astype(BF16)
    second_ref[...] = second
    attended_ref[...] = attended
    logits = dot(second, small)
    lane = lanes(logits.shape)
    routed = jnp.where(lane < count, logits, HIDDEN)
    grown = jnp.exp(routed - jnp.max(routed, axis=1, keepdims=True))
    chances = grown * (1.0 / jnp.sum(grown, axis=1, keepdims=True))
    mixed = jnp.where((lane >= count) & (lane < count + 2), logits, HIDDEN)
    grown = jnp.exp(mixed - jnp.max(mixed, axis=1, keepdims=True))
    mix = grown * (1.0 / jnp.sum(grown, axis=1, keepdims=True))
    routes = routes_ref[...]
    onehot = lane == routes
    gate = jnp.sum(jnp.where(onehot, chances, 0.0), axis=1, keepdims=True)
    mix_expert = jnp.sum(jnp.where(lane == count + 1, mix, 0.0), axis=1, keepdims=True)
    stats_ref[...] = chances + mix + jnp.where(lane == count + 2, gate, 0.0)
    scale = mix_expert * gate
    high = scale.astype(BF16).astype(F32)
    middle_part = (scale - high).astype(BF16).astype(F32)
    low = scale - high - middle_part
    spread = (length, out_ref.shape[1] - width)
    lane = lanes(spread)
    scales = jnp.where(lane == 0, high, 0.0) + jnp.where(lane == 1, middle_part, 0.0)
    scales += jnp.where(lane == 2, low, 0.0)
    placing = placing_ref[...]
    out_ref[:, :width] = dot_tn(placing, second).astype(BF16)
    out_ref[:, width:] = dot_tn(placing, scales.astype(BF16)).astype(BF16)


def place_kernel(routes_ref, g_ref, placing_ref, out_ref, *, count, capacity):
    length = g_ref.shape[0]
    routes = routes_ref[...]
    onehot = jnp.where(lanes((length, -(-count // 128) * 128)) == routes, 1.0, 0.0)
    shape = (length, length)
    before = jnp.where(sublanes(shape) > lanes(shape), 1.0, 0.0).astype(BF16)
    rank = jnp.sum(onehot * dot(before, onehot.astype(BF16)), axis=1, keepdims=True)
    slot = routes * capacity + rank.astype(jnp.int32)
    placing = jnp.where(lanes((length, count * capacity)) == slot, 1.0, 0.0).astype(BF16)
    placing_ref[...] = placing
    out_ref[...] = dot_tn(placing, g_ref[...]).astype(BF16)


def place_rows(routes, cotangent, count, capacity):
    length, width = cotangent.shape
    return pl.pallas_call(
        functools.partial(place_kernel, count=count, capacity=capacity),
        out_shape=(
            shaped(BF16, length, count * capacity),
            shaped(BF16, count * capacity, width),
        ),
        compiler_params=params(56),
        cost_estimate=cost(),
        name="place_rows",
    )(routes, cotangent)


def middle(att, merge, tokens, got, routes, placing, count):
    length, width = tokens.shape
    lanes_small = got.shape[1] - 3 * width // TEAM
    outs = (
        shaped(F32, length, width),
        shaped(BF16, length, width),
        shaped(BF16, length, width),
        shaped(F32, length, lanes_small),
        shaped(BF16, placing.shape[1], width + 128),
    )
    return pl.pallas_call(
        functools.partial(middle_kernel, count=count),
        out_shape=outs,
        compiler_params=params(56),
        cost_estimate=cost(),
        name="middle",
    )(att, merge, tokens, got, routes, placing)


def expert_kernel(
    rows_ref, g_ref, widen_hbm, narrow_hbm, act_hbm, d_hbm, back_ref, d_out_ref,
    widen_ref, narrow_ref, act_ref, d_ref, in_sems, out_sems, *, chunk,
):
    width, hidden = widen_ref.shape
    copies = []
    for i in range(hidden // chunk):
        part = pl.ds(i * chunk, chunk)
        wide = (widen_hbm.at[0, :, part], widen_ref.at[:, part], in_sems.at[2 * i])
        tall = (narrow_hbm.at[0, part, :], narrow_ref.at[part, :], in_sems.at[2 * i + 1])
        copies.append([pltpu.make_async_copy(*wide), pltpu.make_async_copy(*tall)])
    for pair in copies:
        for copy in pair:
            copy.start()
    scale = jnp.sum(rows_ref[:, width:].astype(F32), axis=1, keepdims=True)
    d_out_ref[...] = (g_ref[...].astype(F32) * scale).astype(BF16)

    def step(i, carry):
        part = pl.ds(pl.multiple_of(i * chunk, chunk), chunk)
        wide = (widen_hbm.at[0, :, part], widen_ref.at[:, part], in_sems.at[2 * i])
        tall = (narrow_hbm.at[0, part, :], narrow_ref.at[part, :], in_sems.at[2 * i + 1])
        pltpu.make_async_copy(*wide).wait()
        pltpu.make_async_copy(*tall).wait()
        upper = dot(rows_ref[:, :width], widen_ref[:, part])
        d_act = dot_nt(d_out_ref[...], narrow_ref[part])
        act, slope = gelu_both(upper)
        act_ref[:, part] = act.astype(BF16)
        d_ref[:, part] = (slope * d_act).astype(BF16)
        return carry

    lax.fori_loop(0, hidden // chunk, step, 0)
    outs = [
        pltpu.make_async_copy(act_ref, act_hbm, out_sems.at[0]),
        pltpu.make_async_copy(d_ref, d_hbm, out_sems.at[1]),
    ]
    for copy in outs:
        copy.start()
    half = width // 4

    def finish(i, carry):
        here, there = [pl.ds(pl.multiple_of(j, half), half) for j in (i * half, width + i * half)]
        back_ref[:, here] = dot(act_ref[...], narrow_ref[:, here]).astype(BF16)
        back_ref[:, there] = dot_nt(d_ref[...], widen_ref[here]).astype(BF16)
        return carry

    lax.fori_loop(0, 4, finish, 0)
    for copy in outs:
        copy.wait()


def expert(rows, g_rows, widen, narrow, chunk=512):
    slots, width = g_rows.shape
    hidden = widen.shape[2]
    left = pl.BlockSpec(memory_space=pl.ANY)
    here = pl.BlockSpec(memory_space=pltpu.VMEM)
    return pl.pallas_call(
        functools.partial(expert_kernel, chunk=chunk),
        in_specs=[here, here, left, left],
        out_specs=[left, left, here, here],
        out_shape=(
            shaped(BF16, slots, hidden),
            shaped(BF16, slots, hidden),
            shaped(BF16, slots, 2 * width),
            shaped(BF16, slots, width),
        ),
        scratch_shapes=[
            pltpu.VMEM((width, hidden), BF16),
            pltpu.VMEM((hidden, width), BF16),
            pltpu.VMEM((slots, hidden), BF16),
            pltpu.VMEM((slots, hidden), BF16),
            pltpu.SemaphoreType.DMA((2 * (hidden // chunk),)),
            pltpu.SemaphoreType.DMA((2,)),
        ],
        compiler_params=params(56),
        cost_estimate=cost(),
        name="expert",
    )(rows, g_rows, widen, narrow)


def narrow_grad_kernel(rows_ref, act_ref, out_ref):
    out_ref[0] = dot_tn(act_ref[...], rows_ref[...])


def narrow_grads(rows, act, chunk=512):
    slots, width = rows.shape
    hidden = act.shape[1]
    return pl.pallas_call(
        narrow_grad_kernel,
        grid=(hidden // chunk,),
        in_specs=[
            pl.BlockSpec((slots, width), lambda f: (0, 0)),
            pl.BlockSpec((slots, chunk), lambda f: (0, f)),
        ],
        out_specs=pl.BlockSpec((1, chunk, width), lambda f: (0, f, 0)),
        out_shape=shaped(F32, 1, hidden, width),
        compiler_params=params(56),
        cost_estimate=cost(),
        name="narrow_grads",
    )(rows, act)


def widen_grad_kernel(rows_ref, d_ref, out_ref):
    out_ref[0] = dot_tn(rows_ref[...], d_ref[...])


def widen_grads(rows, d_upper, width, chunk=128):
    slots = rows.shape[0]
    hidden = d_upper.shape[1]
    return pl.pallas_call(
        widen_grad_kernel,
        grid=(width // chunk,),
        in_specs=[
            pl.BlockSpec((slots, chunk), lambda f: (0, f)),
            pl.BlockSpec((slots, hidden), lambda f: (0, 0)),
        ],
        out_specs=pl.BlockSpec((1, chunk, hidden), lambda f: (0, f, 0)),
        out_shape=shaped(F32, 1, width, hidden),
        compiler_params=params(56),
        cost_estimate=cost(),
        name="widen_grads",
    )(rows, d_upper)


def feed_kernel(
    near_ref, far_ref, g_near_ref, g_far_ref, up_ref, down_ref, small_ref,
    keep_ref, low_ref, high_ref, keep_dense_ref, send_dense_ref, up_grad_ref, down_grad_ref,
    *, count,
):
    half, length, width = near_ref.shape
    tall = half * length
    near, far = near_ref[...].reshape(tall, width), far_ref[...].reshape(tall, width)
    second = jnp.concatenate([near, far], axis=0)
    g = jnp.concatenate(
        [g_near_ref[...].reshape(tall, width), g_far_ref[...].reshape(tall, width)], axis=0
    ).astype(F32)
    logits = dot(second, small_ref[:, 3 * width // TEAM :])
    lane = lanes(logits.shape)
    mixed = jnp.where((lane >= count) & (lane < count + 2), logits, HIDDEN)
    grown = jnp.exp(mixed - jnp.max(mixed, axis=1, keepdims=True))
    mix = jnp.sum(jnp.where(lane == count, grown, 0.0), axis=1, keepdims=True)
    mix = mix * (1.0 / jnp.sum(grown, axis=1, keepdims=True))
    d_dense = (g * mix).astype(BF16)
    act, slope = gelu_both(dot(second, up_ref[...]))
    act = act.astype(BF16)
    d_upper = (slope * dot_nt(d_dense, down_ref[...])).astype(BF16)
    d_second = dot_nt(d_upper, up_ref[...])
    dense = dot(act, down_ref[...])
    along = jnp.sum(g * dense, axis=1, keepdims=True)
    rest = along - along.astype(BF16).astype(F32)
    lane = lanes((2 * tall, 128))
    along = jnp.where(lane == 0, along, 0.0) + jnp.where(lane == 1, rest, 0.0)
    keep_ref[:, :, :width] = d_second[:tall].reshape(half, length, width)
    keep_ref[:, :, width:] = along[:tall].reshape(half, length, 128)
    sent = d_second[tall:].astype(BF16).reshape(half, length, width)
    low_ref[...] = sent[:, :, : width // 2]
    high_ref[:, :, : width // 2] = sent[:, :, width // 2 :]
    high_ref[:, :, width // 2 :] = along[tall:].astype(BF16).reshape(half, length, 128)
    keep_dense_ref[...] = dense[:tall].reshape(half, length, width)
    send_dense_ref[...] = dense[tall:].astype(BF16).reshape(half, length, width)
    up_grad_ref[...] = dot_tn(second, d_upper).astype(BF16)
    down_grad_ref[...] = dot_tn(act, d_dense).astype(BF16)


def feed(near, far, g_near, g_far, up, down, got, count):
    half, length, width = near.shape
    hidden = up.shape[1]
    outs = (
        shaped(F32, half, length, width + 128),
        shaped(BF16, half, length, width // 2),
        shaped(BF16, half, length, width // 2 + 128),
        shaped(F32, half, length, width),
        shaped(BF16, half, length, width),
        shaped(BF16, width, hidden),
        shaped(BF16, hidden, width),
    )
    return pl.pallas_call(
        functools.partial(feed_kernel, count=count),
        out_shape=outs,
        compiler_params=params(56),
        cost_estimate=cost(),
        name="feed",
    )(near, far, g_near, g_far, up, down, got)


def halve_kernel(keep_ref, *refs, pieces):
    got_refs, own_ref, send_refs = refs[:pieces], refs[pieces], refs[pieces + 1 :]
    size = 16

    def step(i, carry):
        rows = pl.ds(pl.multiple_of(i * size, size), size)
        start = 0
        for got_ref in got_refs:
            part = slice(start, start + got_ref.shape[2])
            own_ref[rows, part] = keep_ref[0, rows, part] + got_ref[0, rows].astype(F32)
            for j, ref in enumerate(send_refs):
                total = keep_ref[j + 1, rows, part] + got_ref[j + 1, rows].astype(F32)
                ref[rows, part] = total.astype(BF16)
            start = part.stop
        return carry

    lax.fori_loop(0, own_ref.shape[0] // size, step, 0)


def halve(keep, got):
    half, length, width = keep.shape
    outs = (shaped(F32, length, width),) + (shaped(BF16, length, width),) * (half - 1)
    return pl.pallas_call(
        functools.partial(halve_kernel, pieces=len(got)),
        out_shape=outs,
        compiler_params=params(20),
        cost_estimate=cost(),
        name="halve",
    )(keep, *got)


def after_kernel(
    own_ref, r1_ref, r2_ref, r3_ref, back_ref, placing_ref, residual_ref, stats_ref, g_ref,
    small_ref, merge_ref, routes_ref, second_ref,
    result_ref, d_residual_ref, side_ref, d_ref, *, count,
):
    length, width = g_ref.shape
    part = width // TEAM
    small = small_ref[:, 3 * part :]
    gains = gain_rows(small, count)
    summed = (
        own_ref[...] + r1_ref[...].astype(F32) + r2_ref[...].astype(F32) + r3_ref[...].astype(F32)
    )
    d_second = summed[:, :width]
    d_mix_dense = jnp.sum(summed[:, width:], axis=1, keepdims=True)
    stats = stats_ref[...]
    lane = lanes(stats.shape)
    column = lambda i: jnp.sum(jnp.where(lane == i, stats, 0.0), axis=1, keepdims=True)
    mix_dense, mix_expert, gate = column(count), column(count + 1), column(count + 2)
    residual = residual_ref[...]
    g = g_ref[...].astype(F32)
    returned = dot(placing_ref[...], back_ref[:, :width])
    result_ref[...] = residual + mix_expert * gate * returned
    along = jnp.sum(g * returned, axis=1, keepdims=True)
    d_mix_expert = gate * along
    mean = mix_dense * d_mix_dense + mix_expert * d_mix_expert
    onehot = jnp.where(lane == routes_ref[...], 1.0, 0.0)
    side = jnp.where(lane < count, stats * (onehot - gate) * (mix_expert * along), 0.0)
    side += jnp.where(lane == count, mix_dense * (d_mix_dense - mean), 0.0)
    side += jnp.where(lane == count + 1, mix_expert * (d_mix_expert - mean), 0.0)
    side = side.astype(BF16)
    d_second += dot(placing_ref[...], back_ref[:, width:]) + dot_nt(side, small)
    unit, scale = normed(residual)
    d_residual = g + norm_back(d_second * gains[1:2], unit, scale)
    d_residual_ref[...] = d_residual
    d_merged = d_residual.astype(BF16)
    side_grad = dot_tn(second_ref[...], side)
    feed_row = jnp.sum(d_second * unit, axis=0, keepdims=True)
    feed_rows = jnp.where(sublanes((8, width)) == 0, feed_row, 0.0)
    side_ref[...] = side_grad + column_of(feed_rows, count + 2, side.shape[1])
    d_att = dot_nt(d_merged, merge_ref[...]).astype(BF16)
    for p in range(TEAM):
        d_ref[p, :length] = d_att[:, p * part : (p + 1) * part]
        d_ref[p, length:] = d_merged[:, p * part : (p + 1) * part]


def after(
    own, others, back, placing, residual, stats, cotangent, got, merge, routes, second, count
):
    length, width = cotangent.shape
    part = width // TEAM
    outs = (
        shaped(F32, length, width),
        shaped(F32, length, width),
        shaped(F32, width, got.shape[1] - 3 * part),
        shaped(BF16, TEAM, 2 * length, part),
    )
    return pl.pallas_call(
        functools.partial(after_kernel, count=count),
        out_shape=outs,
        compiler_params=params(56),
        cost_estimate=cost(),
        name="after",
    )(own, *others, back, placing, residual, stats, cotangent, got, merge, routes, second)


def last_kernel(
    own_ref, r1_ref, r2_ref, r3_ref, dense_ref, d1_ref, d2_ref, d3_ref, part_ref, stats_ref,
    x_ref, d_residual_ref, small_ref, out_ref, result_ref, *, count,
):
    part = x_ref.shape[1] // TEAM
    gains = gain_rows(small_ref[:, 3 * part :], count)
    size = 32

    def step(i, carry):
        rows = pl.ds(pl.multiple_of(i * size, size), size)
        add = lambda own, *others: own[rows] + sum(ref[rows].astype(F32) for ref in others)
        d_first = add(own_ref, r1_ref, r2_ref, r3_ref)
        unit, scale = normed(x_ref[rows].astype(F32))
        out_ref[rows] = (
            d_residual_ref[rows] + norm_back(d_first * gains[0:1], unit, scale)
        ).astype(BF16)
        stats = stats_ref[rows]
        picked = jnp.where(lanes(stats.shape) == count, stats, 0.0)
        mix_dense = jnp.sum(picked, axis=1, keepdims=True)
        dense = add(dense_ref, d1_ref, d2_ref, d3_ref)
        result_ref[rows] = (part_ref[rows] + mix_dense * dense).astype(BF16)
        return carry

    lax.fori_loop(0, x_ref.shape[0] // size, step, 0)


def last(own, others, dense, more, part, stats, tokens, d_residual, got, count):
    return pl.pallas_call(
        functools.partial(last_kernel, count=count),
        out_shape=(shaped(BF16, *tokens.shape),) * 2,
        compiler_params=params(16),
        cost_estimate=cost(),
        name="last",
    )(own, *others, dense, *more, part, stats, tokens, d_residual, got)


def owner_kernel(
    got_ref, up_got_ref, joint_ref, merge_ref, up_ref, attend_ref, feed_ref, router_ref, mix_ref,
    *, count,
):
    teams, _, rows, wide = got_ref.shape
    part = merge_ref.shape[1] // TEAM
    width = part * TEAM
    block = up_ref.shape[1] // (TEAM * teams)

    def step(p, total):
        own = got_ref[0, p].astype(F32)
        for g in range(1, teams):
            own += got_ref[g, p].astype(F32)
        for c in range(3):
            start = pl.multiple_of(c * width + p * part, part)
            joint_ref[:, pl.ds(start, part)] = own[:, c * part : (c + 1) * part]
        merge_ref[:, pl.ds(pl.multiple_of(p * part, part), part)] = own[:, wide - part :]
        return total + own[:, 3 * part : wide - part]

    total = lax.fori_loop(0, TEAM, step, jnp.zeros((rows, wide - 4 * part), F32))
    for p in range(TEAM):
        for g in range(teams):
            start = (g * TEAM + p) * block
            piece = up_got_ref[p, :, g * block : (g + 1) * block]
            up_ref[:, start : start + block] = piece.astype(F32)
    router_ref[...] = total[:, :count]
    same = sublanes((rows, rows)) == lanes((rows, rows))

    def row(lane):
        column = jnp.sum(jnp.where(lanes(total.shape) == lane, total, 0.0), axis=1, keepdims=True)
        return jnp.sum(jnp.where(same, column, 0.0), axis=0, keepdims=True)

    mix_ref[0:1] = row(count)
    mix_ref[1:2] = row(count + 1)
    feed_ref[...] = row(count + 2)
    attend_ref[...] = row(count + 3)


def owner_sums(got, up, width, hidden, count):
    rows = got.shape[2]
    outs = (
        shaped(F32, rows, 3 * width),
        shaped(F32, rows, width),
        shaped(F32, rows, hidden),
        shaped(F32, 1, rows),
        shaped(F32, 1, rows),
        shaped(F32, rows, count),
        shaped(F32, 2, rows),
    )
    return pl.pallas_call(
        functools.partial(owner_kernel, count=count),
        out_shape=outs,
        compiler_params=params(12),
        cost_estimate=cost(),
        name="owner_sums",
    )(got, up)


def order_kernel(place_ref, near_ref, far_ref, out_ref):
    teams, _, rows, _ = out_ref.shape

    def step(j, carry):
        for k, ref in enumerate((near_ref, far_ref)):
            for d in range(teams):
                team = (place_ref[1] + d) & (teams - 1)
                out_ref[team, place_ref[0] ^ (2 * j + k)] = ref[j, d * rows : (d + 1) * rows]
        return carry

    lax.fori_loop(0, TEAM // 2, step, 0)


def order(place, near, far, teams):
    _, tall, width = near.shape
    out = shaped(BF16, teams, TEAM, tall // teams, width)
    return pl.pallas_call(
        order_kernel,
        in_specs=[pl.BlockSpec(memory_space=pltpu.SMEM)]
        + [pl.BlockSpec(memory_space=pltpu.VMEM)] * 2,
        out_shape=out,
        compiler_params=params(56),
        cost_estimate=cost(),
        name="order",
    )(place, near, far)


def body(
    tokens,
    gain_attend,
    joint_weight,
    merge_weight,
    gain_feed,
    up_weight,
    down_weight,
    router_weight,
    mix_weight,
    widen_weight,
    narrow_weight,
    routes,
    segments,
    cotangent,
):
    count = lax.axis_size("expert")
    teams = count // TEAM
    place = (lax.axis_index("expert") & (TEAM - 1)).astype(jnp.int32)
    team = lax.axis_index("expert") >> 3
    place_arg = jnp.stack([place, team.astype(jnp.int32)])
    length, width = tokens.shape
    capacity = max(2, 2 * length // count)
    planes = [[g * TEAM + p for p in range(TEAM)] for g in range(teams)]
    lines = [[g * TEAM + p for g in range(teams)] for p in range(TEAM)]
    rows = joint_weight.shape[0]
    part = width // TEAM
    hidden = up_weight.shape[1]
    block = hidden // count

    def swap(value, mask):
        return lax.ppermute(value, "expert", [(i, i ^ mask) for i in range(count)])

    def exchange(value):
        return lax.all_to_all(value, "expert", 0, 0, tiled=True)

    def team_exchange(value):
        return lax.all_to_all(value, "expert", 0, 0, tiled=True, axis_index_groups=planes)

    def line_gather(value):
        return lax.all_gather(value, "expert", axis=0, tiled=True, axis_index_groups=lines)

    def line_scatter(value):
        return lax.psum_scatter(
            value, "expert", scatter_dimension=0, tiled=True, axis_index_groups=lines
        )

    def together(*values):
        return lax.optimization_barrier(values)

    def team_sends(value):
        return [value, swap(value, 2), swap(value, 4), swap(value, 6)]

    def team_joins(values):
        near = jnp.stack(values)
        return near, swap(near, 1)

    def team_scatter(keep, *sent):
        own, *sends = halve(keep, [swap(a, 1) for a in sent])
        return own, [swap(s, 2 * j + 2) for j, s in enumerate(sends)]

    small_width = -(-(count + 4) // 128) * 128
    pack_out = shaped(BF16, TEAM, rows, 3 * part + small_width + teams * block)
    pack = pl.pallas_call(
        functools.partial(pack_kernel, teams=teams),
        out_shape=pack_out,
        compiler_params=params(56),
        cost_estimate=cost(),
        name="pack",
    )(
        joint_weight,
        up_weight,
        router_weight,
        mix_weight.T,
        gain_attend[None],
        gain_feed[None],
    )
    pack, merge_weight = together(pack, merge_weight)
    pack = team_exchange(pack).reshape(TEAM * rows, -1)
    placing, g_rows = place_rows(routes, cotangent, count, capacity)
    from_team = lambda d: [
        ((g + d) % teams * TEAM + p, g * TEAM + p) for g in range(teams) for p in range(TEAM)
    ]
    merge_line = [merge_weight]
    merge_line += [lax.ppermute(merge_weight, "expert", from_team(d)) for d in range(1, teams)]
    pack, tokens, g_rows, *merge_line = together(pack, tokens, g_rows, *merge_line)
    joint_rows, g_rows = together(pack[:, : 3 * part + small_width], g_rows)
    g_rows = exchange(g_rows.reshape(count, capacity, width)).reshape(count * capacity, width)
    merge_line = jnp.concatenate(merge_line, axis=0)
    wide = 3 * part + small_width
    x_sent = jnp.concatenate(
        [
            tokens,
            jnp.pad(segments.astype(BF16), ((0, 15), (0, width - length))),
        ],
        axis=0,
    )
    got = line_gather(joint_rows)
    sends = team_sends(x_sent)
    xs = [jnp.stack(sends[:2]), jnp.stack(sends[2:])]
    *xs, pack, g_rows = together(*xs, pack, g_rows)
    xs = xs + [swap(x, 1) for x in xs]
    up_part = line_gather(pack[:, 3 * part + small_width :])
    merge_parts = team_sends(merge_line)

    joint, attended = attend(place_arg, xs, got, length, count)
    attended, *merge_parts = together(attended, *merge_parts)
    merge_near, merge_far = team_joins(merge_parts)
    arrived = team_exchange(attended)
    merge = order(place_arg, merge_near, merge_far, teams).reshape(width, width)
    residual, second, attended, stats, outgoing = middle(
        arrived, merge, tokens, got, routes, placing, count
    )
    received = exchange(outgoing.reshape(count, capacity, -1)).reshape(count * capacity, -1)
    s_near, attended, up_part = together(jnp.stack(team_sends(second)), attended, up_part)
    s_far = swap(s_near, 1)
    a_parts = team_sends(jnp.concatenate([attended, cotangent], axis=0))
    received, s_near, s_far, down_own = together(received, s_near, s_far, down_weight)
    down_part = line_gather(down_own)
    act, d_eupper, back, d_out = expert(received, g_rows, widen_weight, narrow_weight)
    back, s_near, up_part, *a_parts = together(back, s_near, up_part, *a_parts)
    g_near, g_far = team_joins([a[length:] for a in a_parts])
    a_parts = [a[:length] for a in a_parts]
    back = exchange(back.reshape(count, capacity, -1)).reshape(count * capacity, -1)
    keep, low, high, keep_dense, send_dense, up_grad, down_grad = feed(
        s_near, s_far, g_near, g_far, up_part, down_part, got, count
    )
    up_grad = line_scatter(up_grad)
    own, others = team_scatter(keep, low, high)
    own, send_dense, down_grad, d_eupper = together(own, send_dense, down_grad, d_eupper)
    down_grad = line_scatter(down_grad)
    widen_grad = widen_grads(received, d_eupper, width)
    back, widen_grad = together(back, widen_grad)
    a_near, a_far = team_joins(a_parts)
    dense, more = team_scatter(keep_dense, send_dense)
    result, d_residual, side, d_both = after(
        own, others, back, placing, residual, stats, cotangent, got, merge, routes, second, count
    )
    d_both, act = together(d_both, act)
    d_both = team_exchange(d_both)
    narrow_grad = narrow_grads(d_out, act)
    d_both, narrow_grad, up_grad = together(d_both, narrow_grad, up_grad)
    up_grad = team_exchange(up_grad.reshape(TEAM, rows, -1))
    keep, send, grads = attend_back(
        place_arg, xs, a_near, a_far, got, joint, d_both, side, count
    )
    grads, send, up_grad, down_grad = together(grads, send, up_grad, down_grad)
    grads = exchange(grads.reshape(count, rows, -1))
    own, others = team_scatter(keep, send)
    tokens_grad, result = last(
        own, others, dense, more, result, stats, tokens, d_residual, got, count
    )
    grads, tokens_grad = together(grads, tokens_grad)
    grads = grads.reshape(teams, TEAM, rows, -1)
    joint_grad, merge_grad, up_grad, attend_grad, feed_grad, router_grad, mix_grad = owner_sums(
        grads, up_grad, width, hidden, count
    )
    return (
        result,
        tokens_grad,
        attend_grad.reshape(rows),
        joint_grad,
        merge_grad,
        feed_grad.reshape(rows),
        up_grad,
        down_grad.astype(F32),
        router_grad,
        mix_grad.T,
        widen_grad,
        narrow_grad,
    )


def solution(mesh):
    one, two, three = P("expert"), P("expert", None), P("expert", None, None)
    return jax.shard_map(
        body,
        mesh=mesh,
        in_specs=(two, one, two, two, one, two, two, two, two, three, three, two, two, two),
        out_specs=(two, two, one, two, two, one, two, two, two, two, three, three),
        check_vma=False,
    )
```

```python
import functools
import math

import jax
import jax.numpy as jnp
from jax import lax
from jax.experimental import pallas as pl
from jax.experimental.pallas import tpu as pltpu
from jax.sharding import PartitionSpec as P

HEAD_DIM = 64
TEAM = 8
EPSILON = 1e-05
HIDDEN = -1e30
F32 = jnp.float32
BF16 = jnp.bfloat16
CURVE = math.sqrt(2.0 / math.pi)
MIB = 1 << 20


def dot(left, right):
    return jnp.dot(left, right, preferred_element_type=F32)


def dot_tn(left, right):
    return lax.dot_general(left, right, (((0,), (0,)), ((), ())), preferred_element_type=F32)


def dot_nt(left, right):
    return lax.dot_general(left, right, (((1,), (1,)), ((), ())), preferred_element_type=F32)


def gelu_both(u):
    square = u * u
    bent = jnp.tanh(u * (CURVE + (CURVE * 0.044715) * square))
    half = 0.5 + 0.5 * bent
    slope = half + u * (1.0 - bent * bent) * (0.5 * CURVE + (0.5 * CURVE * 0.134145) * square)
    return u * half, slope


def normed(values):
    mean = jnp.mean(values, axis=-1, keepdims=True)
    centered = values - mean
    spread = jnp.mean(centered * centered, axis=-1, keepdims=True)
    scale = lax.rsqrt(spread + EPSILON)
    return centered * scale, scale


def norm_back(dn, unit, scale):
    return scale * (
        dn
        - jnp.mean(dn, axis=-1, keepdims=True)
        - unit * jnp.mean(dn * unit, axis=-1, keepdims=True)
    )


def lanes(shape):
    return lax.broadcasted_iota(jnp.int32, shape, 1)


def sublanes(shape):
    return lax.broadcasted_iota(jnp.int32, shape, 0)


def gain_rows(small, count):
    shape = (8, small.shape[1])
    pick = (lanes(shape) == sublanes(shape) + count + 2) & (sublanes(shape) < 2)
    return dot_nt(jnp.where(pick, 1.0, 0.0).astype(BF16), small)


def column_of(rows, lane, width):
    shape = (rows.shape[0], width)
    pick = jnp.where((lanes(shape) == lane) & (sublanes(shape) == 0), 1.0, 0.0).astype(BF16)
    return dot_tn(rows.astype(BF16), pick)


def visible(segment_row, length):
    shape = (length, length)
    row, column = sublanes(shape), lanes(shape)
    segment = jnp.sum(jnp.where(row == column, segment_row, 0.0), axis=1, keepdims=True)
    return (row >= column) & (segment == segment_row)


def chance_of(query, keys, allowed):
    scores = dot_nt(query, keys) * (1.0 / math.sqrt(HEAD_DIM))
    scores = jnp.where(allowed, scores, HIDDEN)
    grown = jnp.exp(scores - jnp.max(scores, axis=1, keepdims=True))
    return grown * (1.0 / jnp.sum(grown, axis=1, keepdims=True))


def params(mib=56, **more):
    return pltpu.CompilerParams(vmem_limit_bytes=mib * MIB, **more)


def cost(flops=1):
    return pl.CostEstimate(flops=flops, bytes_accessed=1, transcendentals=0)


def shaped(dtype, *shape):
    return jax.ShapeDtypeStruct(shape, dtype)


def pack_kernel(
    joint_ref, up_ref, router_ref, mix_ref, gain_a_ref, gain_f_ref, pack_ref, *, teams
):
    rows = joint_ref.shape[0]
    width = joint_ref.shape[1] // 3
    part = width // TEAM
    block = up_ref.shape[1] // (teams * TEAM)
    count = router_ref.shape[1]
    wide = pack_ref.shape[2] - teams * block
    shape = (rows, wide - 3 * part)
    spread = (count, shape[1])
    spread = jnp.where(lanes(spread) == sublanes(spread), 1.0, 0.0).astype(BF16)
    small = dot(router_ref[...], spread)
    lane = lanes(shape)
    square = (rows, rows)
    same = sublanes(square) == lanes(square)
    columns = [mix_ref[0:1], mix_ref[1:2], gain_a_ref[...], gain_f_ref[...]]
    for i, row in enumerate(columns):
        column = jnp.sum(jnp.where(same, row.astype(F32), 0.0), axis=1, keepdims=True)
        small += jnp.where(lane == count + i, column, 0.0)
    small = small.astype(BF16)
    for p in range(TEAM):
        pieces = [joint_ref[:, c * width + p * part : c * width + (p + 1) * part] for c in range(3)]
        for g in range(teams):
            start = (g * TEAM + p) * block
            pieces.append(up_ref[:, start : start + block])
        pack_ref[p] = jnp.concatenate(pieces[:3] + [small] + pieces[3:], axis=1)


def attend_kernel(place_ref, n0_ref, n1_ref, f0_ref, f1_ref, got_ref, joint_ref, out_ref, *, count):
    _, length, part = out_ref.shape
    members = [ref.at[i] for ref in (n0_ref, n1_ref, f0_ref, f1_ref) for i in range(2)]
    gains = gain_rows(got_ref[:, 3 * part :], count)
    lane = lanes((length, part))
    for j in range(TEAM // 2):
        pair = (members[j], members[j + TEAM // 2])
        x = jnp.concatenate([ref[:length] for ref in pair], axis=0).astype(F32)
        unit, _ = normed(x)
        first = (unit * gains[0:1]).astype(BF16)
        joint = dot(first, got_ref[:, : 3 * part]).astype(BF16)
        for k, ref in enumerate(pair):
            allowed = visible(ref[length:, :length].astype(F32)[0:1], length)
            own = joint[k * length : (k + 1) * length]
            query, keys, values = own[:, :part], own[:, part : 2 * part], own[:, 2 * part :]
            total = jnp.zeros((length, part), F32)
            for h in range(part // HEAD_DIM):
                mine = lane // HEAD_DIM == h
                chance = chance_of(jnp.where(mine, query, 0), keys, allowed)
                total += dot(chance.astype(BF16), jnp.where(mine, values, 0))
            member = place_ref[0] ^ (2 * j + k)
            joint_ref[member] = own
            out_ref[member] = total.astype(BF16)


def attend(place, xs, got, length, count):
    part = xs[0].shape[2] // TEAM
    return pl.pallas_call(
        functools.partial(attend_kernel, count=count),
        in_specs=[pl.BlockSpec(memory_space=pltpu.SMEM)]
        + [pl.BlockSpec(memory_space=pltpu.VMEM)] * 5,
        out_shape=(shaped(BF16, TEAM, length, 3 * part), shaped(BF16, TEAM, length, part)),
        compiler_params=params(56),
        cost_estimate=cost(),
        name="attend",
    )(place, *xs, got)


def attend_back_kernel(
    place_ref, n0_ref, n1_ref, f0_ref, f1_ref, near_att, far_att, got_ref, joint_ref, d_ref, side_ref,
    keep_ref, send_ref, grad_ref, d_joint_ref, first_ref, unit_ref, d_merged_ref, *, count,
):
    _, length, wide = joint_ref.shape
    part = wide // 3
    half, _, width = near_att.shape
    shrink = 1.0 / math.sqrt(HEAD_DIM)
    gains = gain_rows(got_ref[:, 3 * part :], count)
    lane = lanes((length, part))

    def step(i, carry, start, k, ref):
        j = start + i
        rows = pl.ds(pl.multiple_of((k * half + j) * length, length), length)
        x = ref[i]
        unit, _ = normed(x[:length].astype(F32))
        unit_ref[rows] = unit
        first_ref[rows] = (unit * gains[0:1]).astype(BF16)
        allowed = visible(x[length:, :length].astype(F32)[0:1], length)
        member = place_ref[0] ^ (2 * j + k)
        own = joint_ref[member]
        both = d_ref[member]
        d_own = both[:length]
        d_merged_ref[rows] = both[length:]
        query, keys, values = own[:, :part], own[:, part : 2 * part], own[:, 2 * part :]
        d_query = jnp.zeros((length, part), F32)
        d_keys = jnp.zeros((length, part), F32)
        d_values = jnp.zeros((length, part), F32)
        for h in range(part // HEAD_DIM):
            mine = lane // HEAD_DIM == h
            q = jnp.where(mine, query, 0)
            d_head = jnp.where(mine, d_own, 0)
            chance = chance_of(q, keys, allowed)
            d_weights = dot_nt(d_head, values)
            inner = jnp.sum(chance * d_weights, axis=1, keepdims=True)
            d_scores = (chance * (d_weights - inner)).astype(BF16)
            d_query += dot(d_scores, jnp.where(mine, keys, 0))
            d_keys += dot_tn(d_scores, q)
            d_values += dot_tn(chance.astype(BF16), d_head)
        d_joint_ref[rows, :part] = (d_query * shrink).astype(BF16)
        d_joint_ref[rows, part : 2 * part] = (d_keys * shrink).astype(BF16)
        d_joint_ref[rows, 2 * part :] = d_values.astype(BF16)
        return carry

    for k, pair in enumerate(((n0_ref, n1_ref), (f0_ref, f1_ref))):
        for a, ref in enumerate(pair):
            lax.fori_loop(0, 2, functools.partial(step, start=2 * a, k=k, ref=ref), 0)
    d_joint = d_joint_ref[...]
    d_first = dot_nt(d_joint, got_ref[:, : 3 * part])
    tall = half * length
    keep_ref[...] = d_first[:tall].reshape(keep_ref.shape)
    send_ref[...] = d_first[tall:].astype(BF16).reshape(send_ref.shape)
    gain = jnp.sum(d_first * unit_ref[...], axis=0, keepdims=True)
    gain = jnp.where(sublanes((8, width)) == 0, gain, 0.0)
    grad_ref[:, : 3 * part] = dot_tn(first_ref[...], d_joint).astype(BF16)
    side = side_ref[...] + column_of(gain, count + 3, side_ref.shape[1])
    grad_ref[:, 3 * part : -part] = side.astype(BF16)
    d_merged = d_merged_ref[...]
    merged = dot_tn(near_att[...].reshape(tall, width), d_merged[:tall])
    merged += dot_tn(far_att[...].reshape(tall, width), d_merged[tall:])
    grad_ref[:, -part:] = merged.astype(BF16)


def attend_back(place, xs, near_att, far_att, got, joint, d_both, side, count):
    half, length, width = near_att.shape
    part = width // TEAM
    tall = TEAM * length
    outs = (
        shaped(F32, half, length, width),
        shaped(BF16, half, length, width),
        shaped(BF16, width, 4 * part + side.shape[1]),
    )
    return pl.pallas_call(
        functools.partial(attend_back_kernel, count=count),
        in_specs=[pl.BlockSpec(memory_space=pltpu.SMEM)]
        + [pl.BlockSpec(memory_space=pltpu.VMEM)] * 10,
        out_shape=outs,
        scratch_shapes=[
            pltpu.VMEM((tall, 3 * part), BF16),
            pltpu.VMEM((tall, width), BF16),
            pltpu.VMEM((tall, width), F32),
            pltpu.VMEM((tall, part), BF16),
        ],
        compiler_params=params(56),
        cost_estimate=cost(int(2e10)),
        name="attend_back",
    )(place, *xs, near_att, far_att, got, joint, d_both, side)


def middle_kernel(
    att_ref, merge_ref, x_ref, small_ref, routes_ref, placing_ref,
    residual_ref, second_ref, attended_ref, stats_ref, out_ref, *, count,
):
    length, width = x_ref.shape
    small = small_ref[:, 3 * width // TEAM :]
    gains = gain_rows(small, count)
    attended = jnp.concatenate([att_ref[p] for p in range(TEAM)], axis=1)
    residual = x_ref[...].astype(F32) + dot(attended, merge_ref[...])
    residual_ref[...] = residual
    unit, _ = normed(residual)
    second = (unit * gains[1:2]).astype(BF16)
    second_ref[...] = second
    attended_ref[...] = attended
    logits = dot(second, small)
    lane = lanes(logits.shape)
    routed = jnp.where(lane < count, logits, HIDDEN)
    grown = jnp.exp(routed - jnp.max(routed, axis=1, keepdims=True))
    chances = grown * (1.0 / jnp.sum(grown, axis=1, keepdims=True))
    mixed = jnp.where((lane >= count) & (lane < count + 2), logits, HIDDEN)
    grown = jnp.exp(mixed - jnp.max(mixed, axis=1, keepdims=True))
    mix = grown * (1.0 / jnp.sum(grown, axis=1, keepdims=True))
    routes = routes_ref[...]
    onehot = lane == routes
    gate = jnp.sum(jnp.where(onehot, chances, 0.0), axis=1, keepdims=True)
    mix_expert = jnp.sum(jnp.where(lane == count + 1, mix, 0.0), axis=1, keepdims=True)
    stats_ref[...] = chances + mix + jnp.where(lane == count + 2, gate, 0.0)
    scale = mix_expert * gate
    high = scale.astype(BF16).astype(F32)
    middle_part = (scale - high).astype(BF16).astype(F32)
    low = scale - high - middle_part
    spread = (length, out_ref.shape[1] - width)
    lane = lanes(spread)
    scales = jnp.where(lane == 0, high, 0.0) + jnp.where(lane == 1, middle_part, 0.0)
    scales += jnp.where(lane == 2, low, 0.0)
    placing = placing_ref[...]
    out_ref[:, :width] = dot_tn(placing, second).astype(BF16)
    out_ref[:, width:] = dot_tn(placing, scales.astype(BF16)).astype(BF16)


def place_kernel(routes_ref, g_ref, placing_ref, out_ref, *, count, capacity):
    length = g_ref.shape[0]
    routes = routes_ref[...]
    onehot = jnp.where(lanes((length, -(-count // 128) * 128)) == routes, 1.0, 0.0)
    shape = (length, length)
    before = jnp.where(sublanes(shape) > lanes(shape), 1.0, 0.0).astype(BF16)
    rank = jnp.sum(onehot * dot(before, onehot.astype(BF16)), axis=1, keepdims=True)
    slot = routes * capacity + rank.astype(jnp.int32)
    placing = jnp.where(lanes((length, count * capacity)) == slot, 1.0, 0.0).astype(BF16)
    placing_ref[...] = placing
    out_ref[...] = dot_tn(placing, g_ref[...]).astype(BF16)


def place_rows(routes, cotangent, count, capacity):
    length, width = cotangent.shape
    return pl.pallas_call(
        functools.partial(place_kernel, count=count, capacity=capacity),
        out_shape=(
            shaped(BF16, length, count * capacity),
            shaped(BF16, count * capacity, width),
        ),
        compiler_params=params(56),
        cost_estimate=cost(),
        name="place_rows",
    )(routes, cotangent)


def middle(att, merge, tokens, got, routes, placing, count):
    length, width = tokens.shape
    lanes_small = got.shape[1] - 3 * width // TEAM
    outs = (
        shaped(F32, length, width),
        shaped(BF16, length, width),
        shaped(BF16, length, width),
        shaped(F32, length, lanes_small),
        shaped(BF16, placing.shape[1], width + 128),
    )
    return pl.pallas_call(
        functools.partial(middle_kernel, count=count),
        out_shape=outs,
        compiler_params=params(56),
        cost_estimate=cost(),
        name="middle",
    )(att, merge, tokens, got, routes, placing)


def expert_kernel(
    rows_ref, g_ref, widen_hbm, narrow_hbm, act_hbm, d_hbm, back_ref, d_out_ref,
    widen_ref, narrow_ref, act_ref, d_ref, in_sems, out_sems, *, chunk,
):
    width, hidden = widen_ref.shape
    copies = []
    for i in range(hidden // chunk):
        part = pl.ds(i * chunk, chunk)
        wide = (widen_hbm.at[0, :, part], widen_ref.at[:, part], in_sems.at[2 * i])
        tall = (narrow_hbm.at[0, part, :], narrow_ref.at[part, :], in_sems.at[2 * i + 1])
        copies.append([pltpu.make_async_copy(*wide), pltpu.make_async_copy(*tall)])
    for pair in copies:
        for copy in pair:
            copy.start()
    scale = jnp.sum(rows_ref[:, width:].astype(F32), axis=1, keepdims=True)
    d_out_ref[...] = (g_ref[...].astype(F32) * scale).astype(BF16)

    def step(i, carry):
        part = pl.ds(pl.multiple_of(i * chunk, chunk), chunk)
        wide = (widen_hbm.at[0, :, part], widen_ref.at[:, part], in_sems.at[2 * i])
        tall = (narrow_hbm.at[0, part, :], narrow_ref.at[part, :], in_sems.at[2 * i + 1])
        pltpu.make_async_copy(*wide).wait()
        pltpu.make_async_copy(*tall).wait()
        upper = dot(rows_ref[:, :width], widen_ref[:, part])
        d_act = dot_nt(d_out_ref[...], narrow_ref[part])
        act, slope = gelu_both(upper)
        act_ref[:, part] = act.astype(BF16)
        d_ref[:, part] = (slope * d_act).astype(BF16)
        return carry

    lax.fori_loop(0, hidden // chunk, step, 0)
    outs = [
        pltpu.make_async_copy(act_ref, act_hbm, out_sems.at[0]),
        pltpu.make_async_copy(d_ref, d_hbm, out_sems.at[1]),
    ]
    for copy in outs:
        copy.start()
    half = width // 4

    def finish(i, carry):
        here, there = [pl.ds(pl.multiple_of(j, half), half) for j in (i * half, width + i * half)]
        back_ref[:, here] = dot(act_ref[...], narrow_ref[:, here]).astype(BF16)
        back_ref[:, there] = dot_nt(d_ref[...], widen_ref[here]).astype(BF16)
        return carry

    lax.fori_loop(0, 4, finish, 0)
    for copy in outs:
        copy.wait()


def expert(rows, g_rows, widen, narrow, chunk=512):
    slots, width = g_rows.shape
    hidden = widen.shape[2]
    left = pl.BlockSpec(memory_space=pl.ANY)
    here = pl.BlockSpec(memory_space=pltpu.VMEM)
    return pl.pallas_call(
        functools.partial(expert_kernel, chunk=chunk),
        in_specs=[here, here, left, left],
        out_specs=[left, left, here, here],
        out_shape=(
            shaped(BF16, slots, hidden),
            shaped(BF16, slots, hidden),
            shaped(BF16, slots, 2 * width),
            shaped(BF16, slots, width),
        ),
        scratch_shapes=[
            pltpu.VMEM((width, hidden), BF16),
            pltpu.VMEM((hidden, width), BF16),
            pltpu.VMEM((slots, hidden), BF16),
            pltpu.VMEM((slots, hidden), BF16),
            pltpu.SemaphoreType.DMA((2 * (hidden // chunk),)),
            pltpu.SemaphoreType.DMA((2,)),
        ],
        compiler_params=params(56),
        cost_estimate=cost(),
        name="expert",
    )(rows, g_rows, widen, narrow)


def narrow_grad_kernel(rows_ref, act_ref, out_ref):
    out_ref[0] = dot_tn(act_ref[...], rows_ref[...])


def narrow_grads(rows, act, chunk=512):
    slots, width = rows.shape
    hidden = act.shape[1]
    return pl.pallas_call(
        narrow_grad_kernel,
        grid=(hidden // chunk,),
        in_specs=[
            pl.BlockSpec((slots, width), lambda f: (0, 0)),
            pl.BlockSpec((slots, chunk), lambda f: (0, f)),
        ],
        out_specs=pl.BlockSpec((1, chunk, width), lambda f: (0, f, 0)),
        out_shape=shaped(F32, 1, hidden, width),
        compiler_params=params(56),
        cost_estimate=cost(),
        name="narrow_grads",
    )(rows, act)


def widen_grad_kernel(rows_ref, d_ref, out_ref):
    out_ref[0] = dot_tn(rows_ref[...], d_ref[...])


def widen_grads(rows, d_upper, width, chunk=128):
    slots = rows.shape[0]
    hidden = d_upper.shape[1]
    return pl.pallas_call(
        widen_grad_kernel,
        grid=(width // chunk,),
        in_specs=[
            pl.BlockSpec((slots, chunk), lambda f: (0, f)),
            pl.BlockSpec((slots, hidden), lambda f: (0, 0)),
        ],
        out_specs=pl.BlockSpec((1, chunk, hidden), lambda f: (0, f, 0)),
        out_shape=shaped(F32, 1, width, hidden),
        compiler_params=params(56),
        cost_estimate=cost(),
        name="widen_grads",
    )(rows, d_upper)


def feed_kernel(
    near_ref, far_ref, g_near_ref, g_far_ref, up_ref, down_ref, small_ref,
    keep_ref, low_ref, high_ref, keep_dense_ref, send_dense_ref, up_grad_ref, down_grad_ref,
    *, count,
):
    half, length, width = near_ref.shape
    tall = half * length
    near, far = near_ref[...].reshape(tall, width), far_ref[...].reshape(tall, width)
    second = jnp.concatenate([near, far], axis=0)
    g = jnp.concatenate(
        [g_near_ref[...].reshape(tall, width), g_far_ref[...].reshape(tall, width)], axis=0
    ).astype(F32)
    logits = dot(second, small_ref[:, 3 * width // TEAM :])
    lane = lanes(logits.shape)
    mixed = jnp.where((lane >= count) & (lane < count + 2), logits, HIDDEN)
    grown = jnp.exp(mixed - jnp.max(mixed, axis=1, keepdims=True))
    mix = jnp.sum(jnp.where(lane == count, grown, 0.0), axis=1, keepdims=True)
    mix = mix * (1.0 / jnp.sum(grown, axis=1, keepdims=True))
    d_dense = (g * mix).astype(BF16)
    act, slope = gelu_both(dot(second, up_ref[...]))
    act = act.astype(BF16)
    d_upper = (slope * dot_nt(d_dense, down_ref[...])).astype(BF16)
    d_second = dot_nt(d_upper, up_ref[...])
    dense = dot(act, down_ref[...])
    along = jnp.sum(g * dense, axis=1, keepdims=True)
    rest = along - along.astype(BF16).astype(F32)
    lane = lanes((2 * tall, 128))
    along = jnp.where(lane == 0, along, 0.0) + jnp.where(lane == 1, rest, 0.0)
    keep_ref[:, :, :width] = d_second[:tall].reshape(half, length, width)
    keep_ref[:, :, width:] = along[:tall].reshape(half, length, 128)
    sent = d_second[tall:].astype(BF16).reshape(half, length, width)
    low_ref[...] = sent[:, :, : width // 2]
    high_ref[:, :, : width // 2] = sent[:, :, width // 2 :]
    high_ref[:, :, width // 2 :] = along[tall:].astype(BF16).reshape(half, length, 128)
    keep_dense_ref[...] = dense[:tall].reshape(half, length, width)
    send_dense_ref[...] = dense[tall:].astype(BF16).reshape(half, length, width)
    up_grad_ref[...] = dot_tn(second, d_upper).astype(BF16)
    down_grad_ref[...] = dot_tn(act, d_dense).astype(BF16)


def feed(near, far, g_near, g_far, up, down, got, count):
    half, length, width = near.shape
    hidden = up.shape[1]
    outs = (
        shaped(F32, half, length, width + 128),
        shaped(BF16, half, length, width // 2),
        shaped(BF16, half, length, width // 2 + 128),
        shaped(F32, half, length, width),
        shaped(BF16, half, length, width),
        shaped(BF16, width, hidden),
        shaped(BF16, hidden, width),
    )
    return pl.pallas_call(
        functools.partial(feed_kernel, count=count),
        out_shape=outs,
        compiler_params=params(56),
        cost_estimate=cost(),
        name="feed",
    )(near, far, g_near, g_far, up, down, got)


def halve_kernel(keep_ref, *refs, pieces):
    got_refs, own_ref, send_refs = refs[:pieces], refs[pieces], refs[pieces + 1 :]
    size = 16

    def step(i, carry):
        rows = pl.ds(pl.multiple_of(i * size, size), size)
        start = 0
        for got_ref in got_refs:
            part = slice(start, start + got_ref.shape[2])
            own_ref[rows, part] = keep_ref[0, rows, part] + got_ref[0, rows].astype(F32)
            for j, ref in enumerate(send_refs):
                total = keep_ref[j + 1, rows, part] + got_ref[j + 1, rows].astype(F32)
                ref[rows, part] = total.astype(BF16)
            start = part.stop
        return carry

    lax.fori_loop(0, own_ref.shape[0] // size, step, 0)


def halve(keep, got):
    half, length, width = keep.shape
    outs = (shaped(F32, length, width),) + (shaped(BF16, length, width),) * (half - 1)
    return pl.pallas_call(
        functools.partial(halve_kernel, pieces=len(got)),
        out_shape=outs,
        compiler_params=params(20),
        cost_estimate=cost(),
        name="halve",
    )(keep, *got)


def after_kernel(
    own_ref, r1_ref, r2_ref, r3_ref, back_ref, placing_ref, residual_ref, stats_ref, g_ref,
    small_ref, merge_ref, routes_ref, second_ref,
    result_ref, d_residual_ref, side_ref, d_ref, *, count,
):
    length, width = g_ref.shape
    part = width // TEAM
    small = small_ref[:, 3 * part :]
    gains = gain_rows(small, count)
    summed = (
        own_ref[...] + r1_ref[...].astype(F32) + r2_ref[...].astype(F32) + r3_ref[...].astype(F32)
    )
    d_second = summed[:, :width]
    d_mix_dense = jnp.sum(summed[:, width:], axis=1, keepdims=True)
    stats = stats_ref[...]
    lane = lanes(stats.shape)
    column = lambda i: jnp.sum(jnp.where(lane == i, stats, 0.0), axis=1, keepdims=True)
    mix_dense, mix_expert, gate = column(count), column(count + 1), column(count + 2)
    residual = residual_ref[...]
    g = g_ref[...].astype(F32)
    returned = dot(placing_ref[...], back_ref[:, :width])
    result_ref[...] = residual + mix_expert * gate * returned
    along = jnp.sum(g * returned, axis=1, keepdims=True)
    d_mix_expert = gate * along
    mean = mix_dense * d_mix_dense + mix_expert * d_mix_expert
    onehot = jnp.where(lane == routes_ref[...], 1.0, 0.0)
    side = jnp.where(lane < count, stats * (onehot - gate) * (mix_expert * along), 0.0)
    side += jnp.where(lane == count, mix_dense * (d_mix_dense - mean), 0.0)
    side += jnp.where(lane == count + 1, mix_expert * (d_mix_expert - mean), 0.0)
    side = side.astype(BF16)
    d_second += dot(placing_ref[...], back_ref[:, width:]) + dot_nt(side, small)
    unit, scale = normed(residual)
    d_residual = g + norm_back(d_second * gains[1:2], unit, scale)
    d_residual_ref[...] = d_residual
    d_merged = d_residual.astype(BF16)
    side_grad = dot_tn(second_ref[...], side)
    feed_row = jnp.sum(d_second * unit, axis=0, keepdims=True)
    feed_rows = jnp.where(sublanes((8, width)) == 0, feed_row, 0.0)
    side_ref[...] = side_grad + column_of(feed_rows, count + 2, side.shape[1])
    d_att = dot_nt(d_merged, merge_ref[...]).astype(BF16)
    for p in range(TEAM):
        d_ref[p, :length] = d_att[:, p * part : (p + 1) * part]
        d_ref[p, length:] = d_merged[:, p * part : (p + 1) * part]


def after(
    own, others, back, placing, residual, stats, cotangent, got, merge, routes, second, count
):
    length, width = cotangent.shape
    part = width // TEAM
    outs = (
        shaped(F32, length, width),
        shaped(F32, length, width),
        shaped(F32, width, got.shape[1] - 3 * part),
        shaped(BF16, TEAM, 2 * length, part),
    )
    return pl.pallas_call(
        functools.partial(after_kernel, count=count),
        out_shape=outs,
        compiler_params=params(56),
        cost_estimate=cost(),
        name="after",
    )(own, *others, back, placing, residual, stats, cotangent, got, merge, routes, second)


def last_kernel(
    own_ref, r1_ref, r2_ref, r3_ref, dense_ref, d1_ref, d2_ref, d3_ref, part_ref, stats_ref,
    x_ref, d_residual_ref, small_ref, out_ref, result_ref, *, count,
):
    part = x_ref.shape[1] // TEAM
    gains = gain_rows(small_ref[:, 3 * part :], count)
    size = 32

    def step(i, carry):
        rows = pl.ds(pl.multiple_of(i * size, size), size)
        add = lambda own, *others: own[rows] + sum(ref[rows].astype(F32) for ref in others)
        d_first = add(own_ref, r1_ref, r2_ref, r3_ref)
        unit, scale = normed(x_ref[rows].astype(F32))
        out_ref[rows] = (
            d_residual_ref[rows] + norm_back(d_first * gains[0:1], unit, scale)
        ).astype(BF16)
        stats = stats_ref[rows]
        picked = jnp.where(lanes(stats.shape) == count, stats, 0.0)
        mix_dense = jnp.sum(picked, axis=1, keepdims=True)
        dense = add(dense_ref, d1_ref, d2_ref, d3_ref)
        result_ref[rows] = (part_ref[rows] + mix_dense * dense).astype(BF16)
        return carry

    lax.fori_loop(0, x_ref.shape[0] // size, step, 0)


def last(own, others, dense, more, part, stats, tokens, d_residual, got, count):
    return pl.pallas_call(
        functools.partial(last_kernel, count=count),
        out_shape=(shaped(BF16, *tokens.shape),) * 2,
        compiler_params=params(16),
        cost_estimate=cost(),
        name="last",
    )(own, *others, dense, *more, part, stats, tokens, d_residual, got)


def owner_kernel(
    got_ref, up_got_ref, joint_ref, merge_ref, up_ref, attend_ref, feed_ref, router_ref, mix_ref,
    *, count,
):
    teams, _, rows, wide = got_ref.shape
    part = merge_ref.shape[1] // TEAM
    width = part * TEAM
    block = up_ref.shape[1] // (TEAM * teams)

    def step(p, total):
        own = got_ref[0, p].astype(F32)
        for g in range(1, teams):
            own += got_ref[g, p].astype(F32)
        for c in range(3):
            start = pl.multiple_of(c * width + p * part, part)
            joint_ref[:, pl.ds(start, part)] = own[:, c * part : (c + 1) * part]
        merge_ref[:, pl.ds(pl.multiple_of(p * part, part), part)] = own[:, wide - part :]
        return total + own[:, 3 * part : wide - part]

    total = lax.fori_loop(0, TEAM, step, jnp.zeros((rows, wide - 4 * part), F32))
    for p in range(TEAM):
        for g in range(teams):
            start = (g * TEAM + p) * block
            piece = up_got_ref[p, :, g * block : (g + 1) * block]
            up_ref[:, start : start + block] = piece.astype(F32)
    router_ref[...] = total[:, :count]
    same = sublanes((rows, rows)) == lanes((rows, rows))

    def row(lane):
        column = jnp.sum(jnp.where(lanes(total.shape) == lane, total, 0.0), axis=1, keepdims=True)
        return jnp.sum(jnp.where(same, column, 0.0), axis=0, keepdims=True)

    mix_ref[0:1] = row(count)
    mix_ref[1:2] = row(count + 1)
    feed_ref[...] = row(count + 2)
    attend_ref[...] = row(count + 3)


def owner_sums(got, up, width, hidden, count):
    rows = got.shape[2]
    outs = (
        shaped(F32, rows, 3 * width),
        shaped(F32, rows, width),
        shaped(F32, rows, hidden),
        shaped(F32, 1, rows),
        shaped(F32, 1, rows),
        shaped(F32, rows, count),
        shaped(F32, 2, rows),
    )
    return pl.pallas_call(
        functools.partial(owner_kernel, count=count),
        out_shape=outs,
        compiler_params=params(12),
        cost_estimate=cost(),
        name="owner_sums",
    )(got, up)


def order_kernel(place_ref, near_ref, far_ref, out_ref):
    teams, _, rows, _ = out_ref.shape

    def step(j, carry):
        for k, ref in enumerate((near_ref, far_ref)):
            for d in range(teams):
                team = (place_ref[1] + d) & (teams - 1)
                out_ref[team, place_ref[0] ^ (2 * j + k)] = ref[j, d * rows : (d + 1) * rows]
        return carry

    lax.fori_loop(0, TEAM // 2, step, 0)


def order(place, near, far, teams):
    _, tall, width = near.shape
    out = shaped(BF16, teams, TEAM, tall // teams, width)
    return pl.pallas_call(
        order_kernel,
        in_specs=[pl.BlockSpec(memory_space=pltpu.SMEM)]
        + [pl.BlockSpec(memory_space=pltpu.VMEM)] * 2,
        out_shape=out,
        compiler_params=params(56),
        cost_estimate=cost(),
        name="order",
    )(place, near, far)


def body(
    tokens,
    gain_attend,
    joint_weight,
    merge_weight,
    gain_feed,
    up_weight,
    down_weight,
    router_weight,
    mix_weight,
    widen_weight,
    narrow_weight,
    routes,
    segments,
    cotangent,
):
    count = lax.axis_size("expert")
    teams = count // TEAM
    place = (lax.axis_index("expert") & (TEAM - 1)).astype(jnp.int32)
    team = lax.axis_index("expert") >> 3
    place_arg = jnp.stack([place, team.astype(jnp.int32)])
    length, width = tokens.shape
    capacity = max(2, 2 * length // count)
    planes = [[g * TEAM + p for p in range(TEAM)] for g in range(teams)]
    lines = [[g * TEAM + p for g in range(teams)] for p in range(TEAM)]
    rows = joint_weight.shape[0]
    part = width // TEAM
    hidden = up_weight.shape[1]
    block = hidden // count

    def swap(value, mask):
        return lax.ppermute(value, "expert", [(i, i ^ mask) for i in range(count)])

    def exchange(value):
        return lax.all_to_all(value, "expert", 0, 0, tiled=True)

    def team_exchange(value):
        return lax.all_to_all(value, "expert", 0, 0, tiled=True, axis_index_groups=planes)

    def line_gather(value):
        return lax.all_gather(value, "expert", axis=0, tiled=True, axis_index_groups=lines)

    def line_scatter(value):
        return lax.psum_scatter(
            value, "expert", scatter_dimension=0, tiled=True, axis_index_groups=lines
        )

    def together(*values):
        return lax.optimization_barrier(values)

    def team_sends(value):
        return [value, swap(value, 2), swap(value, 4), swap(value, 6)]

    def team_joins(values):
        near = jnp.stack(values)
        return near, swap(near, 1)

    def team_scatter(keep, *sent):
        own, *sends = halve(keep, [swap(a, 1) for a in sent])
        return own, [swap(s, 2 * j + 2) for j, s in enumerate(sends)]

    small_width = -(-(count + 4) // 128) * 128
    pack_out = shaped(BF16, TEAM, rows, 3 * part + small_width + teams * block)
    pack = pl.pallas_call(
        functools.partial(pack_kernel, teams=teams),
        out_shape=pack_out,
        compiler_params=params(56),
        cost_estimate=cost(),
        name="pack",
    )(
        joint_weight,
        up_weight,
        router_weight,
        mix_weight.T,
        gain_attend[None],
        gain_feed[None],
    )
    pack, merge_weight = together(pack, merge_weight)
    pack = team_exchange(pack).reshape(TEAM * rows, -1)
    placing, g_rows = place_rows(routes, cotangent, count, capacity)
    from_team = lambda d: [
        ((g + d) % teams * TEAM + p, g * TEAM + p) for g in range(teams) for p in range(TEAM)
    ]
    merge_line = [merge_weight]
    merge_line += [lax.ppermute(merge_weight, "expert", from_team(d)) for d in range(1, teams)]
    pack, tokens, g_rows, *merge_line = together(pack, tokens, g_rows, *merge_line)
    joint_rows, g_rows = together(pack[:, : 3 * part + small_width], g_rows)
    g_rows = exchange(g_rows.reshape(count, capacity, width)).reshape(count * capacity, width)
    merge_line = jnp.concatenate(merge_line, axis=0)
    wide = 3 * part + small_width
    x_sent = jnp.concatenate(
        [
            tokens,
            jnp.pad(segments.astype(BF16), ((0, 15), (0, width - length))),
        ],
        axis=0,
    )
    got = line_gather(joint_rows)
    sends = team_sends(x_sent)
    xs = [jnp.stack(sends[:2]), jnp.stack(sends[2:])]
    *xs, pack, g_rows = together(*xs, pack, g_rows)
    xs = xs + [swap(x, 1) for x in xs]
    up_part = line_gather(pack[:, 3 * part + small_width :])
    merge_parts = team_sends(merge_line)

    joint, attended = attend(place_arg, xs, got, length, count)
    attended, *merge_parts = together(attended, *merge_parts)
    merge_near, merge_far = team_joins(merge_parts)
    arrived = team_exchange(attended)
    merge = order(place_arg, merge_near, merge_far, teams).reshape(width, width)
    residual, second, attended, stats, outgoing = middle(
        arrived, merge, tokens, got, routes, placing, count
    )
    received = exchange(outgoing.reshape(count, capacity, -1)).reshape(count * capacity, -1)
    s_near, attended, up_part = together(jnp.stack(team_sends(second)), attended, up_part)
    s_far = swap(s_near, 1)
    a_parts = team_sends(jnp.concatenate([attended, cotangent], axis=0))
    received, s_near, s_far, down_own = together(received, s_near, s_far, down_weight)
    down_part = line_gather(down_own)
    act, d_eupper, back, d_out = expert(received, g_rows, widen_weight, narrow_weight)
    back, s_near, up_part, *a_parts = together(back, s_near, up_part, *a_parts)
    g_near, g_far = team_joins([a[length:] for a in a_parts])
    a_parts = [a[:length] for a in a_parts]
    back = exchange(back.reshape(count, capacity, -1)).reshape(count * capacity, -1)
    keep, low, high, keep_dense, send_dense, up_grad, down_grad = feed(
        s_near, s_far, g_near, g_far, up_part, down_part, got, count
    )
    up_grad = line_scatter(up_grad)
    own, others = team_scatter(keep, low, high)
    own, send_dense, down_grad, d_eupper = together(own, send_dense, down_grad, d_eupper)
    down_grad = line_scatter(down_grad)
    widen_grad = widen_grads(received, d_eupper, width)
    back, widen_grad = together(back, widen_grad)
    a_near, a_far = team_joins(a_parts)
    dense, more = team_scatter(keep_dense, send_dense)
    result, d_residual, side, d_both = after(
        own, others, back, placing, residual, stats, cotangent, got, merge, routes, second, count
    )
    d_both, act = together(d_both, act)
    d_both = team_exchange(d_both)
    d_both, up_grad = together(d_both, up_grad)
    up_grad = team_exchange(up_grad.reshape(TEAM, rows, -1))
    keep, send, grads = attend_back(
        place_arg, xs, a_near, a_far, got, joint, d_both, side, count
    )
    grads, send, up_grad, down_grad, act, *more = together(
        grads, send, up_grad, down_grad, act, *more
    )
    grads = exchange(grads.reshape(count, rows, -1))
    own, others = team_scatter(keep, send)
    own, act = together(own, act)
    narrow_grad = narrow_grads(d_out, act)
    tokens_grad, result = last(
        own, others, dense, more, result, stats, tokens, d_residual, got, count
    )
    grads, tokens_grad, narrow_grad = together(grads, tokens_grad, narrow_grad)
    grads = grads.reshape(teams, TEAM, rows, -1)
    joint_grad, merge_grad, up_grad, attend_grad, feed_grad, router_grad, mix_grad = owner_sums(
        grads, up_grad, width, hidden, count
    )
    return (
        result,
        tokens_grad,
        attend_grad.reshape(rows),
        joint_grad,
        merge_grad,
        feed_grad.reshape(rows),
        up_grad,
        down_grad.astype(F32),
        router_grad,
        mix_grad.T,
        widen_grad,
        narrow_grad,
    )


def solution(mesh):
    one, two, three = P("expert"), P("expert", None), P("expert", None, None)
    return jax.shard_map(
        body,
        mesh=mesh,
        in_specs=(two, one, two, two, one, two, two, two, two, three, three, two, two, two),
        out_specs=(two, two, one, two, two, one, two, two, two, two, three, three),
        check_vma=False,
    )
```

```python
import functools
import math

import jax
import jax.numpy as jnp
from jax import lax
from jax.experimental import pallas as pl
from jax.experimental.pallas import tpu as pltpu
from jax.sharding import PartitionSpec as P

HEAD_DIM = 64
TEAM = 8
EPSILON = 1e-05
HIDDEN = -1e30
F32 = jnp.float32
BF16 = jnp.bfloat16
CURVE = math.sqrt(2.0 / math.pi)
MIB = 1 << 20


def dot(left, right):
    return jnp.dot(left, right, preferred_element_type=F32)


def dot_tn(left, right):
    return lax.dot_general(left, right, (((0,), (0,)), ((), ())), preferred_element_type=F32)


def dot_nt(left, right):
    return lax.dot_general(left, right, (((1,), (1,)), ((), ())), preferred_element_type=F32)


def gelu_both(u):
    square = u * u
    bent = jnp.tanh(u * (CURVE + (CURVE * 0.044715) * square))
    half = 0.5 + 0.5 * bent
    slope = half + u * (1.0 - bent * bent) * (0.5 * CURVE + (0.5 * CURVE * 0.134145) * square)
    return u * half, slope


def normed(values):
    mean = jnp.mean(values, axis=-1, keepdims=True)
    centered = values - mean
    spread = jnp.mean(centered * centered, axis=-1, keepdims=True)
    scale = lax.rsqrt(spread + EPSILON)
    return centered * scale, scale


def norm_back(dn, unit, scale):
    return scale * (
        dn
        - jnp.mean(dn, axis=-1, keepdims=True)
        - unit * jnp.mean(dn * unit, axis=-1, keepdims=True)
    )


def lanes(shape):
    return lax.broadcasted_iota(jnp.int32, shape, 1)


def sublanes(shape):
    return lax.broadcasted_iota(jnp.int32, shape, 0)


def gain_rows(small, count):
    shape = (8, small.shape[1])
    pick = (lanes(shape) == sublanes(shape) + count + 2) & (sublanes(shape) < 2)
    return dot_nt(jnp.where(pick, 1.0, 0.0).astype(BF16), small)


def column_of(rows, lane, width):
    shape = (rows.shape[0], width)
    pick = jnp.where((lanes(shape) == lane) & (sublanes(shape) == 0), 1.0, 0.0).astype(BF16)
    return dot_tn(rows.astype(BF16), pick)


def visible(segment_row, length):
    shape = (length, length)
    row, column = sublanes(shape), lanes(shape)
    segment = jnp.sum(jnp.where(row == column, segment_row, 0.0), axis=1, keepdims=True)
    return (row >= column) & (segment == segment_row)


def chance_of(query, keys, allowed):
    scores = dot_nt(query, keys) * (1.0 / math.sqrt(HEAD_DIM))
    scores = jnp.where(allowed, scores, HIDDEN)
    grown = jnp.exp(scores - jnp.max(scores, axis=1, keepdims=True))
    return grown * (1.0 / jnp.sum(grown, axis=1, keepdims=True))


def params(mib=56, **more):
    return pltpu.CompilerParams(vmem_limit_bytes=mib * MIB, **more)


def cost(flops=1):
    return pl.CostEstimate(flops=flops, bytes_accessed=1, transcendentals=0)


def shaped(dtype, *shape):
    return jax.ShapeDtypeStruct(shape, dtype)


def pack_kernel(
    joint_ref, up_ref, router_ref, mix_ref, gain_a_ref, gain_f_ref, pack_ref, *, teams
):
    rows = joint_ref.shape[0]
    width = joint_ref.shape[1] // 3
    part = width // TEAM
    block = up_ref.shape[1] // (teams * TEAM)
    count = router_ref.shape[1]
    wide = pack_ref.shape[2] - teams * block
    shape = (rows, wide - 3 * part)
    spread = (count, shape[1])
    spread = jnp.where(lanes(spread) == sublanes(spread), 1.0, 0.0).astype(BF16)
    small = dot(router_ref[...], spread)
    lane = lanes(shape)
    square = (rows, rows)
    same = sublanes(square) == lanes(square)
    columns = [mix_ref[0:1], mix_ref[1:2], gain_a_ref[...], gain_f_ref[...]]
    for i, row in enumerate(columns):
        column = jnp.sum(jnp.where(same, row.astype(F32), 0.0), axis=1, keepdims=True)
        small += jnp.where(lane == count + i, column, 0.0)
    small = small.astype(BF16)
    for p in range(TEAM):
        pieces = [joint_ref[:, c * width + p * part : c * width + (p + 1) * part] for c in range(3)]
        for g in range(teams):
            start = (g * TEAM + p) * block
            pieces.append(up_ref[:, start : start + block])
        pack_ref[p] = jnp.concatenate(pieces[:3] + [small] + pieces[3:], axis=1)


def attend_kernel(place_ref, n0_ref, n1_ref, f0_ref, f1_ref, got_ref, joint_ref, out_ref, *, count):
    _, length, part = out_ref.shape
    members = [ref.at[i] for ref in (n0_ref, n1_ref, f0_ref, f1_ref) for i in range(2)]
    gains = gain_rows(got_ref[:, 3 * part :], count)
    lane = lanes((length, part))
    for j in range(TEAM // 2):
        pair = (members[j], members[j + TEAM // 2])
        x = jnp.concatenate([ref[:length] for ref in pair], axis=0).astype(F32)
        unit, _ = normed(x)
        first = (unit * gains[0:1]).astype(BF16)
        joint = dot(first, got_ref[:, : 3 * part]).astype(BF16)
        for k, ref in enumerate(pair):
            allowed = visible(ref[length:, :length].astype(F32)[0:1], length)
            own = joint[k * length : (k + 1) * length]
            query, keys, values = own[:, :part], own[:, part : 2 * part], own[:, 2 * part :]
            total = jnp.zeros((length, part), F32)
            for h in range(part // HEAD_DIM):
                mine = lane // HEAD_DIM == h
                chance = chance_of(jnp.where(mine, query, 0), keys, allowed)
                total += dot(chance.astype(BF16), jnp.where(mine, values, 0))
            member = place_ref[0] ^ (2 * j + k)
            joint_ref[member] = own
            out_ref[member] = total.astype(BF16)


def attend(place, xs, got, length, count):
    part = xs[0].shape[2] // TEAM
    return pl.pallas_call(
        functools.partial(attend_kernel, count=count),
        in_specs=[pl.BlockSpec(memory_space=pltpu.SMEM)]
        + [pl.BlockSpec(memory_space=pltpu.VMEM)] * 5,
        out_shape=(shaped(BF16, TEAM, length, 3 * part), shaped(BF16, TEAM, length, part)),
        compiler_params=params(56),
        cost_estimate=cost(),
        name="attend",
    )(place, *xs, got)


def attend_back_kernel(
    place_ref, n0_ref, n1_ref, f0_ref, f1_ref, near_att, far_att, got_ref, joint_ref, d_ref, side_ref,
    keep_ref, send_ref, grad_ref, d_joint_ref, first_ref, unit_ref, d_merged_ref, *, count,
):
    _, length, wide = joint_ref.shape
    part = wide // 3
    half, _, width = near_att.shape
    shrink = 1.0 / math.sqrt(HEAD_DIM)
    gains = gain_rows(got_ref[:, 3 * part :], count)
    lane = lanes((length, part))

    def step(i, carry, start, k, ref):
        j = start + i
        rows = pl.ds(pl.multiple_of((k * half + j) * length, length), length)
        x = ref[i]
        unit, _ = normed(x[:length].astype(F32))
        unit_ref[rows] = unit
        first_ref[rows] = (unit * gains[0:1]).astype(BF16)
        allowed = visible(x[length:, :length].astype(F32)[0:1], length)
        member = place_ref[0] ^ (2 * j + k)
        own = joint_ref[member]
        both = d_ref[member]
        d_own = both[:length]
        d_merged_ref[rows] = both[length:]
        query, keys, values = own[:, :part], own[:, part : 2 * part], own[:, 2 * part :]
        d_query = jnp.zeros((length, part), F32)
        d_keys = jnp.zeros((length, part), F32)
        d_values = jnp.zeros((length, part), F32)
        for h in range(part // HEAD_DIM):
            mine = lane // HEAD_DIM == h
            q = jnp.where(mine, query, 0)
            d_head = jnp.where(mine, d_own, 0)
            chance = chance_of(q, keys, allowed)
            d_weights = dot_nt(d_head, values)
            inner = jnp.sum(chance * d_weights, axis=1, keepdims=True)
            d_scores = (chance * (d_weights - inner)).astype(BF16)
            d_query += dot(d_scores, jnp.where(mine, keys, 0))
            d_keys += dot_tn(d_scores, q)
            d_values += dot_tn(chance.astype(BF16), d_head)
        d_joint_ref[rows, :part] = (d_query * shrink).astype(BF16)
        d_joint_ref[rows, part : 2 * part] = (d_keys * shrink).astype(BF16)
        d_joint_ref[rows, 2 * part :] = d_values.astype(BF16)
        return carry

    for k, pair in enumerate(((n0_ref, n1_ref), (f0_ref, f1_ref))):
        for a, ref in enumerate(pair):
            lax.fori_loop(0, 2, functools.partial(step, start=2 * a, k=k, ref=ref), 0)
    d_joint = d_joint_ref[...]
    d_first = dot_nt(d_joint, got_ref[:, : 3 * part])
    tall = half * length
    keep_ref[...] = d_first[:tall].reshape(keep_ref.shape)
    send_ref[...] = d_first[tall:].astype(BF16).reshape(send_ref.shape)
    gain = jnp.sum(d_first * unit_ref[...], axis=0, keepdims=True)
    gain = jnp.where(sublanes((8, width)) == 0, gain, 0.0)
    grad_ref[:, : 3 * part] = dot_tn(first_ref[...], d_joint).astype(BF16)
    side = side_ref[...] + column_of(gain, count + 3, side_ref.shape[1])
    grad_ref[:, 3 * part : -part] = side.astype(BF16)
    d_merged = d_merged_ref[...]
    merged = dot_tn(near_att[...].reshape(tall, width), d_merged[:tall])
    merged += dot_tn(far_att[...].reshape(tall, width), d_merged[tall:])
    grad_ref[:, -part:] = merged.astype(BF16)


def attend_back(place, xs, near_att, far_att, got, joint, d_both, side, count):
    half, length, width = near_att.shape
    part = width // TEAM
    tall = TEAM * length
    outs = (
        shaped(F32, half, length, width),
        shaped(BF16, half, length, width),
        shaped(BF16, width, 4 * part + side.shape[1]),
    )
    return pl.pallas_call(
        functools.partial(attend_back_kernel, count=count),
        in_specs=[pl.BlockSpec(memory_space=pltpu.SMEM)]
        + [pl.BlockSpec(memory_space=pltpu.VMEM)] * 10,
        out_shape=outs,
        scratch_shapes=[
            pltpu.VMEM((tall, 3 * part), BF16),
            pltpu.VMEM((tall, width), BF16),
            pltpu.VMEM((tall, width), F32),
            pltpu.VMEM((tall, part), BF16),
        ],
        compiler_params=params(56),
        cost_estimate=cost(int(2e10)),
        name="attend_back",
    )(place, *xs, near_att, far_att, got, joint, d_both, side)


def middle_kernel(
    att_ref, merge_ref, x_ref, small_ref, routes_ref, placing_ref,
    residual_ref, second_ref, attended_ref, stats_ref, out_ref, *, count,
):
    length, width = x_ref.shape
    small = small_ref[:, 3 * width // TEAM :]
    gains = gain_rows(small, count)
    attended = jnp.concatenate([att_ref[p] for p in range(TEAM)], axis=1)
    residual = x_ref[...].astype(F32) + dot(attended, merge_ref[...])
    residual_ref[...] = residual
    unit, _ = normed(residual)
    second = (unit * gains[1:2]).astype(BF16)
    second_ref[...] = second
    attended_ref[...] = attended
    logits = dot(second, small)
    lane = lanes(logits.shape)
    routed = jnp.where(lane < count, logits, HIDDEN)
    grown = jnp.exp(routed - jnp.max(routed, axis=1, keepdims=True))
    chances = grown * (1.0 / jnp.sum(grown, axis=1, keepdims=True))
    mixed = jnp.where((lane >= count) & (lane < count + 2), logits, HIDDEN)
    grown = jnp.exp(mixed - jnp.max(mixed, axis=1, keepdims=True))
    mix = grown * (1.0 / jnp.sum(grown, axis=1, keepdims=True))
    routes = routes_ref[...]
    onehot = lane == routes
    gate = jnp.sum(jnp.where(onehot, chances, 0.0), axis=1, keepdims=True)
    mix_expert = jnp.sum(jnp.where(lane == count + 1, mix, 0.0), axis=1, keepdims=True)
    stats_ref[...] = chances + mix + jnp.where(lane == count + 2, gate, 0.0)
    scale = mix_expert * gate
    high = scale.astype(BF16).astype(F32)
    middle_part = (scale - high).astype(BF16).astype(F32)
    low = scale - high - middle_part
    spread = (length, out_ref.shape[1] - width)
    lane = lanes(spread)
    scales = jnp.where(lane == 0, high, 0.0) + jnp.where(lane == 1, middle_part, 0.0)
    scales += jnp.where(lane == 2, low, 0.0)
    placing = placing_ref[...]
    out_ref[:, :width] = dot_tn(placing, second).astype(BF16)
    out_ref[:, width:] = dot_tn(placing, scales.astype(BF16)).astype(BF16)


def place_kernel(routes_ref, g_ref, placing_ref, out_ref, *, count, capacity):
    length = g_ref.shape[0]
    routes = routes_ref[...]
    onehot = jnp.where(lanes((length, -(-count // 128) * 128)) == routes, 1.0, 0.0)
    shape = (length, length)
    before = jnp.where(sublanes(shape) > lanes(shape), 1.0, 0.0).astype(BF16)
    rank = jnp.sum(onehot * dot(before, onehot.astype(BF16)), axis=1, keepdims=True)
    slot = routes * capacity + rank.astype(jnp.int32)
    placing = jnp.where(lanes((length, count * capacity)) == slot, 1.0, 0.0).astype(BF16)
    placing_ref[...] = placing
    out_ref[...] = dot_tn(placing, g_ref[...]).astype(BF16)


def place_rows(routes, cotangent, count, capacity):
    length, width = cotangent.shape
    return pl.pallas_call(
        functools.partial(place_kernel, count=count, capacity=capacity),
        out_shape=(
            shaped(BF16, length, count * capacity),
            shaped(BF16, count * capacity, width),
        ),
        compiler_params=params(56),
        cost_estimate=cost(),
        name="place_rows",
    )(routes, cotangent)


def middle(att, merge, tokens, got, routes, placing, count):
    length, width = tokens.shape
    lanes_small = got.shape[1] - 3 * width // TEAM
    outs = (
        shaped(F32, length, width),
        shaped(BF16, length, width),
        shaped(BF16, length, width),
        shaped(F32, length, lanes_small),
        shaped(BF16, placing.shape[1], width + 128),
    )
    return pl.pallas_call(
        functools.partial(middle_kernel, count=count),
        out_shape=outs,
        compiler_params=params(56),
        cost_estimate=cost(),
        name="middle",
    )(att, merge, tokens, got, routes, placing)


def expert_kernel(
    rows_ref, g_ref, widen_hbm, narrow_hbm, act_hbm, d_hbm, back_ref, d_out_ref,
    widen_ref, narrow_ref, act_ref, d_ref, in_sems, out_sems, *, chunk,
):
    width, hidden = widen_ref.shape
    copies = []
    for i in range(hidden // chunk):
        part = pl.ds(i * chunk, chunk)
        wide = (widen_hbm.at[0, :, part], widen_ref.at[:, part], in_sems.at[2 * i])
        tall = (narrow_hbm.at[0, part, :], narrow_ref.at[part, :], in_sems.at[2 * i + 1])
        copies.append([pltpu.make_async_copy(*wide), pltpu.make_async_copy(*tall)])
    for pair in copies:
        for copy in pair:
            copy.start()
    scale = jnp.sum(rows_ref[:, width:].astype(F32), axis=1, keepdims=True)
    d_out_ref[...] = (g_ref[...].astype(F32) * scale).astype(BF16)

    def step(i, carry):
        part = pl.ds(pl.multiple_of(i * chunk, chunk), chunk)
        wide = (widen_hbm.at[0, :, part], widen_ref.at[:, part], in_sems.at[2 * i])
        tall = (narrow_hbm.at[0, part, :], narrow_ref.at[part, :], in_sems.at[2 * i + 1])
        pltpu.make_async_copy(*wide).wait()
        pltpu.make_async_copy(*tall).wait()
        upper = dot(rows_ref[:, :width], widen_ref[:, part])
        d_act = dot_nt(d_out_ref[...], narrow_ref[part])
        act, slope = gelu_both(upper)
        act_ref[:, part] = act.astype(BF16)
        d_ref[:, part] = (slope * d_act).astype(BF16)
        return carry

    lax.fori_loop(0, hidden // chunk, step, 0)
    outs = [
        pltpu.make_async_copy(act_ref, act_hbm, out_sems.at[0]),
        pltpu.make_async_copy(d_ref, d_hbm, out_sems.at[1]),
    ]
    for copy in outs:
        copy.start()
    half = width // 4

    def finish(i, carry):
        here, there = [pl.ds(pl.multiple_of(j, half), half) for j in (i * half, width + i * half)]
        back_ref[:, here] = dot(act_ref[...], narrow_ref[:, here]).astype(BF16)
        back_ref[:, there] = dot_nt(d_ref[...], widen_ref[here]).astype(BF16)
        return carry

    lax.fori_loop(0, 4, finish, 0)
    for copy in outs:
        copy.wait()


def expert(rows, g_rows, widen, narrow, chunk=512):
    slots, width = g_rows.shape
    hidden = widen.shape[2]
    left = pl.BlockSpec(memory_space=pl.ANY)
    here = pl.BlockSpec(memory_space=pltpu.VMEM)
    return pl.pallas_call(
        functools.partial(expert_kernel, chunk=chunk),
        in_specs=[here, here, left, left],
        out_specs=[left, left, here, here],
        out_shape=(
            shaped(BF16, slots, hidden),
            shaped(BF16, slots, hidden),
            shaped(BF16, slots, 2 * width),
            shaped(BF16, slots, width),
        ),
        scratch_shapes=[
            pltpu.VMEM((width, hidden), BF16),
            pltpu.VMEM((hidden, width), BF16),
            pltpu.VMEM((slots, hidden), BF16),
            pltpu.VMEM((slots, hidden), BF16),
            pltpu.SemaphoreType.DMA((2 * (hidden // chunk),)),
            pltpu.SemaphoreType.DMA((2,)),
        ],
        compiler_params=params(56),
        cost_estimate=cost(),
        name="expert",
    )(rows, g_rows, widen, narrow)


def narrow_grad_kernel(rows_ref, act_ref, out_ref):
    out_ref[0] = dot_tn(act_ref[...], rows_ref[...])


def narrow_grads(rows, act, chunk=512):
    slots, width = rows.shape
    hidden = act.shape[1]
    return pl.pallas_call(
        narrow_grad_kernel,
        grid=(hidden // chunk,),
        in_specs=[
            pl.BlockSpec((slots, width), lambda f: (0, 0)),
            pl.BlockSpec((slots, chunk), lambda f: (0, f)),
        ],
        out_specs=pl.BlockSpec((1, chunk, width), lambda f: (0, f, 0)),
        out_shape=shaped(F32, 1, hidden, width),
        compiler_params=params(56),
        cost_estimate=cost(),
        name="narrow_grads",
    )(rows, act)


def widen_grad_kernel(rows_ref, d_ref, out_ref):
    out_ref[0] = dot_tn(rows_ref[...], d_ref[...])


def widen_grads(rows, d_upper, width, chunk=128):
    slots = rows.shape[0]
    hidden = d_upper.shape[1]
    return pl.pallas_call(
        widen_grad_kernel,
        grid=(width // chunk,),
        in_specs=[
            pl.BlockSpec((slots, chunk), lambda f: (0, f)),
            pl.BlockSpec((slots, hidden), lambda f: (0, 0)),
        ],
        out_specs=pl.BlockSpec((1, chunk, hidden), lambda f: (0, f, 0)),
        out_shape=shaped(F32, 1, width, hidden),
        compiler_params=params(56),
        cost_estimate=cost(),
        name="widen_grads",
    )(rows, d_upper)


def feed_kernel(
    near_ref, far_ref, g_near_ref, g_far_ref, up_ref, down_ref, small_ref,
    keep_ref, low_ref, high_ref, keep_dense_ref, send_dense_ref, up_grad_ref, down_grad_ref,
    *, count,
):
    half, length, width = near_ref.shape
    tall = half * length
    near, far = near_ref[...].reshape(tall, width), far_ref[...].reshape(tall, width)
    second = jnp.concatenate([near, far], axis=0)
    g = jnp.concatenate(
        [g_near_ref[...].reshape(tall, width), g_far_ref[...].reshape(tall, width)], axis=0
    ).astype(F32)
    logits = dot(second, small_ref[:, 3 * width // TEAM :])
    lane = lanes(logits.shape)
    mixed = jnp.where((lane >= count) & (lane < count + 2), logits, HIDDEN)
    grown = jnp.exp(mixed - jnp.max(mixed, axis=1, keepdims=True))
    mix = jnp.sum(jnp.where(lane == count, grown, 0.0), axis=1, keepdims=True)
    mix = mix * (1.0 / jnp.sum(grown, axis=1, keepdims=True))
    d_dense = (g * mix).astype(BF16)
    act, slope = gelu_both(dot(second, up_ref[...]))
    act = act.astype(BF16)
    d_upper = (slope * dot_nt(d_dense, down_ref[...])).astype(BF16)
    d_second = dot_nt(d_upper, up_ref[...])
    dense = dot(act, down_ref[...])
    along = jnp.sum(g * dense, axis=1, keepdims=True)
    rest = along - along.astype(BF16).astype(F32)
    lane = lanes((2 * tall, 128))
    along = jnp.where(lane == 0, along, 0.0) + jnp.where(lane == 1, rest, 0.0)
    keep_ref[:, :, :width] = d_second[:tall].reshape(half, length, width)
    keep_ref[:, :, width:] = along[:tall].reshape(half, length, 128)
    sent = d_second[tall:].astype(BF16).reshape(half, length, width)
    low_ref[...] = sent[:, :, : width // 2]
    high_ref[:, :, : width // 2] = sent[:, :, width // 2 :]
    high_ref[:, :, width // 2 :] = along[tall:].astype(BF16).reshape(half, length, 128)
    keep_dense_ref[...] = dense[:tall].reshape(half, length, width)
    send_dense_ref[...] = dense[tall:].astype(BF16).reshape(half, length, width)
    up_grad_ref[...] = dot_tn(second, d_upper).astype(BF16)
    down_grad_ref[...] = dot_tn(act, d_dense).astype(BF16)


def feed(near, far, g_near, g_far, up, down, got, count):
    half, length, width = near.shape
    hidden = up.shape[1]
    outs = (
        shaped(F32, half, length, width + 128),
        shaped(BF16, half, length, width // 2),
        shaped(BF16, half, length, width // 2 + 128),
        shaped(F32, half, length, width),
        shaped(BF16, half, length, width),
        shaped(BF16, width, hidden),
        shaped(BF16, hidden, width),
    )
    return pl.pallas_call(
        functools.partial(feed_kernel, count=count),
        out_shape=outs,
        compiler_params=params(56),
        cost_estimate=cost(),
        name="feed",
    )(near, far, g_near, g_far, up, down, got)


def halve_kernel(keep_ref, *refs, pieces):
    got_refs, own_ref, send_refs = refs[:pieces], refs[pieces], refs[pieces + 1 :]
    size = 16

    def step(i, carry):
        rows = pl.ds(pl.multiple_of(i * size, size), size)
        start = 0
        for got_ref in got_refs:
            part = slice(start, start + got_ref.shape[2])
            own_ref[rows, part] = keep_ref[0, rows, part] + got_ref[0, rows].astype(F32)
            for j, ref in enumerate(send_refs):
                total = keep_ref[j + 1, rows, part] + got_ref[j + 1, rows].astype(F32)
                ref[rows, part] = total.astype(BF16)
            start = part.stop
        return carry

    lax.fori_loop(0, own_ref.shape[0] // size, step, 0)


def halve(keep, got):
    half, length, width = keep.shape
    outs = (shaped(F32, length, width),) + (shaped(BF16, length, width),) * (half - 1)
    return pl.pallas_call(
        functools.partial(halve_kernel, pieces=len(got)),
        out_shape=outs,
        compiler_params=params(20),
        cost_estimate=cost(),
        name="halve",
    )(keep, *got)


def after_kernel(
    own_ref, r1_ref, r2_ref, r3_ref, back_ref, placing_ref, residual_ref, stats_ref, g_ref,
    small_ref, merge_ref, routes_ref, second_ref,
    result_ref, d_residual_ref, side_ref, d_ref, *, count,
):
    length, width = g_ref.shape
    part = width // TEAM
    small = small_ref[:, 3 * part :]
    gains = gain_rows(small, count)
    summed = (
        own_ref[...] + r1_ref[...].astype(F32) + r2_ref[...].astype(F32) + r3_ref[...].astype(F32)
    )
    d_second = summed[:, :width]
    d_mix_dense = jnp.sum(summed[:, width:], axis=1, keepdims=True)
    stats = stats_ref[...]
    lane = lanes(stats.shape)
    column = lambda i: jnp.sum(jnp.where(lane == i, stats, 0.0), axis=1, keepdims=True)
    mix_dense, mix_expert, gate = column(count), column(count + 1), column(count + 2)
    residual = residual_ref[...]
    g = g_ref[...].astype(F32)
    returned = dot(placing_ref[...], back_ref[:, :width])
    result_ref[...] = residual + mix_expert * gate * returned
    along = jnp.sum(g * returned, axis=1, keepdims=True)
    d_mix_expert = gate * along
    mean = mix_dense * d_mix_dense + mix_expert * d_mix_expert
    onehot = jnp.where(lane == routes_ref[...], 1.0, 0.0)
    side = jnp.where(lane < count, stats * (onehot - gate) * (mix_expert * along), 0.0)
    side += jnp.where(lane == count, mix_dense * (d_mix_dense - mean), 0.0)
    side += jnp.where(lane == count + 1, mix_expert * (d_mix_expert - mean), 0.0)
    side = side.astype(BF16)
    d_second += dot(placing_ref[...], back_ref[:, width:]) + dot_nt(side, small)
    unit, scale = normed(residual)
    d_residual = g + norm_back(d_second * gains[1:2], unit, scale)
    d_residual_ref[...] = d_residual
    d_merged = d_residual.astype(BF16)
    side_grad = dot_tn(second_ref[...], side)
    feed_row = jnp.sum(d_second * unit, axis=0, keepdims=True)
    feed_rows = jnp.where(sublanes((8, width)) == 0, feed_row, 0.0)
    side_ref[...] = side_grad + column_of(feed_rows, count + 2, side.shape[1])
    d_att = dot_nt(d_merged, merge_ref[...]).astype(BF16)
    for p in range(TEAM):
        d_ref[p, :length] = d_att[:, p * part : (p + 1) * part]
        d_ref[p, length:] = d_merged[:, p * part : (p + 1) * part]


def after(
    own, others, back, placing, residual, stats, cotangent, got, merge, routes, second, count
):
    length, width = cotangent.shape
    part = width // TEAM
    outs = (
        shaped(F32, length, width),
        shaped(F32, length, width),
        shaped(F32, width, got.shape[1] - 3 * part),
        shaped(BF16, TEAM, 2 * length, part),
    )
    return pl.pallas_call(
        functools.partial(after_kernel, count=count),
        out_shape=outs,
        compiler_params=params(56),
        cost_estimate=cost(),
        name="after",
    )(own, *others, back, placing, residual, stats, cotangent, got, merge, routes, second)


def last_kernel(
    own_ref, r1_ref, r2_ref, r3_ref, dense_ref, d1_ref, d2_ref, d3_ref, part_ref, stats_ref,
    x_ref, d_residual_ref, small_ref, out_ref, result_ref, *, count,
):
    part = x_ref.shape[1] // TEAM
    gains = gain_rows(small_ref[:, 3 * part :], count)
    size = 32

    def step(i, carry):
        rows = pl.ds(pl.multiple_of(i * size, size), size)
        add = lambda own, *others: own[rows] + sum(ref[rows].astype(F32) for ref in others)
        d_first = add(own_ref, r1_ref, r2_ref, r3_ref)
        unit, scale = normed(x_ref[rows].astype(F32))
        out_ref[rows] = (
            d_residual_ref[rows] + norm_back(d_first * gains[0:1], unit, scale)
        ).astype(BF16)
        stats = stats_ref[rows]
        picked = jnp.where(lanes(stats.shape) == count, stats, 0.0)
        mix_dense = jnp.sum(picked, axis=1, keepdims=True)
        dense = add(dense_ref, d1_ref, d2_ref, d3_ref)
        result_ref[rows] = (part_ref[rows] + mix_dense * dense).astype(BF16)
        return carry

    lax.fori_loop(0, x_ref.shape[0] // size, step, 0)


def last(own, others, dense, more, part, stats, tokens, d_residual, got, count):
    return pl.pallas_call(
        functools.partial(last_kernel, count=count),
        out_shape=(shaped(BF16, *tokens.shape),) * 2,
        compiler_params=params(16),
        cost_estimate=cost(),
        name="last",
    )(own, *others, dense, *more, part, stats, tokens, d_residual, got)


def owner_kernel(
    got_ref, up_got_ref, joint_ref, merge_ref, up_ref, attend_ref, feed_ref, router_ref, mix_ref,
    *, count,
):
    teams, _, rows, wide = got_ref.shape
    part = merge_ref.shape[1] // TEAM
    width = part * TEAM
    block = up_ref.shape[1] // (TEAM * teams)

    def step(p, total):
        own = got_ref[0, p].astype(F32)
        for g in range(1, teams):
            own += got_ref[g, p].astype(F32)
        for c in range(3):
            start = pl.multiple_of(c * width + p * part, part)
            joint_ref[:, pl.ds(start, part)] = own[:, c * part : (c + 1) * part]
        merge_ref[:, pl.ds(pl.multiple_of(p * part, part), part)] = own[:, wide - part :]
        return total + own[:, 3 * part : wide - part]

    total = lax.fori_loop(0, TEAM, step, jnp.zeros((rows, wide - 4 * part), F32))
    for p in range(TEAM):
        for g in range(teams):
            start = (g * TEAM + p) * block
            piece = up_got_ref[p, :, g * block : (g + 1) * block]
            up_ref[:, start : start + block] = piece.astype(F32)
    router_ref[...] = total[:, :count]
    same = sublanes((rows, rows)) == lanes((rows, rows))

    def row(lane):
        column = jnp.sum(jnp.where(lanes(total.shape) == lane, total, 0.0), axis=1, keepdims=True)
        return jnp.sum(jnp.where(same, column, 0.0), axis=0, keepdims=True)

    mix_ref[0:1] = row(count)
    mix_ref[1:2] = row(count + 1)
    feed_ref[...] = row(count + 2)
    attend_ref[...] = row(count + 3)


def owner_sums(got, up, width, hidden, count):
    rows = got.shape[2]
    outs = (
        shaped(F32, rows, 3 * width),
        shaped(F32, rows, width),
        shaped(F32, rows, hidden),
        shaped(F32, 1, rows),
        shaped(F32, 1, rows),
        shaped(F32, rows, count),
        shaped(F32, 2, rows),
    )
    return pl.pallas_call(
        functools.partial(owner_kernel, count=count),
        out_shape=outs,
        compiler_params=params(12),
        cost_estimate=cost(),
        name="owner_sums",
    )(got, up)


def order_kernel(place_ref, near_ref, far_ref, out_ref):
    teams, _, rows, _ = out_ref.shape

    def step(j, carry):
        for k, ref in enumerate((near_ref, far_ref)):
            for d in range(teams):
                team = (place_ref[1] + d) & (teams - 1)
                out_ref[team, place_ref[0] ^ (2 * j + k)] = ref[j, d * rows : (d + 1) * rows]
        return carry

    lax.fori_loop(0, TEAM // 2, step, 0)


def order(place, near, far, teams):
    _, tall, width = near.shape
    out = shaped(BF16, teams, TEAM, tall // teams, width)
    return pl.pallas_call(
        order_kernel,
        in_specs=[pl.BlockSpec(memory_space=pltpu.SMEM)]
        + [pl.BlockSpec(memory_space=pltpu.VMEM)] * 2,
        out_shape=out,
        compiler_params=params(56),
        cost_estimate=cost(),
        name="order",
    )(place, near, far)


def body(
    tokens,
    gain_attend,
    joint_weight,
    merge_weight,
    gain_feed,
    up_weight,
    down_weight,
    router_weight,
    mix_weight,
    widen_weight,
    narrow_weight,
    routes,
    segments,
    cotangent,
):
    count = lax.axis_size("expert")
    teams = count // TEAM
    place = (lax.axis_index("expert") & (TEAM - 1)).astype(jnp.int32)
    team = lax.axis_index("expert") >> 3
    place_arg = jnp.stack([place, team.astype(jnp.int32)])
    length, width = tokens.shape
    capacity = max(2, 2 * length // count)
    planes = [[g * TEAM + p for p in range(TEAM)] for g in range(teams)]
    lines = [[g * TEAM + p for g in range(teams)] for p in range(TEAM)]
    rows = joint_weight.shape[0]
    part = width // TEAM
    hidden = up_weight.shape[1]
    block = hidden // count

    def swap(value, mask):
        return lax.ppermute(value, "expert", [(i, i ^ mask) for i in range(count)])

    def exchange(value):
        return lax.all_to_all(value, "expert", 0, 0, tiled=True)

    def team_exchange(value):
        return lax.all_to_all(value, "expert", 0, 0, tiled=True, axis_index_groups=planes)

    def line_gather(value):
        return lax.all_gather(value, "expert", axis=0, tiled=True, axis_index_groups=lines)

    def line_scatter(value):
        return lax.psum_scatter(
            value, "expert", scatter_dimension=0, tiled=True, axis_index_groups=lines
        )

    def together(*values):
        return lax.optimization_barrier(values)

    def team_sends(value):
        return [value, swap(value, 2), swap(value, 4), swap(value, 6)]

    def team_joins(values):
        near = jnp.stack(values)
        return near, swap(near, 1)

    def team_scatter(keep, *sent):
        own, *sends = halve(keep, [swap(a, 1) for a in sent])
        return own, [swap(s, 2 * j + 2) for j, s in enumerate(sends)]

    small_width = -(-(count + 4) // 128) * 128
    pack_out = shaped(BF16, TEAM, rows, 3 * part + small_width + teams * block)
    pack = pl.pallas_call(
        functools.partial(pack_kernel, teams=teams),
        out_shape=pack_out,
        compiler_params=params(56),
        cost_estimate=cost(),
        name="pack",
    )(
        joint_weight,
        up_weight,
        router_weight,
        mix_weight.T,
        gain_attend[None],
        gain_feed[None],
    )
    pack, merge_weight = together(pack, merge_weight)
    pack = team_exchange(pack).reshape(TEAM * rows, -1)
    placing, g_rows = place_rows(routes, cotangent, count, capacity)
    from_team = lambda d: [
        ((g + d) % teams * TEAM + p, g * TEAM + p) for g in range(teams) for p in range(TEAM)
    ]
    merge_line = [merge_weight]
    merge_line += [lax.ppermute(merge_weight, "expert", from_team(d)) for d in range(1, teams)]
    pack, tokens, g_rows, *merge_line = together(pack, tokens, g_rows, *merge_line)
    joint_rows, g_rows = together(pack[:, : 3 * part + small_width], g_rows)
    g_rows = exchange(g_rows.reshape(count, capacity, width)).reshape(count * capacity, width)
    merge_line = jnp.concatenate(merge_line, axis=0)
    wide = 3 * part + small_width
    x_sent = jnp.concatenate(
        [
            tokens,
            jnp.pad(segments.astype(BF16), ((0, 15), (0, width - length))),
        ],
        axis=0,
    )
    got = line_gather(joint_rows)
    sends = team_sends(x_sent)
    xs = [jnp.stack(sends[:2]), jnp.stack(sends[2:])]
    *xs, pack, g_rows = together(*xs, pack, g_rows)
    xs = xs + [swap(x, 1) for x in xs]
    up_part = line_gather(pack[:, 3 * part + small_width :])
    merge_parts = team_sends(merge_line)

    joint, attended = attend(place_arg, xs, got, length, count)
    attended, *merge_parts = together(attended, *merge_parts)
    merge_near, merge_far = team_joins(merge_parts)
    arrived = team_exchange(attended)
    merge = order(place_arg, merge_near, merge_far, teams).reshape(width, width)
    residual, second, attended, stats, outgoing = middle(
        arrived, merge, tokens, got, routes, placing, count
    )
    received = exchange(outgoing.reshape(count, capacity, -1)).reshape(count * capacity, -1)
    s_near, attended, up_part = together(jnp.stack(team_sends(second)), attended, up_part)
    s_far = swap(s_near, 1)
    a_parts = team_sends(jnp.concatenate([attended, cotangent], axis=0))
    received, s_near, s_far, down_own = together(received, s_near, s_far, down_weight)
    down_part = line_gather(down_own)
    act, d_eupper, back, d_out = expert(received, g_rows, widen_weight, narrow_weight)
    back, s_near, up_part, *a_parts = together(back, s_near, up_part, *a_parts)
    g_near, g_far = team_joins([a[length:] for a in a_parts])
    a_parts = [a[:length] for a in a_parts]
    back = exchange(back.reshape(count, capacity, -1)).reshape(count * capacity, -1)
    keep, low, high, keep_dense, send_dense, up_grad, down_grad = feed(
        s_near, s_far, g_near, g_far, up_part, down_part, got, count
    )
    up_grad = line_scatter(up_grad)
    own, others = team_scatter(keep, low, high)
    own, send_dense, down_grad, d_eupper = together(own, send_dense, down_grad, d_eupper)
    down_grad = line_scatter(down_grad)
    widen_grad = widen_grads(received, d_eupper, width)
    back, widen_grad = together(back, widen_grad)
    a_near, a_far = team_joins(a_parts)
    dense, more = team_scatter(keep_dense, send_dense)
    result, d_residual, side, d_both = after(
        own, others, back, placing, residual, stats, cotangent, got, merge, routes, second, count
    )
    d_both, act = together(d_both, act)
    d_both = team_exchange(d_both)
    d_both, up_grad = together(d_both, up_grad)
    up_grad = team_exchange(up_grad.reshape(TEAM, rows, -1))
    keep, send, grads = attend_back(
        place_arg, xs, a_near, a_far, got, joint, d_both, side, count
    )
    grads, send, up_grad, act, *more = together(grads, send, up_grad, act, *more)
    grads = exchange(grads.reshape(count, rows, -1))
    own, others = team_scatter(keep, send)
    own, act = together(own, act)
    narrow_grad = narrow_grads(d_out, act)
    tokens_grad, result = last(
        own, others, dense, more, result, stats, tokens, d_residual, got, count
    )
    grads, tokens_grad, narrow_grad = together(grads, tokens_grad, narrow_grad)
    grads = grads.reshape(teams, TEAM, rows, -1)
    joint_grad, merge_grad, up_grad, attend_grad, feed_grad, router_grad, mix_grad = owner_sums(
        grads, up_grad, width, hidden, count
    )
    return (
        result,
        tokens_grad,
        attend_grad.reshape(rows),
        joint_grad,
        merge_grad,
        feed_grad.reshape(rows),
        up_grad,
        down_grad.astype(F32),
        router_grad,
        mix_grad.T,
        widen_grad,
        narrow_grad,
    )


def solution(mesh):
    one, two, three = P("expert"), P("expert", None), P("expert", None, None)
    return jax.shard_map(
        body,
        mesh=mesh,
        in_specs=(two, one, two, two, one, two, two, two, two, three, three, two, two, two),
        out_specs=(two, two, one, two, two, one, two, two, two, two, three, three),
        check_vma=False,
    )
```
